256 devices in a mesh: dp: 8 (over z_hi, x), space: 32 (over z_lo, y, core).
Axes of the slice: x: 4, y: 4, z: 8 (z_hi: 2, z_lo: 4; z = z_hi * 4 + z_lo), core: 2. Of those that a mesh axis runs over, the one named last changes fastest.
Arguments:
- crop: bfloat16 [8, 4, 128, 64, 64], P('dp', None, 'space'), may hold values from -6 to 6
- filter_one: bfloat16 [3, 3, 3, 4, 32], replicated, may hold values from -0.625 to 0.625
- filter_two: bfloat16 [3, 3, 3, 32, 64], replicated, may hold values from -0.21875 to 0.21875
- cotangent: bfloat16 [8, 64, 32, 16, 16], P('dp', None, 'space'), may hold values from -1 to 1
Outputs:
- features: bfloat16 [8, 64, 32, 16, 16], P('dp', None, 'space')
- grad_one: float32 [3, 3, 3, 4, 32], replicated
- grad_two: float32 [3, 3, 3, 32, 64], replicated
The draws below stay inside these ranges and needn't reach their ends.
All inputs are finite; a program needn't handle non-finite values.
Results may differ from the reference program's by a relative error of at most 0.0045.
The reference program's roundings to bfloat16 on the way count: a program that leaves them out, or rounds other values in their place, can miss the bound.
Values may be sent and summed in bfloat16 or wider, within the bound.
A program may use at most 128 MiB of HBM per device.

```python
import jax
import jax.numpy as jnp
from jax import lax

C0 = 4
C1 = 32
C2 = 64
SIDE = 64
BATCH = 8
EXTENT = 128
CELLS2 = 524288


def steps_of(rng, dims, pieces, low, largest):
    factor_of, own = 1.0, jax.random.fold_in(rng, 6)
    for position, shards_of in pieces:
        steps = jnp.exp(jax.random.uniform(jax.random.fold_in(own, position), (shards_of,), jnp.float32, low / len(pieces), largest / len(pieces)))
        factor_of = factor_of * jnp.repeat(steps, dims[position] // shards_of).reshape([-1 if axis == position else 1 for axis in range(len(dims))])
    return factor_of


def normal_values(rng, extent, deviation, reach, pieces=(), dtype=jnp.bfloat16):
    entries = jax.random.normal(rng, extent, jnp.float32) * deviation
    if len(pieces) > 0:
        entries = steps_of(rng, extent, pieces, -0.22, 0.18) * entries
    return jnp.clip(entries, min=-reach, max=reach).astype(dtype)


def setup_inputs(seed: int = 0) -> dict:
    splits = jax.random.split(jax.random.key(seed), 5)
    return {
        "crop": normal_values(splits[0], (BATCH, C0, EXTENT, SIDE, SIDE), 1.0, 6.0, ((0, 8), (2, 32))),
        "filter_one": normal_values(splits[1], (3, 3, 3, C0, C1), (27 * C0) ** -0.5, 0.625),
        "filter_two": normal_values(splits[2], (3, 3, 3, C1, C2), (27 * C1) ** -0.5, 0.21875),
        "cotangent": normal_values(splits[3], (BATCH, C2, EXTENT // 4, SIDE // 4, SIDE // 4), (48 * CELLS2 ** -0.5), 1.0, ((0, 8), (2, 32))),
    }


def leaky(value):
    return jnp.where(value > 0, value, 0.3 * value)

def slope(value):
    return jnp.where(value > 0, 1.0, 0.3)

def pooled(value):
    shape = value.shape
    blocks = value.reshape(shape[0], shape[1], shape[2] // 2, 2, shape[3] // 2, 2, shape[4] // 2, 2)
    return blocks.mean(axis=(3, 5, 7))

def widened(value):
    shape = value.shape
    spread = jnp.broadcast_to(value[:, :, :, None, :, None, :, None], (shape[0], shape[1], shape[2], 2, shape[3], 2, shape[4], 2))
    return spread.reshape(shape[0], shape[1], 2 * shape[2], 2 * shape[3], 2 * shape[4])

def conv_same(source, kernel):
    return lax.conv_general_dilated(source, kernel, (1, 1, 1), ((1, 1), (1, 1), (1, 1)), dimension_numbers=('NCDHW', 'DHWIO', 'NCDHW'), preferred_element_type=jnp.float32)

def flipped(kernel):
    return jnp.transpose(kernel[::-1, ::-1, ::-1], (0, 1, 2, 4, 3))

def filter_grad(source, gradient):
    planes, extent_y, extent_z = (gradient.shape[2], gradient.shape[3], gradient.shape[4])
    padded = jnp.pad(source, ((0, 0), (0, 0), (1, 1), (1, 1), (1, 1)))
    partials = []
    for offset in range(27):
        shift_a, shift_b, shift_c = (offset // 9, offset // 3 % 3, offset % 3)
        window = padded[:, :, shift_a:shift_a + planes, shift_b:shift_b + extent_y, shift_c:shift_c + extent_z]
        partials.append(jnp.einsum('bcxyz,bdxyz->cd', window.astype(jnp.float32), gradient.astype(jnp.float32)))
    return jnp.stack(partials).reshape(3, 3, 3, source.shape[1], gradient.shape[1])

def one_sample(crop_one, cot_one, filter_one, filter_two):
    z_one = conv_same(crop_one, filter_one)
    maps_one = pooled(leaky(z_one)).astype(jnp.bfloat16)
    z_two = conv_same(maps_one, filter_two)
    maps_two = pooled(leaky(z_two)).astype(jnp.bfloat16)
    grad_pre_two = (slope(z_two) * widened(cot_one.astype(jnp.float32)) * 0.125).astype(jnp.bfloat16)
    grad_two = filter_grad(maps_one, grad_pre_two)
    back_one = conv_same(grad_pre_two, flipped(filter_two))
    grad_pre_one = (slope(z_one) * widened(back_one) * 0.125).astype(jnp.bfloat16)
    grad_one = filter_grad(crop_one, grad_pre_one)
    return (maps_two[0], grad_one, grad_two)

def reference(crop, filter_one, filter_two, cotangent):

    def handle(pair):
        return one_sample(pair[0][None], pair[1][None], filter_one, filter_two)
    features, grads_one, grads_two = lax.map(handle, (crop, cotangent))
    return (features, lax.optimization_barrier(jnp.sum(grads_one, axis=0)), lax.optimization_barrier(jnp.sum(grads_two, axis=0)))
```

```python
import functools

import jax
import jax.numpy as jnp
import numpy as np
from jax import lax
from jax.experimental import pallas as pl
from jax.experimental.pallas import tpu as pltpu
from jax.sharding import PartitionSpec as P

F32, BF16 = jnp.float32, jnp.bfloat16
LANES = 1024


def leaky(value):
    return jnp.where(value > 0, value, 0.3 * value)


def dot_nn(a, b):
    return lax.dot_general(a, b, (((1,), (0,)), ((), ())), preferred_element_type=F32)


def dot_nt(a, b):
    return lax.dot_general(a, b, (((1,), (1,)), ((), ())), preferred_element_type=F32)


def split2(value):
    high = value.astype(BF16)
    return high, (value - high.astype(F32)).astype(BF16)


def tap_selection():
    table = np.zeros((128, 8, 256), np.float32)
    for d in range(8):
        dp, dq, dr = d // 4, d // 2 % 2, d % 2
        for pi in range(4):
            for sq in range(2):
                for sr in range(2):
                    for qe in range(2):
                        for re in range(2):
                            qi = (1 + qe) if sq == 0 else (0 if qe else 3)
                            ri = (1 + re) if sr == 0 else (0 if re else 3)
                            a, b, c = pi - dp, qi - dq, ri - dr
                            if min(a, b, c) < 0 or max(a, b, c) > 2:
                                continue
                            for i in range(4):
                                k = pi * 64 + (sq * 2 + sr) * 16 + (qe * 2 + re) * 4 + i
                                table[((a * 3 + b) * 3 + c) * 4 + i, d, k] = 1
    return table.reshape(128, 2048)


def lane_masks(rows):
    lane = lax.broadcasted_iota(jnp.int32, (rows, LANES), 1)
    return lane % 32, lane // 32


def ones(mask):
    return jnp.where(mask, 1.0, 0.0).astype(BF16)


def rolled(value, amount):
    return pltpu.roll(value, amount % LANES, 1)


def compute(first, s, crop_ref, w1_ref, w2_ref, w3_ref, sel_ref, cot_ref, feat_ref, g2_out, g1_out,
            px, maps, z1s, g2s, g1s):
    r, q = lane_masks(16)
    row = lax.broadcasted_iota(jnp.int32, (16, LANES), 0)
    q_odd, r_odd = row // 8 == 1, row // 4 % 2 == 1
    r_up, r_down = ones(r_odd & (r != 0)), ones(~r_odd & (r != 31))
    q_up, q_down = ones(q_odd & (q != 0)), ones(~q_odd & (q != 31))
    for plane in range(14):
        x = crop_ref[plane]
        xr = rolled(x, 1) * r_up + rolled(x, -1) * r_down
        xq = rolled(x, 32) * q_up + rolled(x, -32) * q_down
        xqr = rolled(xr, 32) * q_up + rolled(xr, -32) * q_down
        for k, piece in enumerate((x, xr, xq, xqr)):
            px[plane * 64 + k * 16 : plane * 64 + k * 16 + 16, :] = piece
    w1 = w1_ref[...]
    r, q = lane_masks(32)
    keep, keep_ones = {}, {}
    for db in (-1, 0, 1):
        for dc in (-1, 0, 1):
            ok = jnp.ones((32, LANES), jnp.bool_)
            if db:
                ok = ok & ((q != 0) if db < 0 else (q != 31))
            if dc:
                ok = ok & ((r != 0) if dc < 0 else (r != 31))
            keep[db, dc] = ok
            keep_ones[db, dc] = ones(ok)
    left_ok = jnp.where(s > 0, 1.0, 0.0)
    right_ok = jnp.where(s < 31, 1.0, 0.0)
    for plane in range(6):
        z = dot_nn(w1, px[plane * 128 : plane * 128 + 256, :])
        if plane in (2, 3):
            z1s[(plane - 2) * 256 : (plane - 1) * 256, :] = z.astype(BF16)
        z = leaky(z)
        total = z[0:32]
        for d in range(1, 8):
            total = total + z[d * 32 : d * 32 + 32]
        scale = 0.125 * (left_ok if plane < 2 else right_ok if plane > 3 else 1.0)
        a1 = (total * scale).astype(BF16)
        for b in range(3):
            for c in range(3):
                v = a1
                if (b, c) != (1, 1):
                    v = rolled(v, -(32 * (b - 1) + (c - 1)))
                    v = v * keep_ones[b - 1, c - 1]
                at = plane * 288 + (b * 3 + c) * 32
                maps[at : at + 32, :] = v
    k_id = lax.broadcasted_iota(jnp.int32, (128, 512), 0)
    n_id = lax.broadcasted_iota(jnp.int32, (128, 512), 1)
    spread = ((n_id // 64 == k_id // 16) & (n_id % 32 // 2 == k_id % 16)).astype(F32).astype(BF16)
    pk = lax.broadcasted_iota(jnp.int32, (256, 64), 0)
    pn = lax.broadcasted_iota(jnp.int32, (256, 64), 1)
    gather = ((pk // 64 == pn // 16) & (pk % 32 // 2 == pn % 16)).astype(F32).astype(BF16)
    w2 = w2_ref[...]
    pair = None
    for plane in range(4):
        z = dot_nn(w2, maps[plane * 288 : plane * 288 + 864, :])
        cot = cot_ref[(0, 1, 1, 2)[plane]]
        wide = jnp.concatenate([dot_nn(cot[:, 0:128], spread), dot_nn(cot[:, 128:256], spread)], axis=1) * 0.125
        g2s[plane * 64 : plane * 64 + 64, :] = jnp.where(z > 0, wide, 0.3 * wide).astype(BF16)
        if plane == 1:
            pair = leaky(z)
        elif plane == 2:
            pair = pair + leaky(z)
            high, low = split2(pair)
            for j in range(4):
                lanes = slice(256 * j, 256 * j + 256)
                feat_ref[:, 64 * j : 64 * j + 64] = (
                    (dot_nn(high[:, lanes], gather) + dot_nn(low[:, lanes], gather)) * 0.125
                ).astype(BF16)
    grad = dot_nt(maps[288 : 288 + 864, :], g2s[64:128, :])
    grad = grad + dot_nt(maps[576 : 576 + 864, :], g2s[128:192, :])
    g2_out[...] = jnp.concatenate([grad[0:432], grad[432:864]], axis=1)
    w3 = w3_ref[...]
    for plane in range(2):
        u = dot_nn(w3, g2s[plane * 64 : plane * 64 + 192, :])
        back = None
        for b in range(3):
            for c in range(3):
                v = u[(b * 3 + c) * 32 : (b * 3 + c) * 32 + 32]
                if (b, c) != (1, 1):
                    v = rolled(v, -(32 * (1 - b) + (1 - c)))
                    v = jnp.where(keep[1 - b, 1 - c], v, 0.0)
                back = v if back is None else back + v
        back = back * 0.125
        low = 0.3 * back
        for d in range(8):
            at = plane * 256 + d * 32
            g1s[at : at + 32, :] = jnp.where(z1s[at : at + 32, :].astype(F32) > 0, back, low).astype(BF16)
    gram = dot_nt(g1s[0:256, :], px[256:512, :]) + dot_nt(g1s[256:512, :], px[384:640, :])
    total = None
    for d in range(8):
        high, low = split2(gram[d * 32 : d * 32 + 32])
        sel = sel_ref[:, d * 256 : d * 256 + 256]
        term = dot_nt(high, sel) + dot_nt(low, sel)
        total = term if total is None else total + term
    g1_out[...] = total
def compute_kernel(*refs):
    compute(None, lax.axis_index("space"), *refs)


def shift_planes(value, axis, hops):
    count = lax.axis_size(axis)
    return lax.ppermute(value, axis, [(j, j + hops) for j in range(count) if 0 <= j + hops < count])


def local(crop, filter_one, filter_two, cotangent):
    planes = crop[0].reshape(4, 4, 32, 2, 32, 2).transpose(1, 3, 5, 0, 2, 4).reshape(4, 16, LANES)
    cot = cotangent.reshape(64, 256)
    crop14 = jnp.concatenate(
        [
            shift_planes(planes[3:4], "space", 2),
            shift_planes(planes, "space", 1),
            planes,
            shift_planes(planes, "space", -1),
            shift_planes(planes[0:1], "space", -2),
        ]
    )
    cot3 = jnp.stack([shift_planes(cot, "space", 1), cot, shift_planes(cot, "space", -1)])
    sel = jnp.asarray(tap_selection(), BF16)
    taps = jnp.pad(filter_one.reshape(108, 32), ((0, 20), (0, 0)))
    w1 = jnp.einsum("to,tdk->dok", taps, sel.reshape(128, 8, 256), preferred_element_type=F32)
    w1 = w1.astype(BF16).reshape(256, 256)
    f2 = filter_two.reshape(864, 64)
    w2 = f2.T
    w3 = jnp.concatenate([f2[576:864], f2[288:576], f2[0:288]], axis=1)
    feat, two, one = pl.pallas_call(
        compute_kernel,
        out_shape=(
            jax.ShapeDtypeStruct((64, 256), BF16),
            jax.ShapeDtypeStruct((432, 128), F32),
            jax.ShapeDtypeStruct((32, 128), F32),
        ),
        scratch_shapes=[
            pltpu.VMEM((896, LANES), BF16),
            pltpu.VMEM((1728, LANES), BF16),
            pltpu.VMEM((512, LANES), BF16),
            pltpu.VMEM((256, LANES), BF16),
            pltpu.VMEM((512, LANES), BF16),
        ],
        compiler_params=pltpu.CompilerParams(vmem_limit_bytes=60 * 1024 * 1024),
    )(crop14, w1, w2, w3, sel, cot3)
    two, one = lax.psum((two, one), ("dp", "space"))
    two = jnp.concatenate([two[:, 0:64], two[:, 64:128]]).reshape(3, 3, 3, 32, 64)
    one = one.T[0:108].reshape(3, 3, 3, 4, 32)
    return feat.reshape(1, 64, 1, 16, 16), one, two


def solution(mesh):
    placed = (P("dp", None, "space", None, None), P(), P(), P("dp", None, "space", None, None))
    return jax.shard_map(
        local, mesh=mesh, in_specs=placed, out_specs=(P("dp", None, "space", None, None), P(), P()), check_vma=False
    )
```

```python
import functools

import jax
import jax.numpy as jnp
import numpy as np
from jax import lax
from jax.experimental import pallas as pl
from jax.experimental.pallas import tpu as pltpu
from jax.sharding import PartitionSpec as P

F32, BF16 = jnp.float32, jnp.bfloat16
LANES = 1024


def leaky(value):
    return jnp.where(value > 0, value, 0.3 * value)


def dot_nn(a, b):
    return lax.dot_general(a, b, (((1,), (0,)), ((), ())), preferred_element_type=F32)


def dot_nt(a, b):
    return lax.dot_general(a, b, (((1,), (1,)), ((), ())), preferred_element_type=F32)


def split2(value):
    high = value.astype(BF16)
    return high, (value - high.astype(F32)).astype(BF16)


def tap_selection():
    table = np.zeros((128, 8, 256), np.float32)
    for d in range(8):
        dp, dq, dr = d // 4, d // 2 % 2, d % 2
        for pi in range(4):
            for sq in range(2):
                for sr in range(2):
                    for qe in range(2):
                        for re in range(2):
                            qi = (1 + qe) if sq == 0 else (0 if qe else 3)
                            ri = (1 + re) if sr == 0 else (0 if re else 3)
                            a, b, c = pi - dp, qi - dq, ri - dr
                            if min(a, b, c) < 0 or max(a, b, c) > 2:
                                continue
                            for i in range(4):
                                k = pi * 64 + (sq * 2 + sr) * 16 + (qe * 2 + re) * 4 + i
                                table[((a * 3 + b) * 3 + c) * 4 + i, d, k] = 1
    return table.reshape(128, 2048)


def lane_masks(rows):
    lane = lax.broadcasted_iota(jnp.int32, (rows, LANES), 1)
    return lane % 32, lane // 32


def ones(mask):
    return jnp.where(mask, 1.0, 0.0).astype(BF16)


def rolled(value, amount):
    return pltpu.roll(value, amount % LANES, 1)


def compute(first, s, crop_ref, w1_ref, w2_ref, w3_ref, sel_ref, cot_ref, feat_ref, g2_out, g1_out,
            px, maps, z1s, g2s, g1s):
    r, q = lane_masks(16)
    row = lax.broadcasted_iota(jnp.int32, (16, LANES), 0)
    q_odd, r_odd = row // 8 == 1, row // 4 % 2 == 1
    r_up, r_down = ones(r_odd & (r != 0)), ones(~r_odd & (r != 31))
    q_up, q_down = ones(q_odd & (q != 0)), ones(~q_odd & (q != 31))
    for plane in range(14):
        x = crop_ref[plane]
        xr = rolled(x, 1) * r_up + rolled(x, -1) * r_down
        xq = rolled(x, 32) * q_up + rolled(x, -32) * q_down
        xqr = rolled(xr, 32) * q_up + rolled(xr, -32) * q_down
        for k, piece in enumerate((x, xr, xq, xqr)):
            px[plane * 64 + k * 16 : plane * 64 + k * 16 + 16, :] = piece
    w1 = w1_ref[...]
    r, q = lane_masks(32)
    keep, keep_ones = {}, {}
    for db in (-1, 0, 1):
        for dc in (-1, 0, 1):
            ok = jnp.ones((32, LANES), jnp.bool_)
            if db:
                ok = ok & ((q != 0) if db < 0 else (q != 31))
            if dc:
                ok = ok & ((r != 0) if dc < 0 else (r != 31))
            keep[db, dc] = ok
            keep_ones[db, dc] = ones(ok)
    left_ok = jnp.where(s > 0, 1.0, 0.0)
    right_ok = jnp.where(s < 31, 1.0, 0.0)
    for plane in range(6):
        z = dot_nn(w1, px[plane * 128 : plane * 128 + 256, :])
        if plane in (2, 3):
            z1s[(plane - 2) * 256 : (plane - 1) * 256, :] = z.astype(BF16)
        z = leaky(z)
        total = z[0:32]
        for d in range(1, 8):
            total = total + z[d * 32 : d * 32 + 32]
        scale = 0.125 * (left_ok if plane < 2 else right_ok if plane > 3 else 1.0)
        a1 = (total * scale).astype(BF16)
        for b in range(3):
            for c in range(3):
                v = a1
                if (b, c) != (1, 1):
                    v = rolled(v, -(32 * (b - 1) + (c - 1)))
                    v = v * keep_ones[b - 1, c - 1]
                at = plane * 288 + (b * 3 + c) * 32
                maps[at : at + 32, :] = v
    k_id = lax.broadcasted_iota(jnp.int32, (128, 512), 0)
    n_id = lax.broadcasted_iota(jnp.int32, (128, 512), 1)
    spread = ((n_id // 64 == k_id // 16) & (n_id % 32 // 2 == k_id % 16)).astype(F32).astype(BF16)
    pk = lax.broadcasted_iota(jnp.int32, (256, 64), 0)
    pn = lax.broadcasted_iota(jnp.int32, (256, 64), 1)
    gather = ((pk // 64 == pn // 16) & (pk % 32 // 2 == pn % 16)).astype(F32).astype(BF16)
    w2 = w2_ref[...]
    pair = None
    for plane in range(4):
        z = dot_nn(w2, maps[plane * 288 : plane * 288 + 864, :])
        cot = cot_ref[(0, 1, 1, 2)[plane]]
        wide = jnp.concatenate([dot_nn(cot[:, 0:128], spread), dot_nn(cot[:, 128:256], spread)], axis=1) * 0.125
        g2s[plane * 64 : plane * 64 + 64, :] = jnp.where(z > 0, wide, 0.3 * wide).astype(BF16)
        if plane == 1:
            pair = leaky(z)
        elif plane == 2:
            pair = pair + leaky(z)
            high, low = split2(pair)
            for j in range(4):
                lanes = slice(256 * j, 256 * j + 256)
                feat_ref[:, 64 * j : 64 * j + 64] = (
                    (dot_nn(high[:, lanes], gather) + dot_nn(low[:, lanes], gather)) * 0.125
                ).astype(BF16)
    grad = dot_nt(maps[288 : 288 + 864, :], g2s[64:128, :])
    grad = grad + dot_nt(maps[576 : 576 + 864, :], g2s[128:192, :])
    g2_out[...] = jnp.concatenate([grad[0:432], grad[432:864]], axis=1)
    w3 = w3_ref[...]
    for plane in range(2):
        u = dot_nn(w3, g2s[plane * 64 : plane * 64 + 192, :])
        back = None
        for b in range(3):
            for c in range(3):
                v = u[(b * 3 + c) * 32 : (b * 3 + c) * 32 + 32]
                if (b, c) != (1, 1):
                    v = rolled(v, -(32 * (1 - b) + (1 - c)))
                    v = jnp.where(keep[1 - b, 1 - c], v, 0.0)
                back = v if back is None else back + v
        back = back * 0.125
        low = 0.3 * back
        for d in range(8):
            at = plane * 256 + d * 32
            g1s[at : at + 32, :] = jnp.where(z1s[at : at + 32, :].astype(F32) > 0, back, low).astype(BF16)
    gram = dot_nt(g1s[0:256, :], px[256:512, :]) + dot_nt(g1s[256:512, :], px[384:640, :])
    total = None
    for d in range(8):
        high, low = split2(gram[d * 32 : d * 32 + 32])
        sel = sel_ref[:, d * 256 : d * 256 + 256]
        term = dot_nt(high, sel) + dot_nt(low, sel)
        total = term if total is None else total + term
    g1_out[...] = total


NX, NY, NZH, NZL = 4, 4, 2, 4
ROWS = 16


class Place:
    def __init__(self):
        dp, self.s = lax.axis_index("dp"), lax.axis_index("space")
        self.zh, self.x = dp // NX, dp % NX
        self.core = self.s % 2
        self.y = self.s // 2 % NY
        self.zl = self.s // 2 // NY
        self.z = self.zh * NZL + self.zl

    def at(self, x, y, z, core):
        return {"dp": z // NZL * NX + x, "space": (z % NZL * NY + y) * 2 + core}

    def plane_peer(self, dx, dy):
        x, y = (self.x + dx) % NX, (self.y + dy) % NY
        return self.at(x, y, self.z, self.core), x * NY + y

    def depth_peer(self, dz):
        return self.at(self.x, self.y, (self.z + dz) % (NZH * NZL), self.core)

    def partner(self):
        return self.at(self.x, self.y, self.z, 1 - self.core)


def ring_order(count):
    return sorted(range(count), key=lambda d: -min(d, count - d))


def plane_offsets():
    far = lambda d: min(d[0], NX - d[0]) + min(d[1], NY - d[1])
    every = [(dx, dy) for dx in range(NX) for dy in range(NY)]
    return sorted(every, key=lambda d: -far(d))


def remote(src, dst, send, recv, peer):
    return pltpu.make_async_remote_copy(
        src_ref=src, dst_ref=dst, send_sem=send, recv_sem=recv, device_id=peer, device_id_type=pl.DeviceIdType.MESH
    )


HALO_HOPS = (1, -1, 2, -2)


def greet(place, with_halo):
    barrier = pltpu.get_barrier_semaphore()
    peers = [place.partner()]
    peers += [place.plane_peer(dx, dy)[0] for dx, dy in plane_offsets()[:-1]]
    peers += [place.depth_peer(d) for d in range(1, NZH * NZL)]
    if with_halo:
        count = lax.axis_size("space")
        peers += [{"space": (place.s + hop + count) % count} for hop in HALO_HOPS]
    for peer in peers:
        pl.semaphore_signal(barrier, inc=1, device_id=peer, device_id_type=pl.DeviceIdType.MESH)
    return lambda: pl.semaphore_wait(barrier, len(peers))


class Halo:
    def __init__(self, place, own_ref, cot_ref, wide, cots, send, recv):
        self.s, self.count = place.s, lax.axis_size("space")
        moves = (
            (1, own_ref, wide.at[1:5]),
            (-1, own_ref, wide.at[9:13]),
            (2, own_ref.at[3:4], wide.at[0:1]),
            (-2, own_ref.at[0:1], wide.at[13:14]),
            (1, cot_ref, cots.at[0]),
            (-1, cot_ref, cots.at[2]),
        )
        self.items = []
        for k, (hop, src, dst) in enumerate(moves):
            peer = {"space": (self.s + hop + self.count) % self.count}
            self.items.append((hop, dst, remote(src, dst, send.at[k], recv.at[k], peer)))

    def exists(self, hop):
        there = self.s + hop
        return (there >= 0) & (there < self.count)

    def start(self):
        for hop, dst, copy in self.items:
            pl.when(self.exists(hop))(copy.start)

            @pl.when(jnp.logical_not(self.exists(-hop)))
            def _():
                dst[...] = jnp.zeros(dst.shape, BF16)

    def wait(self):
        for hop, dst, copy in self.items:
            pl.when(self.exists(-hop))(copy.wait_recv)

    def drain(self):
        for hop, dst, copy in self.items:
            pl.when(self.exists(hop))(copy.wait_send)


def all_reduce(place, acc, r0, s0, r1, r2, fin, sems):
    send0, recv0, send1, recv1, send2, recv2, send3, recv3, send4, recv4 = sems
    half = NX * NY * ROWS
    offsets = plane_offsets()
    last = len(offsets) - 1
    mine = place.core * half
    other = half - mine

    def rows(start):
        return pl.ds(pl.multiple_of(start, ROWS), ROWS)

    partner = place.partner()
    sent = []
    chunk = [place.plane_peer(dx, dy) for dx, dy in offsets]
    arrive0 = []
    for k, (_, j) in enumerate(chunk):
        copy = remote(acc.at[rows(other + j * ROWS)], r0.at[rows(j * ROWS)], send0.at[k], recv0.at[k], partner)
        copy.start()
        arrive0.append(copy)
    sent += arrive0
    arrive1 = []

    def pass_on(k):
        peer, j = chunk[k]
        copy = remote(s0.at[rows(j * ROWS)], r1.at[k], send1.at[k], recv1.at[k], peer)
        copy.start()
        arrive1.append(copy)

    for k, (peer, j) in enumerate(chunk):
        arrive0[k].wait_recv()
        s0[rows(j * ROWS), :] = acc[rows(mine + j * ROWS), :] + r0[rows(j * ROWS), :]
        if k >= 1:
            pass_on(k - 1)
    sent += arrive1
    own = chunk[last][1]
    total = s0[rows(own * ROWS), :]
    for k in range(last - 1, -1, -1):
        arrive1[k].wait_recv()
        total = total + r1[k]
    r2[place.z] = total
    arrive2 = []
    depth = NZH * NZL
    for k, d in enumerate(ring_order(depth)[:-1]):
        copy = remote(r2.at[place.z], r2.at[place.z], send2.at[k], recv2.at[k], place.depth_peer(d))
        copy.start()
        arrive2.append(copy)
    sent += arrive2
    for copy in arrive2:
        copy.wait_recv()
    total = r2[0]
    for z in range(1, depth):
        total = total + r2[z]
    at_own = rows(mine + own * ROWS)
    fin[at_own, :] = total
    arrive3 = []
    for k in range(last):
        copy = remote(fin.at[at_own], fin.at[at_own], send3.at[k], recv3.at[k], chunk[k][0])
        copy.start()
        arrive3.append(copy)
    sent += arrive3

    def hand_over(k, start):
        at = rows(mine + start * ROWS)
        copy = remote(fin.at[at], fin.at[at], send4.at[k], recv4.at[k], partner)
        copy.start()
        return copy

    arrive4 = [hand_over(last, own)]
    for k in range(last - 1, -1, -1):
        arrive3[k].wait_recv()
        dx, dy = offsets[k]
        source = (place.x - dx + NX) % NX * NY + (place.y - dy + NY) % NY
        arrive4.append(hand_over(k, source))
    for copy in arrive4:
        copy.wait_recv()
    return sent + arrive4


def reduce_scratch():
    half = NX * NY * ROWS
    n, depth = NX * NY, NZH * NZL
    dma = pltpu.SemaphoreType.DMA
    return [
        pltpu.VMEM((2 * half, 128), F32),
        pltpu.VMEM((half, 128), F32),
        pltpu.VMEM((half, 128), F32),
        pltpu.VMEM((n, ROWS, 128), F32),
        pltpu.VMEM((depth, ROWS, 128), F32),
        pltpu.VMEM((2 * half, 128), F32),
    ], [dma((n,)), dma((n,)), dma((n,)), dma((n,)), dma((depth,)), dma((depth,)), dma((n,)), dma((n,)), dma((n,)), dma((n,))]


def whole_kernel(crop_ref, w1_ref, w2_ref, w3_ref, sel_ref, cot_ref, feat_ref, sum_ref, wide, cots, px, maps, z1s, g2s, g1s,
                 acc, r0, s0, r1, r2, fin, halo_send, halo_recv, *sems):
    place = Place()
    ready = greet(place, True)
    wide[5:9] = crop_ref[...]
    cots[1] = cot_ref[...]
    acc[464:512, :] = jnp.zeros((48, 128), F32)
    halo = Halo(place, crop_ref, cot_ref, wide, cots, halo_send, halo_recv)
    ready()
    halo.start()
    halo.wait()
    compute(None, place.s, wide, w1_ref, w2_ref, w3_ref, sel_ref, cots, feat_ref, acc.at[0:432], acc.at[432:464],
            px, maps, z1s, g2s, g1s)
    sent = all_reduce(place, acc, r0, s0, r1, r2, fin, sems)
    sum_ref[...] = fin[...]
    halo.drain()
    for copy in sent:
        copy.wait_send()


def local(crop, filter_one, filter_two, cotangent):
    planes = crop[0].reshape(4, 4, 32, 2, 32, 2).transpose(1, 3, 5, 0, 2, 4).reshape(4, 16, LANES)
    cot = cotangent.reshape(64, 256)
    sel = jnp.asarray(tap_selection(), BF16)
    taps = jnp.pad(filter_one.reshape(108, 32), ((0, 20), (0, 0)))
    w1 = jnp.einsum("to,tdk->dok", taps, sel.reshape(128, 8, 256), preferred_element_type=F32)
    w1 = w1.astype(BF16).reshape(256, 256)
    f2 = filter_two.reshape(864, 64)
    w2 = f2.T
    w3 = jnp.concatenate([f2[576:864], f2[288:576], f2[0:288]], axis=1)
    buffers, sems = reduce_scratch()
    feat, sums = pl.pallas_call(
        whole_kernel,
        out_shape=(jax.ShapeDtypeStruct((64, 256), BF16), jax.ShapeDtypeStruct((512, 128), F32)),
        scratch_shapes=[
            pltpu.VMEM((14, 16, LANES), BF16),
            pltpu.VMEM((3, 64, 256), BF16),
            pltpu.VMEM((896, LANES), BF16),
            pltpu.VMEM((1728, LANES), BF16),
            pltpu.VMEM((512, LANES), BF16),
            pltpu.VMEM((256, LANES), BF16),
            pltpu.VMEM((512, LANES), BF16),
            *buffers,
            pltpu.SemaphoreType.DMA((6,)),
            pltpu.SemaphoreType.DMA((6,)),
            *sems,
        ],
        compiler_params=pltpu.CompilerParams(
            vmem_limit_bytes=60 * 1024 * 1024, collective_id=0, has_side_effects=True
        ),
    )(planes, w1, w2, w3, sel, cot)
    two = jnp.concatenate([sums[0:432, 0:64], sums[0:432, 64:128]]).reshape(3, 3, 3, 32, 64)
    one = sums[432:464].T[0:108].reshape(3, 3, 3, 4, 32)
    return feat.reshape(1, 64, 1, 16, 16), one, two


def solution(mesh):
    placed = (P("dp", None, "space", None, None), P(), P(), P("dp", None, "space", None, None))
    return jax.shard_map(
        local, mesh=mesh, in_specs=placed, out_specs=(P("dp", None, "space", None, None), P(), P()), check_vma=False
    )
```

```python
import functools

import jax
import jax.numpy as jnp
import numpy as np
from jax import lax
from jax.experimental import pallas as pl
from jax.experimental.pallas import tpu as pltpu
from jax.sharding import PartitionSpec as P

F32, BF16 = jnp.float32, jnp.bfloat16
LANES = 1024


def leaky(value):
    return jnp.where(value > 0, value, 0.3 * value)


def dot_nn(a, b):
    return lax.dot_general(a, b, (((1,), (0,)), ((), ())), preferred_element_type=F32)


def dot_nt(a, b):
    return lax.dot_general(a, b, (((1,), (1,)), ((), ())), preferred_element_type=F32)


def split2(value):
    high = value.astype(BF16)
    return high, (value - high.astype(F32)).astype(BF16)


def tap_selection():
    table = np.zeros((128, 8, 256), np.float32)
    for d in range(8):
        dp, dq, dr = d // 4, d // 2 % 2, d % 2
        for pi in range(4):
            for sq in range(2):
                for sr in range(2):
                    for qe in range(2):
                        for re in range(2):
                            qi = (1 + qe) if sq == 0 else (0 if qe else 3)
                            ri = (1 + re) if sr == 0 else (0 if re else 3)
                            a, b, c = pi - dp, qi - dq, ri - dr
                            if min(a, b, c) < 0 or max(a, b, c) > 2:
                                continue
                            for i in range(4):
                                k = pi * 64 + (sq * 2 + sr) * 16 + (qe * 2 + re) * 4 + i
                                table[((a * 3 + b) * 3 + c) * 4 + i, d, k] = 1
    return table.reshape(128, 2048)


def lane_masks(rows):
    lane = lax.broadcasted_iota(jnp.int32, (rows, LANES), 1)
    return lane % 32, lane // 32


def ones(mask):
    return jnp.where(mask, 1.0, 0.0).astype(BF16)


def rolled(value, amount):
    return pltpu.roll(value, amount % LANES, 1)


def compute(first, s, crop_ref, w1_ref, w2_ref, w3_ref, sel_ref, cot_ref, feat_ref, g2_out, g1_out,
            px, maps, z1s, g2s, g1s):
    r, q = lane_masks(16)
    row = lax.broadcasted_iota(jnp.int32, (16, LANES), 0)
    q_odd, r_odd = row // 8 == 1, row // 4 % 2 == 1
    r_up, r_down = ones(r_odd & (r != 0)), ones(~r_odd & (r != 31))
    q_up, q_down = ones(q_odd & (q != 0)), ones(~q_odd & (q != 31))
    for plane in range(14):
        x = crop_ref[plane]
        xr = rolled(x, 1) * r_up + rolled(x, -1) * r_down
        xq = rolled(x, 32) * q_up + rolled(x, -32) * q_down
        xqr = rolled(xr, 32) * q_up + rolled(xr, -32) * q_down
        for k, piece in enumerate((x, xr, xq, xqr)):
            px[plane * 64 + k * 16 : plane * 64 + k * 16 + 16, :] = piece
    w1 = w1_ref[...]
    r, q = lane_masks(32)
    keep, keep_ones = {}, {}
    for db in (-1, 0, 1):
        for dc in (-1, 0, 1):
            ok = jnp.ones((32, LANES), jnp.bool_)
            if db:
                ok = ok & ((q != 0) if db < 0 else (q != 31))
            if dc:
                ok = ok & ((r != 0) if dc < 0 else (r != 31))
            keep[db, dc] = ok
            keep_ones[db, dc] = ones(ok)
    left_ok = jnp.where(s > 0, 1.0, 0.0)
    right_ok = jnp.where(s < 31, 1.0, 0.0)
    for plane in range(6):
        z = dot_nn(w1, px[plane * 128 : plane * 128 + 256, :])
        if plane in (2, 3):
            z1s[(plane - 2) * 256 : (plane - 1) * 256, :] = z.astype(BF16)
        z = leaky(z)
        total = z[0:32]
        for d in range(1, 8):
            total = total + z[d * 32 : d * 32 + 32]
        scale = 0.125 * (left_ok if plane < 2 else right_ok if plane > 3 else 1.0)
        a1 = (total * scale).astype(BF16)
        for b in range(3):
            for c in range(3):
                v = a1
                if (b, c) != (1, 1):
                    v = rolled(v, -(32 * (b - 1) + (c - 1)))
                    v = v * keep_ones[b - 1, c - 1]
                at = plane * 288 + (b * 3 + c) * 32
                maps[at : at + 32, :] = v
    k_id = lax.broadcasted_iota(jnp.int32, (128, 512), 0)
    n_id = lax.broadcasted_iota(jnp.int32, (128, 512), 1)
    spread = ((n_id // 64 == k_id // 16) & (n_id % 32 // 2 == k_id % 16)).astype(F32).astype(BF16)
    pk = lax.broadcasted_iota(jnp.int32, (256, 64), 0)
    pn = lax.broadcasted_iota(jnp.int32, (256, 64), 1)
    gather = ((pk // 64 == pn // 16) & (pk % 32 // 2 == pn % 16)).astype(F32).astype(BF16)
    w2 = w2_ref[...]
    pair = None
    for plane in range(4):
        z = dot_nn(w2, maps[plane * 288 : plane * 288 + 864, :])
        cot = cot_ref[(0, 1, 1, 2)[plane]]
        wide = jnp.concatenate([dot_nn(cot[:, 0:128], spread), dot_nn(cot[:, 128:256], spread)], axis=1) * 0.125
        g2s[plane * 64 : plane * 64 + 64, :] = jnp.where(z > 0, wide, 0.3 * wide).astype(BF16)
        if plane == 1:
            pair = leaky(z)
        elif plane == 2:
            pair = pair + leaky(z)
            high, low = split2(pair)
            for j in range(4):
                lanes = slice(256 * j, 256 * j + 256)
                feat_ref[:, 64 * j : 64 * j + 64] = (
                    (dot_nn(high[:, lanes], gather) + dot_nn(low[:, lanes], gather)) * 0.125
                )
    grad = dot_nt(maps[288 : 288 + 864, :], g2s[64:128, :])
    grad = grad + dot_nt(maps[576 : 576 + 864, :], g2s[128:192, :])
    g2_out[...] = jnp.concatenate([grad[0:432], grad[432:864]], axis=1)
    w3 = w3_ref[...]
    for plane in range(2):
        u = dot_nn(w3, g2s[plane * 64 : plane * 64 + 192, :])
        back = None
        for b in range(3):
            for c in range(3):
                v = u[(b * 3 + c) * 32 : (b * 3 + c) * 32 + 32]
                if (b, c) != (1, 1):
                    v = rolled(v, -(32 * (1 - b) + (1 - c)))
                    v = jnp.where(keep[1 - b, 1 - c], v, 0.0)
                back = v if back is None else back + v
        back = back * 0.125
        low = 0.3 * back
        for d in range(8):
            at = plane * 256 + d * 32
            g1s[at : at + 32, :] = jnp.where(z1s[at : at + 32, :].astype(F32) > 0, back, low).astype(BF16)
    gram = dot_nt(g1s[0:256, :], px[256:512, :]) + dot_nt(g1s[256:512, :], px[384:640, :])
    total = None
    for d in range(8):
        high, low = split2(gram[d * 32 : d * 32 + 32])
        sel = sel_ref[:, d * 256 : d * 256 + 256]
        term = dot_nt(high, sel) + dot_nt(low, sel)
        total = term if total is None else total + term
    g1_out[...] = total


NX, NY, NZH, NZL = 4, 4, 2, 4
ROWS = 16


class Place:
    def __init__(self):
        dp, self.s = lax.axis_index("dp"), lax.axis_index("space")
        self.zh, self.x = dp // NX, dp % NX
        self.core = self.s % 2
        self.y = self.s // 2 % NY
        self.zl = self.s // 2 // NY
        self.z = self.zh * NZL + self.zl

    def at(self, x, y, z, core):
        return {"dp": z // NZL * NX + x, "space": (z % NZL * NY + y) * 2 + core}

    def plane_peer(self, dx, dy):
        x, y = (self.x + dx) % NX, (self.y + dy) % NY
        return self.at(x, y, self.z, self.core), x * NY + y

    def depth_peer(self, dz):
        return self.at(self.x, self.y, (self.z + dz) % (NZH * NZL), self.core)

    def partner(self):
        return self.at(self.x, self.y, self.z, 1 - self.core)


def ring_order(count):
    return sorted(range(count), key=lambda d: -min(d, count - d))


def plane_offsets():
    far = lambda d: min(d[0], NX - d[0]) + min(d[1], NY - d[1])
    every = [(dx, dy) for dx in range(NX) for dy in range(NY)]
    return sorted(every, key=lambda d: -far(d))


def remote(src, dst, send, recv, peer):
    return pltpu.make_async_remote_copy(
        src_ref=src, dst_ref=dst, send_sem=send, recv_sem=recv, device_id=peer, device_id_type=pl.DeviceIdType.MESH
    )


HALO_HOPS = (1, -1, 2, -2)


def greet(place, with_halo):
    barrier = pltpu.get_barrier_semaphore()
    peers = [place.partner()]
    peers += [place.plane_peer(dx, dy)[0] for dx, dy in plane_offsets()[:-1]]
    peers += [place.depth_peer(d) for d in range(1, NZH * NZL)]
    if with_halo:
        count = lax.axis_size("space")
        peers += [{"space": (place.s + hop + count) % count} for hop in HALO_HOPS]
    for peer in peers:
        pl.semaphore_signal(barrier, inc=1, device_id=peer, device_id_type=pl.DeviceIdType.MESH)
    return lambda: pl.semaphore_wait(barrier, len(peers))


class Halo:
    def __init__(self, place, own_ref, cot_ref, wide, cots, send, recv):
        self.s, self.count = place.s, lax.axis_size("space")
        moves = (
            (1, own_ref, wide.at[1:5]),
            (-1, own_ref, wide.at[9:13]),
            (2, own_ref.at[3:4], wide.at[0:1]),
            (-2, own_ref.at[0:1], wide.at[13:14]),
            (1, cot_ref, cots.at[0]),
            (-1, cot_ref, cots.at[2]),
        )
        self.items = []
        for k, (hop, src, dst) in enumerate(moves):
            peer = {"space": (self.s + hop + self.count) % self.count}
            self.items.append((hop, dst, remote(src, dst, send.at[k], recv.at[k], peer)))

    def exists(self, hop):
        there = self.s + hop
        return (there >= 0) & (there < self.count)

    def start(self):
        for hop, dst, copy in self.items:
            pl.when(self.exists(hop))(copy.start)

            @pl.when(jnp.logical_not(self.exists(-hop)))
            def _():
                dst[...] = jnp.zeros(dst.shape, BF16)

    def wait(self):
        for hop, dst, copy in self.items:
            pl.when(self.exists(-hop))(copy.wait_recv)

    def drain(self):
        for hop, dst, copy in self.items:
            pl.when(self.exists(hop))(copy.wait_send)


def all_reduce(place, acc, r0, s0, r1, r2, fin, sems):
    send0, recv0, send1, recv1, send2, recv2, send3, recv3, send4, recv4 = sems
    half = NX * NY * ROWS
    offsets = plane_offsets()
    last = len(offsets) - 1
    mine = place.core * half
    other = half - mine

    def rows(start):
        return pl.ds(pl.multiple_of(start, ROWS), ROWS)

    partner = place.partner()
    sent = []
    chunk = [place.plane_peer(dx, dy) for dx, dy in offsets]
    arrive0 = []
    for k, (_, j) in enumerate(chunk):
        copy = remote(acc.at[rows(other + j * ROWS)], r0.at[rows(j * ROWS)], send0.at[k], recv0.at[k], partner)
        copy.start()
        arrive0.append(copy)
    sent += arrive0
    arrive1 = []

    def pass_on(k):
        peer, j = chunk[k]
        copy = remote(s0.at[rows(j * ROWS)], r1.at[k], send1.at[k], recv1.at[k], peer)
        copy.start()
        arrive1.append(copy)

    for k, (peer, j) in enumerate(chunk):
        arrive0[k].wait_recv()
        s0[rows(j * ROWS), :] = acc[rows(mine + j * ROWS), :] + r0[rows(j * ROWS), :]
        if k >= 1:
            pass_on(k - 1)
    sent += arrive1
    own = chunk[last][1]
    total = s0[rows(own * ROWS), :]
    for k in range(last - 1, -1, -1):
        arrive1[k].wait_recv()
        total = total + r1[k]
    r2[place.z] = total
    arrive2 = []
    depth = NZH * NZL
    for k, d in enumerate(ring_order(depth)[:-1]):
        copy = remote(r2.at[place.z], r2.at[place.z], send2.at[k], recv2.at[k], place.depth_peer(d))
        copy.start()
        arrive2.append(copy)
    sent += arrive2
    for copy in arrive2:
        copy.wait_recv()
    total = r2[0]
    for z in range(1, depth):
        total = total + r2[z]
    at_own = rows(mine + own * ROWS)
    fin[at_own, :] = total
    arrive3 = []
    for k in range(last):
        copy = remote(fin.at[at_own], fin.at[at_own], send3.at[k], recv3.at[k], chunk[k][0])
        copy.start()
        arrive3.append(copy)
    sent += arrive3

    def hand_over(k, start):
        at = rows(mine + start * ROWS)
        copy = remote(fin.at[at], fin.at[at], send4.at[k], recv4.at[k], partner)
        copy.start()
        return copy

    arrive4 = [hand_over(last, own)]
    for k in range(last - 1, -1, -1):
        arrive3[k].wait_recv()
        dx, dy = offsets[k]
        source = (place.x - dx + NX) % NX * NY + (place.y - dy + NY) % NY
        arrive4.append(hand_over(k, source))
    for copy in arrive4:
        copy.wait_recv()
    return sent + arrive4


def reduce_scratch():
    half = NX * NY * ROWS
    n, depth = NX * NY, NZH * NZL
    dma = pltpu.SemaphoreType.DMA
    return [
        pltpu.VMEM((2 * half, 128), F32),
        pltpu.VMEM((half, 128), F32),
        pltpu.VMEM((half, 128), F32),
        pltpu.VMEM((n, ROWS, 128), F32),
        pltpu.VMEM((depth, ROWS, 128), F32),
        pltpu.VMEM((2 * half, 128), F32),
    ], [dma((n,)), dma((n,)), dma((n,)), dma((n,)), dma((depth,)), dma((depth,)), dma((n,)), dma((n,)), dma((n,)), dma((n,))]


def iota2(shape):
    return lax.broadcasted_iota(jnp.int32, shape, 0), lax.broadcasted_iota(jnp.int32, shape, 1)


def flatten_planes(crop_ref, wide, cf, lp, fs):
    cf[...] = crop_ref[...].astype(F32)
    for h in range(32):
        pair = [cf[pl.ds(2 * h + e, 16, stride=64), :] for e in range(2)]
        lp[h // 4 * 16 : h // 4 * 16 + 16, h % 4 * 128 : h % 4 * 128 + 128] = jnp.concatenate(pair, axis=1).astype(BF16)
    k, n = iota2((512, 512))
    to = (k // 64 % 2 * 2 + k % 2) * 128 + k // 128 * 32 + k % 64 // 2
    moved = dot_nn(lp[...], ones(to == n))
    for block in range(8):
        for c in range(4):
            fs[16 * c : 16 * c + 16, 128 * block : 128 * block + 128] = moved[
                16 * block : 16 * block + 16, 128 * c : 128 * c + 128
            ].astype(BF16)
    m, n = iota2((64, 64))
    rows = dot_nn(ones(m // 4 % 4 * 16 + m % 4 * 4 + m // 16 == n), fs[...])
    for p in range(4):
        wide[5 + p] = rows[16 * p : 16 * p + 16].astype(BF16)


def whole_kernel(crop_ref, f1_ref, f2_ref, sel_ref, cot_ref, feat_ref, one_ref, two_ref, wide, cots, px, maps, z1s, g2s, g1s,
                 cf, lp, fs, f1s, w1s, w2s, w3s, feats, acc, r0, s0, r1, r2, fin, halo_send, halo_recv, *sems):
    place = Place()
    ready = greet(place, True)
    flatten_planes(crop_ref, wide, cf, lp, fs)
    cots[1] = cot_ref[...].astype(F32).T.astype(BF16)
    halo = Halo(place, wide.at[5:9], cots.at[1], wide, cots, halo_send, halo_recv)
    ready()
    halo.start()
    f1s[108:128, :] = jnp.zeros((20, 32), F32)
    for t in range(27):
        f1s[4 * t : 4 * t + 4, :] = f1_ref[t].astype(F32)
    w1 = dot_nn(f1s[...].T.astype(BF16), sel_ref[...]).astype(BF16)
    for d in range(8):
        w1s[32 * d : 32 * d + 32, :] = w1[:, 256 * d : 256 * d + 256]
    w2s[...] = f2_ref[...].astype(F32).T.astype(BF16)
    for a in range(3):
        w3s[:, 64 * a : 64 * a + 64] = f2_ref[288 * (2 - a) : 288 * (3 - a), :]
    acc[464:512, :] = jnp.zeros((48, 128), F32)
    halo.wait()
    compute(None, place.s, wide, w1s, w2s, w3s, sel_ref, cots, feats, acc.at[0:432], acc.at[432:464],
            px, maps, z1s, g2s, g1s)
    feat_ref[...] = feats[...].T.astype(BF16)
    sent = all_reduce(place, acc, r0, s0, r1, r2, fin, sems)
    two_ref[0:432, :] = fin[0:432, 0:64]
    two_ref[432:864, :] = fin[0:432, 64:128]
    one = fin[432:464, :].T
    for t in range(27):
        one_ref[t] = one[4 * t : 4 * t + 4]
    halo.drain()
    for copy in sent:
        copy.wait_send()


def local(crop, filter_one, filter_two, cotangent):
    sel = jnp.asarray(tap_selection(), BF16)
    buffers, sems = reduce_scratch()
    feat, one, two = pl.pallas_call(
        whole_kernel,
        out_shape=(
            jax.ShapeDtypeStruct((256, 64), BF16),
            jax.ShapeDtypeStruct((27, 4, 32), F32),
            jax.ShapeDtypeStruct((864, 64), F32),
        ),
        scratch_shapes=[
            pltpu.VMEM((14, 16, LANES), BF16),
            pltpu.VMEM((3, 64, 256), BF16),
            pltpu.VMEM((896, LANES), BF16),
            pltpu.VMEM((1728, LANES), BF16),
            pltpu.VMEM((512, LANES), BF16),
            pltpu.VMEM((256, LANES), BF16),
            pltpu.VMEM((512, LANES), BF16),
            pltpu.VMEM((1024, 64), F32),
            pltpu.VMEM((128, 512), BF16),
            pltpu.VMEM((64, LANES), BF16),
            pltpu.VMEM((128, 32), F32),
            pltpu.VMEM((256, 256), BF16),
            pltpu.VMEM((64, 864), BF16),
            pltpu.VMEM((288, 192), BF16),
            pltpu.VMEM((64, 256), F32),
            *buffers,
            pltpu.SemaphoreType.DMA((6,)),
            pltpu.SemaphoreType.DMA((6,)),
            *sems,
        ],
        compiler_params=pltpu.CompilerParams(
            vmem_limit_bytes=60 * 1024 * 1024, collective_id=0, has_side_effects=True
        ),
    )(
        crop.reshape(1024, 64),
        filter_one.reshape(27, 4, 32),
        filter_two.reshape(864, 64),
        sel,
        cotangent.transpose(0, 2, 3, 4, 1).reshape(256, 64),
    )
    feat = feat.reshape(1, 1, 16, 16, 64).transpose(0, 4, 1, 2, 3)
    return feat, one.reshape(3, 3, 3, 4, 32), two.reshape(3, 3, 3, 32, 64)


def solution(mesh):
    placed = (P("dp", None, "space", None, None), P(), P(), P("dp", None, "space", None, None))
    return jax.shard_map(
        local, mesh=mesh, in_specs=placed, out_specs=(P("dp", None, "space", None, None), P(), P()), check_vma=False
    )
```

```python
import functools

import jax
import jax.numpy as jnp
import numpy as np
from jax import lax
from jax.experimental import pallas as pl
from jax.experimental.pallas import tpu as pltpu
from jax.sharding import PartitionSpec as P

F32, BF16 = jnp.float32, jnp.bfloat16
LANES = 1024


def leaky(value):
    return jnp.where(value > 0, value, 0.3 * value)


def dot_nn(a, b):
    return lax.dot_general(a, b, (((1,), (0,)), ((), ())), preferred_element_type=F32)


def dot_nt(a, b):
    return lax.dot_general(a, b, (((1,), (1,)), ((), ())), preferred_element_type=F32)


def split2(value):
    high = value.astype(BF16)
    return high, (value - high.astype(F32)).astype(BF16)


def tap_selection():
    table = np.zeros((128, 8, 256), np.float32)
    for d in range(8):
        dp, dq, dr = d // 4, d // 2 % 2, d % 2
        for pi in range(4):
            for sq in range(2):
                for sr in range(2):
                    for qe in range(2):
                        for re in range(2):
                            qi = (1 + qe) if sq == 0 else (0 if qe else 3)
                            ri = (1 + re) if sr == 0 else (0 if re else 3)
                            a, b, c = pi - dp, qi - dq, ri - dr
                            if min(a, b, c) < 0 or max(a, b, c) > 2:
                                continue
                            for i in range(4):
                                k = pi * 64 + (sq * 2 + sr) * 16 + (qe * 2 + re) * 4 + i
                                table[((a * 3 + b) * 3 + c) * 4 + i, d, k] = 1
    return table.reshape(128, 2048)


def lane_masks(rows):
    lane = lax.broadcasted_iota(jnp.int32, (rows, LANES), 1)
    return lane % 32, lane // 32


def ones(mask):
    return jnp.where(mask, 1.0, 0.0).astype(BF16)


def rolled(value, amount):
    return pltpu.roll(value, amount % LANES, 1)


NX, NY, NZH, NZL = 4, 4, 2, 4
ROWS = 16
HALF = NX * NY * ROWS
MESH = pl.DeviceIdType.MESH


class Place:
    def __init__(self):
        dp, self.s = lax.axis_index("dp"), lax.axis_index("space")
        self.zh, self.x = dp // NX, dp % NX
        self.core = self.s % 2
        self.y = self.s // 2 % NY
        self.zl = self.s // 2 // NY
        self.z = self.zh * NZL + self.zl

    def at(self, x, y, z, core):
        return {"dp": z // NZL * NX + x, "space": (z % NZL * NY + y) * 2 + core}

    def plane_peer(self, dx, dy):
        x, y = (self.x + dx) % NX, (self.y + dy) % NY
        return self.at(x, y, self.z, self.core), x * NY + y

    def plane_source(self, dx, dy):
        return (self.x - dx + NX) % NX * NY + (self.y - dy + NY) % NY

    def depth_peer(self, dz):
        return self.at(self.x, self.y, (self.z + dz) % (NZH * NZL), self.core)

    def depth_source(self, dz):
        return (self.z - dz + NZH * NZL) % (NZH * NZL)

    def partner(self):
        return self.at(self.x, self.y, self.z, 1 - self.core)


def plane_offsets():
    far = lambda d: min(d[0], NX - d[0]) + min(d[1], NY - d[1])
    every = [(dx, dy) for dx in range(NX) for dy in range(NY)]
    return sorted(every, key=lambda d: -far(d))[:-1]


def depth_offsets():
    count = NZH * NZL
    return sorted(range(1, count), key=lambda d: -min(d, count - d))


def remote(src, dst, send, recv, peer):
    copy = pltpu.make_async_remote_copy(
        src_ref=src, dst_ref=dst, send_sem=send, recv_sem=recv, device_id=peer, device_id_type=MESH
    )
    return copy


def started(src, dst, send, recv, peer):
    copy = remote(src, dst, send, recv, peer)
    copy.start()
    return copy


def rows16(start):
    return pl.ds(pl.multiple_of(start, ROWS), ROWS)


def greet(place):
    barrier = pltpu.get_barrier_semaphore()
    count = lax.axis_size("space")
    peers = [place.plane_peer(dx, dy)[0] for dx, dy in plane_offsets()]
    peers += [place.depth_peer(d) for d in depth_offsets()]
    peers += [{"space": (place.s + hop + count) % count} for hop in (1, -1, 2, -2)]
    peers += [place.partner()]
    for peer in peers:
        pl.semaphore_signal(barrier, inc=1, device_id=peer, device_id_type=MESH)
    return lambda: pl.semaphore_wait(barrier, len(peers))


HALO_MOVES = ((1, 3, 1, 4), (-1, 0, 1, 9), (1, 1, 2, 2), (-1, 1, 2, 10), (1, 0, 1, 1), (-1, 3, 1, 12), (2, 3, 1, 0), (-2, 0, 1, 13))


class Halo:
    def __init__(self, place, wide, cots, send, recv):
        self.s, self.count = place.s, lax.axis_size("space")
        self.items = {}
        for k, (hop, own, planes, to) in enumerate(HALO_MOVES):
            self.add(to, hop, wide.at[5 + own : 5 + own + planes], wide.at[to : to + planes], send.at[k], recv.at[k])
            if k == 3:
                self.add("left", 1, cots.at[1], cots.at[0], send.at[8], recv.at[8])
                self.add("right", -1, cots.at[1], cots.at[2], send.at[9], recv.at[9])

    def add(self, name, hop, src, dst, send, recv):
        peer = {"space": (self.s + hop + self.count) % self.count}
        self.items[name] = (hop, dst, remote(src, dst, send, recv, peer))

    def exists(self, hop):
        there = self.s + hop
        return (there >= 0) & (there < self.count)

    def start(self):
        for hop, dst, copy in self.items.values():
            pl.when(self.exists(hop))(copy.start)

    def clear(self):
        for hop, dst, copy in self.items.values():

            @pl.when(jnp.logical_not(self.exists(-hop)))
            def _(dst=dst):
                dst[...] = jnp.zeros(dst.shape, BF16)

    def wait(self, *names):
        for name in names:
            hop, dst, copy = self.items[name]
            pl.when(self.exists(-hop))(copy.wait_recv)

    def drain(self):
        for hop, dst, copy in self.items.values():
            pl.when(self.exists(hop))(copy.wait_send)


class LargeFlow:
    def __init__(self, place, acc, r0, s0, r1, r2, fin, sems):
        self.place, self.acc, self.r0, self.s0, self.r1, self.r2, self.fin = place, acc, r0, s0, r1, r2, fin
        self.sems, self.sent = sems, []
        self.peers = [place.plane_peer(dx, dy) for dx, dy in plane_offsets()]
        self.own = place.x * NY + place.y
        self.mine = place.core * HALF
        self.other = HALF - self.mine
        self.order = [j for _, j in self.peers] + [self.own]

    def go(self, *args):
        copy = started(*args)
        self.sent.append(copy)
        return copy

    def halves(self):
        send, recv = self.sems[0:2]
        self.step0 = [
            self.go(self.acc.at[rows16(self.other + j * ROWS)], self.r0.at[rows16(j * ROWS)], send.at[k], recv.at[k],
                    self.place.partner())
            for k, j in enumerate(self.order)
        ]

    def shares(self):
        send, recv = self.sems[2:4]
        self.step1 = []

        def pass_on(k):
            peer, j = self.peers[k]
            self.step1.append(self.go(self.s0.at[rows16(j * ROWS)], self.r1.at[k], send.at[k], recv.at[k], peer))

        count = len(self.peers)
        for k, j in enumerate(self.order):
            self.step0[k].wait_recv()
            total = self.acc[rows16(self.mine + j * ROWS), :] + self.r0[rows16(j * ROWS), :]
            if k < count:
                self.s0[rows16(j * ROWS), :] = total.astype(BF16)
            else:
                self.r2[self.place.z] = total
            if k >= 1:
                pass_on(k - 1)

    def depth(self):
        total = self.r2[self.place.z]
        for k in range(len(self.peers) - 1, -1, -1):
            self.step1[k].wait_recv()
            total = total + self.r1[k].astype(F32)
        self.r2[self.place.z] = total
        send, recv = self.sems[4:6]
        here = self.r2.at[self.place.z]
        self.step2 = [
            self.go(here, here, send.at[k], recv.at[k], self.place.depth_peer(d)) for k, d in enumerate(depth_offsets())
        ]

    def gather(self):
        for copy in self.step2:
            copy.wait_recv()
        total = self.r2[0]
        for z in range(1, NZH * NZL):
            total = total + self.r2[z]
        at = rows16(self.mine + self.own * ROWS)
        self.fin[at, :] = total.astype(BF16)
        send, recv = self.sems[6:8]
        here = self.fin.at[at]
        self.step3 = [self.go(here, here, send.at[k], recv.at[k], peer) for k, (peer, _) in enumerate(self.peers)]
        self.step4 = []
        self.hand_over(self.own)

    def hand_over(self, share):
        send, recv = self.sems[8:10]
        k = len(self.step4)
        here = self.fin.at[rows16(self.mine + share * ROWS)]
        self.step4.append(self.go(here, here, send.at[k], recv.at[k], self.place.partner()))

    def give_back(self):
        offsets = plane_offsets()
        for k in range(len(offsets) - 1, -1, -1):
            self.step3[k].wait_recv()
            self.hand_over(self.place.plane_source(*offsets[k]))

    def finish(self):
        for copy in self.step4:
            copy.wait_recv()


class SmallFlow:
    def __init__(self, place, acc, r0, q1, q2, out, sems):
        self.place, self.acc, self.r0, self.q1, self.q2, self.out = place, acc, r0, q1, q2, out
        self.sems, self.sent = sems, []
        self.mine = place.core * ROWS
        self.own = place.x * NY + place.y

    def go(self, *args):
        copy = started(*args)
        self.sent.append(copy)
        return copy

    def halves(self):
        send, recv = self.sems[0:2]
        self.step0 = self.go(self.acc.at[rows16(ROWS - self.mine)], self.r0, send.at[0], recv.at[0], self.place.partner())

    def plane(self):
        self.step0.wait_recv()
        self.q1[self.own] = (self.acc[rows16(self.mine), :] + self.r0[...]).astype(BF16)
        send, recv = self.sems[2:4]
        here = self.q1.at[self.own]
        self.step1 = [
            self.go(here, here, send.at[k], recv.at[k], self.place.plane_peer(dx, dy)[0])
            for k, (dx, dy) in enumerate(plane_offsets())
        ]

    def depth(self):
        for copy in self.step1:
            copy.wait_recv()
        total = self.q1[0].astype(F32)
        for j in range(1, NX * NY):
            total = total + self.q1[j].astype(F32)
        self.q2[self.place.z] = total
        send, recv = self.sems[4:6]
        here = self.q2.at[self.place.z]
        self.step2 = [
            self.go(here, here, send.at[k], recv.at[k], self.place.depth_peer(d)) for k, d in enumerate(depth_offsets())
        ]

    def give_back(self):
        for copy in self.step2:
            copy.wait_recv()
        total = self.q2[0]
        for z in range(1, NZH * NZL):
            total = total + self.q2[z]
        at = rows16(self.mine)
        self.out[at, :] = total
        send, recv = self.sems[6:8]
        here = self.out.at[at]
        self.step3 = self.go(here, here, send.at[0], recv.at[0], self.place.partner())

    def finish(self):
        self.step3.wait_recv()


def flow_scratch():
    n, depth = NX * NY, NZH * NZL
    dma = pltpu.SemaphoreType.DMA
    large = [
        pltpu.VMEM((2 * HALF, 128), F32),
        pltpu.VMEM((HALF, 128), F32),
        pltpu.VMEM((HALF, 128), BF16),
        pltpu.VMEM((n - 1, ROWS, 128), BF16),
        pltpu.VMEM((depth, ROWS, 128), F32),
        pltpu.VMEM((2 * HALF, 128), BF16),
    ]
    large_sems = [dma((k,)) for k in (n, n, n - 1, n - 1, depth - 1, depth - 1, n - 1, n - 1, n, n)]
    small = [
        pltpu.VMEM((2 * ROWS, 128), F32),
        pltpu.VMEM((ROWS, 128), F32),
        pltpu.VMEM((n, ROWS, 128), BF16),
        pltpu.VMEM((depth, ROWS, 128), F32),
        pltpu.VMEM((2 * ROWS, 128), F32),
    ]
    small_sems = [dma((k,)) for k in (1, 1, n - 1, n - 1, depth - 1, depth - 1, 1, 1)]
    return large, large_sems, small, small_sems


def iota2(shape):
    return lax.broadcasted_iota(jnp.int32, shape, 0), lax.broadcasted_iota(jnp.int32, shape, 1)


def flatten_planes(crop_ref, wide, cf, lp, fs):
    cf[...] = crop_ref[...].astype(F32)
    for h in range(32):
        pair = [cf[pl.ds(2 * h + e, 16, stride=64), :] for e in range(2)]
        lp[h // 4 * 16 : h // 4 * 16 + 16, h % 4 * 128 : h % 4 * 128 + 128] = jnp.concatenate(pair, axis=1).astype(BF16)
    k, n = iota2((512, 512))
    to = (k // 64 % 2 * 2 + k % 2) * 128 + k // 128 * 32 + k % 64 // 2
    moved = dot_nn(lp[...], ones(to == n))
    for block in range(8):
        for c in range(4):
            fs[16 * c : 16 * c + 16, 128 * block : 128 * block + 128] = moved[
                16 * block : 16 * block + 16, 128 * c : 128 * c + 128
            ].astype(BF16)
    m, n = iota2((64, 64))
    rows = dot_nn(ones(m // 4 % 4 * 16 + m % 4 * 4 + m // 16 == n), fs[...])
    for p in range(4):
        wide[5 + p] = rows[16 * p : 16 * p + 16].astype(BF16)


class Local:
    def __init__(self, s, wide, cots, px, maps, z1s, g2s, g1s, w1s, w2s, w3s):
        self.wide, self.cots, self.px, self.maps = wide, cots, px, maps
        self.z1s, self.g2s, self.g1s, self.w1s, self.w2s, self.w3s = z1s, g2s, g1s, w1s, w2s, w3s
        r, q = lane_masks(16)
        row = lax.broadcasted_iota(jnp.int32, (16, LANES), 0)
        q_odd, r_odd = row // 8 == 1, row // 4 % 2 == 1
        self.r_up, self.r_down = ones(r_odd & (r != 0)), ones(~r_odd & (r != 31))
        self.q_up, self.q_down = ones(q_odd & (q != 0)), ones(~q_odd & (q != 31))
        self.left_ok = jnp.where(s > 0, 0.125, 0.0)
        self.right_ok = jnp.where(s < lax.axis_size("space") - 1, 0.125, 0.0)
        r, q = lane_masks(32)
        self.keep, self.keep_ones = {}, {}
        for db in (-1, 0, 1):
            for dc in (-1, 0, 1):
                ok = jnp.ones((32, LANES), jnp.bool_)
                if db:
                    ok = ok & ((q != 0) if db < 0 else (q != 31))
                if dc:
                    ok = ok & ((r != 0) if dc < 0 else (r != 31))
                self.keep[db, dc] = ok
                self.keep_ones[db, dc] = ones(ok)
        k, n = iota2((128, 512))
        self.spread = ones((n // 64 == k // 16) & (n % 32 // 2 == k % 16))
        k, n = iota2((256, 64))
        self.collect = ones((k // 64 == n // 16) & (k % 32 // 2 == n % 16))

    def patch(self, *planes):
        for plane in planes:
            x = self.wide[plane]
            xr = rolled(x, 1) * self.r_up + rolled(x, -1) * self.r_down
            xq = rolled(x, 32) * self.q_up + rolled(x, -32) * self.q_down
            xqr = rolled(xr, 32) * self.q_up + rolled(xr, -32) * self.q_down
            for k, piece in enumerate((x, xr, xq, xqr)):
                self.px[plane * 64 + k * 16 : plane * 64 + k * 16 + 16, :] = piece

    def first(self, plane):
        z = dot_nn(self.w1s[...], self.px[plane * 128 : plane * 128 + 256, :])
        if plane in (2, 3):
            self.z1s[(plane - 2) * 256 : (plane - 1) * 256, :] = z.astype(BF16)
        z = leaky(z)
        total = z[0:32]
        for d in range(1, 8):
            total = total + z[d * 32 : d * 32 + 32]
        a1 = (total * (self.left_ok if plane < 2 else self.right_ok if plane > 3 else 0.125)).astype(BF16)
        for b in range(3):
            for c in range(3):
                v = a1
                if (b, c) != (1, 1):
                    v = rolled(v, -(32 * (b - 1) + (c - 1))) * self.keep_ones[b - 1, c - 1]
                at = plane * 288 + (b * 3 + c) * 32
                self.maps[at : at + 32, :] = v

    def second(self, plane):
        z = dot_nn(self.w2s[...], self.maps[plane * 288 : plane * 288 + 864, :])
        cot = self.cots[(0, 1, 1, 2)[plane]]
        wide = jnp.concatenate([dot_nn(cot[:, 0:128], self.spread), dot_nn(cot[:, 128:256], self.spread)], axis=1) * 0.125
        self.g2s[plane * 64 : plane * 64 + 64, :] = jnp.where(z > 0, wide, 0.3 * wide).astype(BF16)
        return leaky(z)

    def features(self, pair, feats):
        high, low = split2(pair)
        for j in range(4):
            lanes = slice(256 * j, 256 * j + 256)
            feats[:, 64 * j : 64 * j + 64] = (
                dot_nn(high[:, lanes], self.collect) + dot_nn(low[:, lanes], self.collect)
            ) * 0.125

    def grad_two(self, acc, start):
        at = pl.ds(pl.multiple_of(start, HALF), HALF)
        parts = []
        for fold in range(2):
            part = None
            for p in range(2):
                first = pl.multiple_of(start + 288 * (p + 1) + 432 * fold, 16)
                term = dot_nt(self.maps[pl.ds(first, HALF), :], self.g2s[64 * (p + 1) : 64 * (p + 2), :])
                part = term if part is None else part + term
            parts.append(part)
        acc[at, :] = jnp.concatenate(parts, axis=1)

    def back(self, plane):
        u = dot_nn(self.w3s[...], self.g2s[plane * 64 : plane * 64 + 192, :])
        back = None
        for b in range(3):
            for c in range(3):
                v = u[(b * 3 + c) * 32 : (b * 3 + c) * 32 + 32]
                if (b, c) != (1, 1):
                    v = rolled(v, -(32 * (1 - b) + (1 - c)))
                    v = jnp.where(self.keep[1 - b, 1 - c], v, 0.0)
                back = v if back is None else back + v
        back = back * 0.125
        low = 0.3 * back
        for d in range(8):
            at = plane * 256 + d * 32
            self.g1s[at : at + 32, :] = jnp.where(self.z1s[at : at + 32, :].astype(F32) > 0, back, low).astype(BF16)

    def grad_one(self, sel_ref, acc):
        gram = dot_nt(self.g1s[0:256, :], self.px[256:512, :]) + dot_nt(self.g1s[256:512, :], self.px[384:640, :])
        total = None
        for d in range(8):
            high, low = split2(gram[d * 32 : d * 32 + 32])
            sel = sel_ref[:, d * 256 : d * 256 + 256]
            term = dot_nt(high, sel) + dot_nt(low, sel)
            total = term if total is None else total + term
        acc[...] = total


def whole_kernel(crop_hbm, f1_hbm, f2_hbm, sel_hbm, cot_hbm, feat_ref, one_ref, two_ref,
                 crop_ref, f1_ref, f2_ref, sel_ref, cot_ref, wide, cots, px, maps, z1s, g2s, g1s,
                 cf, lp, fs, f1s, w1s, w2s, w3s, feats, fetch, halo_send, halo_recv, *flows):
    place = Place()
    ready = greet(place)
    pairs = ((crop_hbm, crop_ref), (cot_hbm, cot_ref), (f1_hbm, f1_ref), (sel_hbm, sel_ref), (f2_hbm, f2_ref))
    fetched = [pltpu.make_async_copy(src, dst, fetch.at[k]) for k, (src, dst) in enumerate(pairs)]
    for copy in fetched:
        copy.start()
    halo = Halo(place, wide, cots, halo_send, halo_recv)
    halo.clear()
    local = Local(place.s, wide, cots, px, maps, z1s, g2s, g1s, w1s, w2s, w3s)
    large = LargeFlow(place, *flows[0:6], flows[6:16])
    small = SmallFlow(place, *flows[16:21], flows[21:29])
    fetched[0].wait()
    flatten_planes(crop_ref, wide, cf, lp, fs)
    fetched[1].wait()
    cots[1] = cot_ref[...].astype(F32).T.astype(BF16)
    ready()
    halo.start()
    fetched[2].wait()
    f1s[108:128, :] = jnp.zeros((20, 32), F32)
    for t in range(27):
        f1s[4 * t : 4 * t + 4, :] = f1_ref[t].astype(F32)
    fetched[3].wait()
    w1 = dot_nn(f1s[...].T.astype(BF16), sel_ref[...]).astype(BF16)
    for d in range(8):
        w1s[32 * d : 32 * d + 32, :] = w1[:, 256 * d : 256 * d + 256]
    fetched[4].wait()
    w2s[...] = f2_ref[...].astype(F32).T.astype(BF16)
    for a in range(3):
        w3s[:, 64 * a : 64 * a + 64] = f2_ref[288 * (2 - a) : 288 * (3 - a), :]
    local.patch(5, 6, 7, 8)
    halo.wait(4)
    local.patch(4)
    local.first(2)
    halo.wait(9)
    local.patch(9)
    local.first(3)
    halo.wait(2)
    local.patch(2, 3)
    local.first(1)
    halo.wait(10)
    local.patch(10, 11)
    local.first(4)
    pair = local.second(1)
    pair = pair + local.second(2)
    local.features(pair, feats)
    local.grad_two(large.acc, large.other)
    large.halves()
    local.grad_two(large.acc, large.mine)
    halo.wait(0, 1)
    local.patch(0, 1)
    local.first(0)
    halo.wait("left")
    local.second(0)
    halo.wait(12, 13)
    local.patch(12, 13)
    local.first(5)
    halo.wait("right")
    local.second(3)
    large.shares()
    local.back(0)
    local.back(1)
    local.grad_one(sel_ref, small.acc)
    small.halves()
    feat_ref[...] = feats[...].T.astype(BF16)
    small.plane()
    large.depth()
    large.gather()
    small.depth()
    large.give_back()
    small.give_back()
    large.finish()
    two_ref[0:432, :] = large.fin[0:432, 0:64].astype(F32)
    two_ref[432:864, :] = large.fin[0:432, 64:128].astype(F32)
    small.finish()
    one = small.out[...].T
    for t in range(27):
        one_ref[t] = one[4 * t : 4 * t + 4]
    halo.drain()
    for copy in large.sent + small.sent:
        copy.wait_send()


def local(crop, filter_one, filter_two, cotangent):
    sel = jnp.asarray(tap_selection(), BF16)
    large, large_sems, small, small_sems = flow_scratch()
    hbm = pl.BlockSpec(memory_space=pltpu.HBM)
    operands = (
        crop.reshape(1024, 64),
        filter_one.reshape(27, 4, 32),
        filter_two.reshape(864, 64),
        sel,
        cotangent.transpose(0, 2, 3, 4, 1).reshape(256, 64),
    )
    feat, one, two = pl.pallas_call(
        whole_kernel,
        out_shape=(
            jax.ShapeDtypeStruct((256, 64), BF16),
            jax.ShapeDtypeStruct((27, 4, 32), F32),
            jax.ShapeDtypeStruct((864, 64), F32),
        ),
        in_specs=[hbm] * 5,
        scratch_shapes=[
            pltpu.VMEM((1024, 64), BF16),
            pltpu.VMEM((27, 4, 32), BF16),
            pltpu.VMEM((864, 64), BF16),
            pltpu.VMEM((128, 2048), BF16),
            pltpu.VMEM((256, 64), BF16),
            pltpu.VMEM((14, 16, LANES), BF16),
            pltpu.VMEM((3, 64, 256), BF16),
            pltpu.VMEM((896, LANES), BF16),
            pltpu.VMEM((1728, LANES), BF16),
            pltpu.VMEM((512, LANES), BF16),
            pltpu.VMEM((256, LANES), BF16),
            pltpu.VMEM((512, LANES), BF16),
            pltpu.VMEM((1024, 64), F32),
            pltpu.VMEM((128, 512), BF16),
            pltpu.VMEM((64, LANES), BF16),
            pltpu.VMEM((128, 32), F32),
            pltpu.VMEM((256, 256), BF16),
            pltpu.VMEM((64, 864), BF16),
            pltpu.VMEM((288, 192), BF16),
            pltpu.VMEM((64, 256), F32),
            pltpu.SemaphoreType.DMA((5,)),
            pltpu.SemaphoreType.DMA((10,)),
            pltpu.SemaphoreType.DMA((10,)),
            *large,
            *large_sems,
            *small,
            *small_sems,
        ],
        compiler_params=pltpu.CompilerParams(
            vmem_limit_bytes=32 * 1024 * 1024, collective_id=0, has_side_effects=True
        ),
    )(*[pltpu.with_memory_space_constraint(value, pltpu.HBM) for value in operands])
    feat = feat.reshape(1, 1, 16, 16, 64).transpose(0, 4, 1, 2, 3)
    return feat, one.reshape(3, 3, 3, 4, 32), two.reshape(3, 3, 3, 32, 64)


def solution(mesh):
    placed = (P("dp", None, "space", None, None), P(), P(), P("dp", None, "space", None, None))
    return jax.shard_map(
        local, mesh=mesh, in_specs=placed, out_specs=(P("dp", None, "space", None, None), P(), P()), check_vma=False
    )
```

```python
import functools

import jax
import jax.numpy as jnp
import numpy as np
from jax import lax
from jax.experimental import pallas as pl
from jax.experimental.pallas import tpu as pltpu
from jax.sharding import PartitionSpec as P

F32, BF16 = jnp.float32, jnp.bfloat16
LANES = 1024


def leaky(value):
    return jnp.where(value > 0, value, 0.3 * value)


def dot_nn(a, b):
    return lax.dot_general(a, b, (((1,), (0,)), ((), ())), preferred_element_type=F32)


def dot_nt(a, b):
    return lax.dot_general(a, b, (((1,), (1,)), ((), ())), preferred_element_type=F32)


def split2(value):
    high = value.astype(BF16)
    return high, (value - high.astype(F32)).astype(BF16)


def tap_selection():
    table = np.zeros((128, 8, 256), np.float32)
    for d in range(8):
        dp, dq, dr = d // 4, d // 2 % 2, d % 2
        for pi in range(4):
            for sq in range(2):
                for sr in range(2):
                    for qe in range(2):
                        for re in range(2):
                            qi = (1 + qe) if sq == 0 else (0 if qe else 3)
                            ri = (1 + re) if sr == 0 else (0 if re else 3)
                            a, b, c = pi - dp, qi - dq, ri - dr
                            if min(a, b, c) < 0 or max(a, b, c) > 2:
                                continue
                            for i in range(4):
                                k = pi * 64 + (sq * 2 + sr) * 16 + (qe * 2 + re) * 4 + i
                                table[((a * 3 + b) * 3 + c) * 4 + i, d, k] = 1
    return table.reshape(128, 2048)


def lane_masks(rows):
    lane = lax.broadcasted_iota(jnp.int32, (rows, LANES), 1)
    return lane % 32, lane // 32


def ones(mask):
    return jnp.where(mask, 1.0, 0.0).astype(BF16)


def rolled(value, amount):
    return pltpu.roll(value, amount % LANES, 1)


NX, NY, NZH, NZL = 4, 4, 2, 4
ROWS = 16
HALF = NX * NY * ROWS
MESH = pl.DeviceIdType.MESH


class Place:
    def __init__(self):
        dp, self.s = lax.axis_index("dp"), lax.axis_index("space")
        self.zh, self.x = dp // NX, dp % NX
        self.core = self.s % 2
        self.y = self.s // 2 % NY
        self.zl = self.s // 2 // NY
        self.z = self.zh * NZL + self.zl

    def at(self, x, y, z, core):
        return {"dp": z // NZL * NX + x, "space": (z % NZL * NY + y) * 2 + core}

    def plane_peers(self):
        peers = []
        for dx, dy, flip in plane_offsets():
            x, y = (self.x + dx) % NX, (self.y + dy) % NY
            core = 1 - self.core if flip else self.core
            peers.append((self.at(x, y, self.z, core), core, core * HALF + (x * NY + y) * ROWS))
        return peers

    def depth_peer(self, dz):
        return self.at(self.x, self.y, (self.z + dz) % (NZH * NZL), self.core)

    def partner(self):
        return self.at(self.x, self.y, self.z, 1 - self.core)


def plane_offsets():
    far = lambda d: min(d[0], NX - d[0]) + min(d[1], NY - d[1])
    every = [(dx, dy, flip) for dx in range(NX) for dy in range(NY) for flip in (1, 0)]
    return sorted(every, key=lambda d: -far(d))[:-1]


def depth_offsets():
    count = NZH * NZL
    return sorted(range(1, count), key=lambda d: -min(d, count - d))


def remote(src, dst, send, recv, peer):
    copy = pltpu.make_async_remote_copy(
        src_ref=src, dst_ref=dst, send_sem=send, recv_sem=recv, device_id=peer, device_id_type=MESH
    )
    return copy


def rows16(start):
    return pl.ds(pl.multiple_of(start, ROWS), ROWS)


def greet(place):
    barrier = pltpu.get_barrier_semaphore()
    count = lax.axis_size("space")
    peers = [peer for peer, _, _ in place.plane_peers()]
    peers += [place.depth_peer(d) for d in depth_offsets()]
    peers += [{"space": (place.s + hop + count) % count} for hop in (1, -1, 2, -2)]
    for peer in peers:
        pl.semaphore_signal(barrier, inc=1, device_id=peer, device_id_type=MESH)
    return lambda: pl.semaphore_wait(barrier, len(peers))


HALO_MOVES = ((1, 3, 1, 4), (-1, 0, 1, 9), (1, 1, 2, 2), (-1, 1, 2, 10), (1, 0, 1, 1), (-1, 3, 1, 12), (2, 3, 1, 0), (-2, 0, 1, 13))


class Halo:
    def __init__(self, place, wide, cots, send, recv):
        self.s, self.count = place.s, lax.axis_size("space")
        self.items = {}
        for k, (hop, own, planes, to) in enumerate(HALO_MOVES):
            self.add(to, hop, wide.at[5 + own : 5 + own + planes], wide.at[to : to + planes], send.at[k], recv.at[k])
            if k == 3:
                self.add("left", 1, cots.at[1], cots.at[0], send.at[8], recv.at[8])
                self.add("right", -1, cots.at[1], cots.at[2], send.at[9], recv.at[9])

    def add(self, name, hop, src, dst, send, recv):
        peer = {"space": (self.s + hop + self.count) % self.count}
        self.items[name] = (hop, dst, remote(src, dst, send, recv, peer))

    def exists(self, hop):
        there = self.s + hop
        return (there >= 0) & (there < self.count)

    def start(self):
        for hop, dst, copy in self.items.values():
            pl.when(self.exists(hop))(copy.start)

    def clear(self):
        for hop, dst, copy in self.items.values():

            @pl.when(jnp.logical_not(self.exists(-hop)))
            def _(dst=dst):
                dst[...] = jnp.zeros(dst.shape, BF16)

    def wait(self, *names):
        for name in names:
            hop, dst, copy = self.items[name]
            pl.when(self.exists(-hop))(copy.wait_recv)

    def drain(self):
        for hop, dst, copy in self.items.values():
            pl.when(self.exists(hop))(copy.wait_send)


class Flow:
    def __init__(self, place, sems):
        self.place, self.sems, self.sent = place, sems, []

    def send(self, phase, items):
        for src, dst, peer in items:
            remote(src, dst, self.sems.at[0, phase], self.sems.at[1, phase], peer).start()

    def arrive(self, phase, whole):
        self.sent.append((phase, whole))
        remote(whole, whole, self.sems.at[0, phase], self.sems.at[1, phase], self.place.partner()).wait_recv()

    def drain(self):
        for phase, whole in self.sent:
            remote(whole, whole, self.sems.at[0, phase], self.sems.at[1, phase], self.place.partner()).wait_send()


class LargeFlow(Flow):
    def __init__(self, place, acc, accb, r1, r2, fin, sems):
        super().__init__(place, sems)
        self.acc, self.accb, self.r1, self.r2, self.fin = acc, accb, r1, r2, fin
        self.peers = place.plane_peers()
        self.own = place.core * HALF + (place.x * NY + place.y) * ROWS

    def shares(self, half):
        at = slice(half * HALF, half * HALF + HALF)
        self.accb[at, :] = self.acc[at, :].astype(BF16)
        for k, (peer, core, row) in enumerate(self.peers):
            go = remote(self.accb.at[rows16(row)], self.r1.at[k], self.sems.at[0, 0], self.sems.at[1, 0], peer)
            pl.when(core == half)(go.start)

    def depth(self):
        self.arrive(0, self.r1)
        total = self.acc[rows16(self.own), :]
        for k in range(len(self.peers)):
            total = total + self.r1[k].astype(F32)
        self.r2[self.place.z] = total
        here = self.r2.at[self.place.z]
        self.send(1, [(here, here, self.place.depth_peer(d)) for d in depth_offsets()])

    def gather(self):
        self.arrive(1, self.r2.at[1:])
        total = self.r2[0]
        for z in range(1, NZH * NZL):
            total = total + self.r2[z]
        self.fin[rows16(self.own), :] = total.astype(BF16)
        here = self.fin.at[rows16(self.own)]
        self.send(2, [(here, here, peer) for peer, _, _ in self.peers])

    def finish(self):
        self.arrive(2, self.fin.at[ROWS:])


class SmallFlow(Flow):
    def __init__(self, place, acc, accb, q1, q2, out, sems):
        super().__init__(place, sems)
        self.acc, self.accb, self.q1, self.q2, self.out = acc, accb, q1, q2, out
        self.mine = place.core * ROWS
        self.own = place.core * NX * NY + place.x * NY + place.y

    def shares(self):
        for half in range(2):
            self.accb[half] = self.acc[half * ROWS : half * ROWS + ROWS, :].astype(BF16)
        self.q1[self.own] = self.accb[self.place.core]
        there = self.q1.at[self.own]
        self.send(0, [(self.accb.at[core], there, peer) for peer, core, _ in self.place.plane_peers()])

    def depth(self):
        self.arrive(0, self.q1.at[1:])
        total = self.q1[0].astype(F32)
        for j in range(1, 2 * NX * NY):
            total = total + self.q1[j].astype(F32)
        self.q2[self.place.z] = total
        here = self.q2.at[self.place.z]
        self.send(1, [(here, here, self.place.depth_peer(d)) for d in depth_offsets()])

    def give_back(self):
        self.arrive(1, self.q2.at[1:])
        total = self.q2[0]
        for z in range(1, NZH * NZL):
            total = total + self.q2[z]
        self.out[rows16(self.mine), :] = total
        here = self.out.at[rows16(self.mine)]
        self.send(2, [(here, here, self.place.partner())])

    def finish(self):
        self.arrive(2, self.out.at[0:ROWS])


def flow_scratch():
    n, depth = 2 * NX * NY, NZH * NZL
    large = [
        pltpu.VMEM((2 * HALF, 128), F32),
        pltpu.VMEM((2 * HALF, 128), BF16),
        pltpu.VMEM((n - 1, ROWS, 128), BF16),
        pltpu.VMEM((depth, ROWS, 128), F32),
        pltpu.VMEM((2 * HALF, 128), BF16),
        pltpu.SemaphoreType.DMA((2, 3)),
    ]
    small = [
        pltpu.VMEM((2 * ROWS, 128), F32),
        pltpu.VMEM((2, ROWS, 128), BF16),
        pltpu.VMEM((n, ROWS, 128), BF16),
        pltpu.VMEM((depth, ROWS, 128), F32),
        pltpu.VMEM((2 * ROWS, 128), F32),
        pltpu.SemaphoreType.DMA((2, 3)),
    ]
    return large, small


def iota2(shape):
    return lax.broadcasted_iota(jnp.int32, shape, 0), lax.broadcasted_iota(jnp.int32, shape, 1)


def flatten_planes(crop_ref, wide, cf, lp, fs):
    cf[...] = crop_ref[...].astype(F32)
    for h in range(32):
        pair = [cf[pl.ds(2 * h + e, 16, stride=64), :] for e in range(2)]
        lp[h // 4 * 16 : h // 4 * 16 + 16, h % 4 * 128 : h % 4 * 128 + 128] = jnp.concatenate(pair, axis=1).astype(BF16)
    k, n = iota2((512, 512))
    to = (k // 64 % 2 * 2 + k % 2) * 128 + k // 128 * 32 + k % 64 // 2
    moved = dot_nn(lp[...], ones(to == n))
    for block in range(8):
        for c in range(4):
            fs[16 * c : 16 * c + 16, 128 * block : 128 * block + 128] = moved[
                16 * block : 16 * block + 16, 128 * c : 128 * c + 128
            ].astype(BF16)
    m, n = iota2((64, 64))
    rows = dot_nn(ones(m // 4 % 4 * 16 + m % 4 * 4 + m // 16 == n), fs[...])
    for p in range(4):
        wide[5 + p] = rows[16 * p : 16 * p + 16].astype(BF16)


class Local:
    def __init__(self, s, wide, cots, px, maps, z1s, g2s, g1s, w1s, w2s, w3s):
        self.wide, self.cots, self.px, self.maps = wide, cots, px, maps
        self.z1s, self.g2s, self.g1s, self.w1s, self.w2s, self.w3s = z1s, g2s, g1s, w1s, w2s, w3s
        r, q = lane_masks(16)
        row = lax.broadcasted_iota(jnp.int32, (16, LANES), 0)
        q_odd, r_odd = row // 8 == 1, row // 4 % 2 == 1
        self.r_up, self.r_down = ones(r_odd & (r != 0)), ones(~r_odd & (r != 31))
        self.q_up, self.q_down = ones(q_odd & (q != 0)), ones(~q_odd & (q != 31))
        self.left_ok = jnp.where(s > 0, 0.125, 0.0)
        self.right_ok = jnp.where(s < lax.axis_size("space") - 1, 0.125, 0.0)
        r, q = lane_masks(32)
        self.keep, self.keep_ones = {}, {}
        for db in (-1, 0, 1):
            for dc in (-1, 0, 1):
                ok = jnp.ones((32, LANES), jnp.bool_)
                if db:
                    ok = ok & ((q != 0) if db < 0 else (q != 31))
                if dc:
                    ok = ok & ((r != 0) if dc < 0 else (r != 31))
                self.keep[db, dc] = ok
                self.keep_ones[db, dc] = ones(ok)
        k, n = iota2((128, 512))
        self.spread = ones((n // 64 == k // 16) & (n % 32 // 2 == k % 16))
        k, n = iota2((256, 64))
        self.collect = ones((k // 64 == n // 16) & (k % 32 // 2 == n % 16))

    def patch(self, *planes):
        for plane in planes:
            x = self.wide[plane]
            xr = rolled(x, 1) * self.r_up + rolled(x, -1) * self.r_down
            xq = rolled(x, 32) * self.q_up + rolled(x, -32) * self.q_down
            xqr = rolled(xr, 32) * self.q_up + rolled(xr, -32) * self.q_down
            for k, piece in enumerate((x, xr, xq, xqr)):
                self.px[plane * 64 + k * 16 : plane * 64 + k * 16 + 16, :] = piece

    def first(self, plane):
        z = dot_nn(self.w1s[...], self.px[plane * 128 : plane * 128 + 256, :])
        if plane in (2, 3):
            self.z1s[(plane - 2) * 256 : (plane - 1) * 256, :] = z.astype(BF16)
        z = leaky(z)
        total = z[0:32]
        for d in range(1, 8):
            total = total + z[d * 32 : d * 32 + 32]
        a1 = (total * (self.left_ok if plane < 2 else self.right_ok if plane > 3 else 0.125)).astype(BF16)
        for b in range(3):
            for c in range(3):
                v = a1
                if (b, c) != (1, 1):
                    v = rolled(v, -(32 * (b - 1) + (c - 1))) * self.keep_ones[b - 1, c - 1]
                at = plane * 288 + (b * 3 + c) * 32
                self.maps[at : at + 32, :] = v

    def second(self, plane):
        z = dot_nn(self.w2s[...], self.maps[plane * 288 : plane * 288 + 864, :])
        cot = self.cots[(0, 1, 1, 2)[plane]]
        wide = jnp.concatenate([dot_nn(cot[:, 0:128], self.spread), dot_nn(cot[:, 128:256], self.spread)], axis=1) * 0.125
        self.g2s[plane * 64 : plane * 64 + 64, :] = jnp.where(z > 0, wide, 0.3 * wide).astype(BF16)
        return leaky(z)

    def features(self, pair, feats):
        high, low = split2(pair)
        for j in range(4):
            lanes = slice(256 * j, 256 * j + 256)
            feats[:, 64 * j : 64 * j + 64] = (
                dot_nn(high[:, lanes], self.collect) + dot_nn(low[:, lanes], self.collect)
            ) * 0.125

    def grad_two(self, acc, half):
        parts = []
        for fold in range(2):
            part = None
            for p in range(2):
                first = half * HALF + 288 * (p + 1) + 432 * fold
                term = dot_nt(self.maps[first : first + HALF, :], self.g2s[64 * (p + 1) : 64 * (p + 2), :])
                part = term if part is None else part + term
            parts.append(part)
        acc[half * HALF : half * HALF + HALF, :] = jnp.concatenate(parts, axis=1)

    def back(self, plane):
        u = dot_nn(self.w3s[...], self.g2s[plane * 64 : plane * 64 + 192, :])
        back = None
        for b in range(3):
            for c in range(3):
                v = u[(b * 3 + c) * 32 : (b * 3 + c) * 32 + 32]
                if (b, c) != (1, 1):
                    v = rolled(v, -(32 * (1 - b) + (1 - c)))
                    v = jnp.where(self.keep[1 - b, 1 - c], v, 0.0)
                back = v if back is None else back + v
        back = back * 0.125
        low = 0.3 * back
        for d in range(8):
            at = plane * 256 + d * 32
            self.g1s[at : at + 32, :] = jnp.where(self.z1s[at : at + 32, :].astype(F32) > 0, back, low).astype(BF16)

    def grad_one(self, sel_ref, acc):
        gram = dot_nt(self.g1s[0:256, :], self.px[256:512, :]) + dot_nt(self.g1s[256:512, :], self.px[384:640, :])
        total = None
        for d in range(8):
            high, low = split2(gram[d * 32 : d * 32 + 32])
            sel = sel_ref[:, d * 256 : d * 256 + 256]
            term = dot_nt(high, sel) + dot_nt(low, sel)
            total = term if total is None else total + term
        acc[...] = total


def whole_kernel(crop_hbm, f1_hbm, f2_hbm, sel_hbm, cot_hbm, feat_ref, one_ref, two_ref,
                 crop_ref, f1_ref, f2_ref, sel_ref, cot_ref, wide, cots, px, maps, z1s, g2s, g1s,
                 cf, lp, fs, f1s, w1s, w2s, w3s, feats, fetch, halo_send, halo_recv, *flows):
    place = Place()
    ready = greet(place)
    pairs = ((crop_hbm, crop_ref), (cot_hbm, cot_ref), (f1_hbm, f1_ref), (sel_hbm, sel_ref), (f2_hbm, f2_ref))
    fetched = [pltpu.make_async_copy(src, dst, fetch.at[k]) for k, (src, dst) in enumerate(pairs)]
    for copy in fetched:
        copy.start()
    halo = Halo(place, wide, cots, halo_send, halo_recv)
    halo.clear()
    local = Local(place.s, wide, cots, px, maps, z1s, g2s, g1s, w1s, w2s, w3s)
    large = LargeFlow(place, *flows[0:6])
    small = SmallFlow(place, *flows[6:12])
    fetched[0].wait()
    flatten_planes(crop_ref, wide, cf, lp, fs)
    fetched[1].wait()
    cots[1] = cot_ref[...].astype(F32).T.astype(BF16)
    ready()
    halo.start()
    fetched[2].wait()
    f1s[108:128, :] = jnp.zeros((20, 32), F32)
    for t in range(27):
        f1s[4 * t : 4 * t + 4, :] = f1_ref[t].astype(F32)
    fetched[3].wait()
    w1 = dot_nn(f1s[...].T.astype(BF16), sel_ref[...]).astype(BF16)
    for d in range(8):
        w1s[32 * d : 32 * d + 32, :] = w1[:, 256 * d : 256 * d + 256]
    fetched[4].wait()
    w2s[...] = f2_ref[...].astype(F32).T.astype(BF16)
    for a in range(3):
        w3s[:, 64 * a : 64 * a + 64] = f2_ref[288 * (2 - a) : 288 * (3 - a), :]
    local.patch(5, 6, 7, 8)
    halo.wait(4)
    local.patch(4)
    local.first(2)
    halo.wait(9)
    local.patch(9)
    local.first(3)
    halo.wait(2)
    local.patch(2, 3)
    local.first(1)
    halo.wait(10)
    local.patch(10, 11)
    local.first(4)
    pair = local.second(1)
    pair = pair + local.second(2)
    local.features(pair, feats)
    local.grad_two(large.acc, 0)
    large.shares(0)
    local.grad_two(large.acc, 1)
    large.shares(1)
    halo.wait(0, 1)
    local.patch(0, 1)
    local.first(0)
    halo.wait("left")
    local.second(0)
    halo.wait(12, 13)
    local.patch(12, 13)
    local.first(5)
    halo.wait("right")
    local.second(3)
    local.back(0)
    local.back(1)
    local.grad_one(sel_ref, small.acc)
    small.shares()
    feat_ref[...] = feats[...].T.astype(BF16)
    large.depth()
    large.gather()
    small.depth()
    small.give_back()
    large.finish()
    two_ref[0:432, :] = large.fin[0:432, 0:64].astype(F32)
    two_ref[432:864, :] = large.fin[0:432, 64:128].astype(F32)
    small.finish()
    one = small.out[...].T
    for t in range(27):
        one_ref[t] = one[4 * t : 4 * t + 4]
    halo.drain()
    large.drain()
    small.drain()


def store_kernel(*refs):
    sems = refs[6]
    copies = [pltpu.make_async_copy(refs[k], refs[3 + k], sems.at[k]) for k in range(3)]
    for copy in copies:
        copy.start()
    for copy in copies:
        copy.wait()


def local(crop, filter_one, filter_two, cotangent):
    sel = jnp.asarray(tap_selection(), BF16)
    large, small = flow_scratch()
    hbm = pl.BlockSpec(memory_space=pltpu.HBM)
    operands = (
        crop.reshape(1024, 64),
        filter_one.reshape(27, 4, 32),
        filter_two.reshape(864, 64),
        sel,
        cotangent.transpose(0, 2, 3, 4, 1).reshape(256, 64),
    )
    shapes = (
        jax.ShapeDtypeStruct((256, 64), BF16),
        jax.ShapeDtypeStruct((27, 4, 32), F32),
        jax.ShapeDtypeStruct((864, 64), F32),
    )
    results = pl.pallas_call(
        whole_kernel,
        out_shape=shapes,
        in_specs=[hbm] * 5,
        scratch_shapes=[
            pltpu.VMEM((1024, 64), BF16),
            pltpu.VMEM((27, 4, 32), BF16),
            pltpu.VMEM((864, 64), BF16),
            pltpu.VMEM((128, 2048), BF16),
            pltpu.VMEM((256, 64), BF16),
            pltpu.VMEM((14, 16, LANES), BF16),
            pltpu.VMEM((3, 64, 256), BF16),
            pltpu.VMEM((896, LANES), BF16),
            pltpu.VMEM((1728, LANES), BF16),
            pltpu.VMEM((512, LANES), BF16),
            pltpu.VMEM((256, LANES), BF16),
            pltpu.VMEM((512, LANES), BF16),
            pltpu.VMEM((1024, 64), F32),
            pltpu.VMEM((128, 512), BF16),
            pltpu.VMEM((64, LANES), BF16),
            pltpu.VMEM((128, 32), F32),
            pltpu.VMEM((256, 256), BF16),
            pltpu.VMEM((64, 864), BF16),
            pltpu.VMEM((288, 192), BF16),
            pltpu.VMEM((64, 256), F32),
            pltpu.SemaphoreType.DMA((5,)),
            pltpu.SemaphoreType.DMA((10,)),
            pltpu.SemaphoreType.DMA((10,)),
            *large,
            *small,
        ],
        compiler_params=pltpu.CompilerParams(
            vmem_limit_bytes=32 * 1024 * 1024, collective_id=0, has_side_effects=True
        ),
    )(*[pltpu.with_memory_space_constraint(value, pltpu.HBM) for value in operands])
    feat, one, two = pl.pallas_call(
        store_kernel,
        out_shape=shapes,
        in_specs=[pl.BlockSpec(memory_space=pl.ANY)] * 3,
        out_specs=[hbm] * 3,
        scratch_shapes=[pltpu.SemaphoreType.DMA((3,))],
        compiler_params=pltpu.CompilerParams(vmem_limit_bytes=1024 * 1024),
    )(*results)
    feat = feat.reshape(1, 1, 16, 16, 64).transpose(0, 4, 1, 2, 3)
    return feat, one.reshape(3, 3, 3, 4, 32), two.reshape(3, 3, 3, 32, 64)


def solution(mesh):
    placed = (P("dp", None, "space", None, None), P(), P(), P("dp", None, "space", None, None))
    return jax.shard_map(
        local, mesh=mesh, in_specs=placed, out_specs=(P("dp", None, "space", None, None), P(), P()), check_vma=False
    )
```

```python
import functools

import jax
import jax.numpy as jnp
import numpy as np
from jax import lax
from jax.experimental import pallas as pl
from jax.experimental.pallas import tpu as pltpu
from jax.sharding import PartitionSpec as P

F32, BF16 = jnp.float32, jnp.bfloat16
LANES = 1024


def leaky(value):
    return jnp.maximum(value, 0.3 * value)


def dot_nn(a, b):
    return lax.dot_general(a, b, (((1,), (0,)), ((), ())), preferred_element_type=F32)


def dot_nt(a, b):
    return lax.dot_general(a, b, (((1,), (1,)), ((), ())), preferred_element_type=F32)


def split2(value):
    high = value.astype(BF16)
    return high, (value - high.astype(F32)).astype(BF16)


def tap_selection():
    table = np.zeros((128, 8, 256), np.float32)
    for d in range(8):
        dp, dq, dr = d // 4, d // 2 % 2, d % 2
        for pi in range(4):
            for sq in range(2):
                for sr in range(2):
                    for qe in range(2):
                        for re in range(2):
                            qi = (1 + qe) if sq == 0 else (0 if qe else 3)
                            ri = (1 + re) if sr == 0 else (0 if re else 3)
                            a, b, c = pi - dp, qi - dq, ri - dr
                            if min(a, b, c) < 0 or max(a, b, c) > 2:
                                continue
                            for i in range(4):
                                k = pi * 64 + (sq * 2 + sr) * 16 + (qe * 2 + re) * 4 + i
                                table[((a * 3 + b) * 3 + c) * 4 + i, d, k] = 1
    return table.reshape(128, 2048)


def lane_masks(rows):
    lane = lax.broadcasted_iota(jnp.int32, (rows, LANES), 1)
    return lane % 32, lane // 32


def ones(mask):
    return jnp.where(mask, 1.0, 0.0).astype(BF16)


def rolled(value, amount):
    return pltpu.roll(value, amount % LANES, 1)


NX, NY, NZH, NZL = 4, 4, 2, 4
ROWS = 16
HALF = NX * NY * ROWS
MESH = pl.DeviceIdType.MESH


class Place:
    def __init__(self):
        dp, self.s = lax.axis_index("dp"), lax.axis_index("space")
        self.zh, self.x = dp // NX, dp % NX
        self.core = self.s % 2
        self.y = self.s // 2 % NY
        self.zl = self.s // 2 // NY
        self.z = self.zh * NZL + self.zl

    def at(self, x, y, z, core):
        return {"dp": z // NZL * NX + x, "space": (z % NZL * NY + y) * 2 + core}

    def plane_peers(self):
        peers = []
        for dx, dy, flip in plane_offsets():
            x, y = (self.x + dx) % NX, (self.y + dy) % NY
            core = 1 - self.core if flip else self.core
            peers.append((self.at(x, y, self.z, core), core, core * HALF + (x * NY + y) * ROWS))
        return peers

    def depth_peer(self, dz):
        return self.at(self.x, self.y, (self.z + dz) % (NZH * NZL), self.core)

    def partner(self):
        return self.at(self.x, self.y, self.z, 1 - self.core)


def plane_offsets():
    far = lambda d: min(d[0], NX - d[0]) + min(d[1], NY - d[1])
    every = [(dx, dy, flip) for dx in range(NX) for dy in range(NY) for flip in (1, 0)]
    return sorted(every, key=lambda d: -far(d))[:-1]


def depth_offsets():
    count = NZH * NZL
    return sorted(range(1, count), key=lambda d: -min(d, count - d))


def chip_offsets():
    far = lambda d: min(d[0], NX - d[0]) + min(d[1], NY - d[1])
    return sorted([(dx, dy) for dx in range(NX) for dy in range(NY)], key=lambda d: -far(d))


def remote(src, dst, send, recv, peer):
    copy = pltpu.make_async_remote_copy(
        src_ref=src, dst_ref=dst, send_sem=send, recv_sem=recv, device_id=peer, device_id_type=MESH
    )
    return copy


def rows16(start):
    return pl.ds(pl.multiple_of(start, ROWS), ROWS)


def greet(place):
    barrier = pltpu.get_barrier_semaphore()
    count = lax.axis_size("space")
    peers = [peer for peer, _, _ in place.plane_peers()]
    peers += [place.depth_peer(d) for d in depth_offsets()]
    peers += [{"space": (place.s + hop + count) % count} for hop in (1, -1, 2, -2)]
    for peer in peers:
        pl.semaphore_signal(barrier, inc=1, device_id=peer, device_id_type=MESH)
    return lambda: pl.semaphore_wait(barrier, len(peers))


HALO_MOVES = ((1, 3, 1, 4), (-1, 0, 1, 9), (1, 1, 2, 2), (-1, 1, 2, 10), (1, 0, 1, 1), (-1, 3, 1, 12), (2, 3, 1, 0), (-2, 0, 1, 13))


class Halo:
    def __init__(self, place, wide, cots, send, recv):
        self.s, self.count = place.s, lax.axis_size("space")
        self.items = {}
        for k, (hop, own, planes, to) in enumerate(HALO_MOVES):
            self.add(to, hop, wide.at[5 + own : 5 + own + planes], wide.at[to : to + planes], send.at[k], recv.at[k])
            if k == 3:
                self.add("left", 1, cots.at[1], cots.at[0], send.at[8], recv.at[8])
                self.add("right", -1, cots.at[1], cots.at[2], send.at[9], recv.at[9])

    def add(self, name, hop, src, dst, send, recv):
        peer = {"space": (self.s + hop + self.count) % self.count}
        self.items[name] = (hop, dst, remote(src, dst, send, recv, peer))

    def exists(self, hop):
        there = self.s + hop
        return (there >= 0) & (there < self.count)

    def start(self):
        for hop, dst, copy in self.items.values():
            pl.when(self.exists(hop))(copy.start)

    def clear(self):
        for hop, dst, copy in self.items.values():

            @pl.when(jnp.logical_not(self.exists(-hop)))
            def _(dst=dst):
                dst[...] = jnp.zeros(dst.shape, BF16)

    def wait(self, *names):
        for name in names:
            hop, dst, copy = self.items[name]
            pl.when(self.exists(-hop))(copy.wait_recv)

    def drain(self):
        for hop, dst, copy in self.items.values():
            pl.when(self.exists(hop))(copy.wait_send)


class Flow:
    def __init__(self, place, sems):
        self.place, self.sems, self.sent = place, sems, []

    def send(self, phase, items):
        for src, dst, peer in items:
            remote(src, dst, self.sems.at[0, phase], self.sems.at[1, phase], peer).start()

    def arrive(self, phase, whole):
        self.sent.append((phase, whole))
        remote(whole, whole, self.sems.at[0, phase], self.sems.at[1, phase], self.place.partner()).wait_recv()

    def drain(self):
        for phase, whole in self.sent:
            remote(whole, whole, self.sems.at[0, phase], self.sems.at[1, phase], self.place.partner()).wait_send()


class LargeFlow(Flow):
    def __init__(self, place, acc, accb, r1, r2, fin, sems):
        super().__init__(place, sems)
        self.acc, self.accb, self.r1, self.r2, self.fin = acc, accb, r1, r2, fin
        self.peers = place.plane_peers()
        self.own = place.core * HALF + (place.x * NY + place.y) * ROWS

    def shares(self, half):
        at = slice(half * HALF, half * HALF + HALF)
        self.accb[at, :] = self.acc[at, :].astype(BF16)
        place = self.place
        for k, (dx, dy) in enumerate(chip_offsets()):
            x, y = (place.x + dx) % NX, (place.y + dy) % NY
            src = self.accb.at[rows16(half * HALF + (x * NY + y) * ROWS)]
            go = remote(src, self.r1.at[2 * k + place.core], self.sems.at[0, 0], self.sems.at[1, 0], place.at(x, y, place.z, half))
            if (dx, dy) == (0, 0):
                pl.when(place.core != half)(go.start)
            else:
                go.start()

    def depth(self):
        self.arrive(0, self.r1.at[1:])
        count = NX * NY - 1
        total = self.acc[rows16(self.own), :] + self.r1[2 * count + 1 - self.place.core].astype(F32)
        for k in range(2 * count):
            total = total + self.r1[k].astype(F32)
        self.r2[self.place.z] = total
        here = self.r2.at[self.place.z]
        self.send(1, [(here, here, self.place.depth_peer(d)) for d in depth_offsets()])

    def gather(self):
        self.arrive(1, self.r2.at[1:])
        total = self.r2[0]
        for z in range(1, NZH * NZL):
            total = total + self.r2[z]
        self.fin[rows16(self.own), :] = total.astype(BF16)
        here = self.fin.at[rows16(self.own)]
        self.send(2, [(here, here, peer) for peer, _, _ in self.peers])

    def finish(self):
        self.arrive(2, self.fin.at[ROWS:])


class SmallFlow(Flow):
    def __init__(self, place, acc, accb, q1, q2, out, sems):
        super().__init__(place, sems)
        self.acc, self.accb, self.q1, self.q2, self.out = acc, accb, q1, q2, out
        self.mine = place.core * ROWS
        self.own = place.core * NX * NY + place.x * NY + place.y

    def shares(self):
        for half in range(2):
            self.accb[half] = self.acc[half * ROWS : half * ROWS + ROWS, :].astype(BF16)
        self.q1[self.own] = self.accb[self.place.core]
        there = self.q1.at[self.own]
        self.send(0, [(self.accb.at[core], there, peer) for peer, core, _ in self.place.plane_peers()])

    def depth(self):
        self.arrive(0, self.q1.at[1:])
        total = self.q1[0].astype(F32)
        for j in range(1, 2 * NX * NY):
            total = total + self.q1[j].astype(F32)
        self.q2[self.place.z] = total
        here = self.q2.at[self.place.z]
        self.send(1, [(here, here, self.place.depth_peer(d)) for d in depth_offsets()])

    def give_back(self):
        self.arrive(1, self.q2.at[1:])
        total = self.q2[0]
        for z in range(1, NZH * NZL):
            total = total + self.q2[z]
        self.out[rows16(self.mine), :] = total
        here = self.out.at[rows16(self.mine)]
        self.send(2, [(here, here, self.place.partner())])

    def finish(self):
        self.arrive(2, self.out.at[0:ROWS])


def flow_scratch():
    n, depth = 2 * NX * NY, NZH * NZL
    large = [
        pltpu.VMEM((2 * HALF, 128), F32),
        pltpu.VMEM((2 * HALF, 128), BF16),
        pltpu.VMEM((n, ROWS, 128), BF16),
        pltpu.VMEM((depth, ROWS, 128), F32),
        pltpu.VMEM((2 * HALF, 128), BF16),
        pltpu.SemaphoreType.DMA((2, 3)),
    ]
    small = [
        pltpu.VMEM((2 * ROWS, 128), F32),
        pltpu.VMEM((2, ROWS, 128), BF16),
        pltpu.VMEM((n, ROWS, 128), BF16),
        pltpu.VMEM((depth, ROWS, 128), F32),
        pltpu.VMEM((2 * ROWS, 128), F32),
        pltpu.SemaphoreType.DMA((2, 3)),
    ]
    return large, small


def iota2(shape):
    return lax.broadcasted_iota(jnp.int32, shape, 0), lax.broadcasted_iota(jnp.int32, shape, 1)


def flatten_planes(crop_ref, wide, cf, lp, fs):
    cf[...] = crop_ref[...].astype(F32)
    for h in range(32):
        pair = [cf[pl.ds(2 * h + e, 16, stride=64), :] for e in range(2)]
        lp[h // 4 * 16 : h // 4 * 16 + 16, h % 4 * 128 : h % 4 * 128 + 128] = jnp.concatenate(pair, axis=1).astype(BF16)
    k, n = iota2((512, 512))
    to = (k // 64 % 2 * 2 + k % 2) * 128 + k // 128 * 32 + k % 64 // 2
    moved = dot_nn(lp[...], ones(to == n))
    for block in range(8):
        for c in range(4):
            fs[16 * c : 16 * c + 16, 128 * block : 128 * block + 128] = moved[
                16 * block : 16 * block + 16, 128 * c : 128 * c + 128
            ].astype(BF16)
    m, n = iota2((64, 64))
    rows = dot_nn(ones(m // 4 % 4 * 16 + m % 4 * 4 + m // 16 == n), fs[...])
    for p in range(4):
        wide[5 + p] = rows[16 * p : 16 * p + 16].astype(BF16)


class Local:
    def __init__(self, s, wide, cots, px, maps, z1s, g2s, g1s, w1s, w2s, w3s, widened):
        self.widened = widened
        self.wide, self.cots, self.px, self.maps = wide, cots, px, maps
        self.z1s, self.g2s, self.g1s, self.w1s, self.w2s, self.w3s = z1s, g2s, g1s, w1s, w2s, w3s
        r, q = lane_masks(16)
        row = lax.broadcasted_iota(jnp.int32, (16, LANES), 0)
        q_odd, r_odd = row // 8 == 1, row // 4 % 2 == 1
        self.r_up, self.r_down = ones(r_odd & (r != 0)), ones(~r_odd & (r != 31))
        self.q_up, self.q_down = ones(q_odd & (q != 0)), ones(~q_odd & (q != 31))
        self.left_ok = jnp.where(s > 0, 0.125, 0.0)
        self.right_ok = jnp.where(s < lax.axis_size("space") - 1, 0.125, 0.0)
        r, q = lane_masks(32)
        self.keep, self.keep_ones = {}, {}
        for db in (-1, 0, 1):
            for dc in (-1, 0, 1):
                ok = jnp.ones((32, LANES), jnp.bool_)
                if db:
                    ok = ok & ((q != 0) if db < 0 else (q != 31))
                if dc:
                    ok = ok & ((r != 0) if dc < 0 else (r != 31))
                self.keep[db, dc] = ok
                self.keep_ones[db, dc] = ones(ok)
        k, n = iota2((128, 512))
        self.spread = ones((n // 64 == k // 16) & (n % 32 // 2 == k % 16))
        k, n = iota2((256, 64))
        self.collect = ones((k // 64 == n // 16) & (k % 32 // 2 == n % 16))

    def patch(self, *planes):
        for plane in planes:
            x = self.wide[plane]
            xr = rolled(x, 1) * self.r_up + rolled(x, -1) * self.r_down
            xq = rolled(x, 32) * self.q_up + rolled(x, -32) * self.q_down
            xqr = rolled(xr, 32) * self.q_up + rolled(xr, -32) * self.q_down
            for k, piece in enumerate((x, xr, xq, xqr)):
                self.px[plane * 64 + k * 16 : plane * 64 + k * 16 + 16, :] = piece

    def first(self, plane):
        z = dot_nn(self.w1s[...], self.px[plane * 128 : plane * 128 + 256, :])
        if plane in (2, 3):
            self.z1s[(plane - 2) * 256 : (plane - 1) * 256, :] = z.astype(BF16)
        z = leaky(z)
        total = z[0:32]
        for d in range(1, 8):
            total = total + z[d * 32 : d * 32 + 32]
        a1 = (total * (self.left_ok if plane < 2 else self.right_ok if plane > 3 else 0.125)).astype(BF16)
        for b in range(3):
            for c in range(3):
                v = a1
                if (b, c) != (1, 1):
                    v = rolled(v, -(32 * (b - 1) + (c - 1))) * self.keep_ones[b - 1, c - 1]
                at = plane * 288 + (b * 3 + c) * 32
                self.maps[at : at + 32, :] = v

    def second(self, plane):
        z = dot_nn(self.w2s[...], self.maps[plane * 288 : plane * 288 + 864, :])
        wide = self.widened[...]
        self.g2s[plane * 64 : plane * 64 + 64, :] = jnp.where(z > 0, wide, 0.3 * wide).astype(BF16)
        return leaky(z)

    def widen(self, which):
        cot = self.cots[which]
        self.widened[:, 0:512] = dot_nn(cot[:, 0:128], self.spread) * 0.125
        self.widened[:, 512:1024] = dot_nn(cot[:, 128:256], self.spread) * 0.125

    def features(self, pair, feats):
        high, low = split2(pair)
        for j in range(4):
            lanes = slice(256 * j, 256 * j + 256)
            feats[:, 64 * j : 64 * j + 64] = (
                dot_nn(high[:, lanes], self.collect) + dot_nn(low[:, lanes], self.collect)
            ) * 0.125

    def grad_two(self, acc):
        both = self.g2s[64:192, :]
        low = dot_nt(self.maps[288:576, :], both[0:64])
        mid = dot_nt(self.maps[576:1152, :], both)
        high = dot_nt(self.maps[1152:1440, :], both[64:128])
        acc[0:288, 0:64] = low + mid[0:288, 64:128]
        acc[288:432, 0:64] = mid[0:144, 0:64] + mid[288:432, 64:128]
        acc[0:144, 64:128] = mid[144:288, 0:64] + mid[432:576, 64:128]
        acc[144:432, 64:128] = mid[288:576, 0:64] + high

    def back(self, plane):
        u = dot_nn(self.w3s[...], self.g2s[plane * 64 : plane * 64 + 192, :])
        back = None
        for b in range(3):
            for c in range(3):
                v = u[(b * 3 + c) * 32 : (b * 3 + c) * 32 + 32]
                if (b, c) != (1, 1):
                    v = rolled(v, -(32 * (1 - b) + (1 - c)))
                    v = jnp.where(self.keep[1 - b, 1 - c], v, 0.0)
                back = v if back is None else back + v
        back = back * 0.125
        low = 0.3 * back
        for d in range(8):
            at = plane * 256 + d * 32
            self.g1s[at : at + 32, :] = jnp.where(self.z1s[at : at + 32, :].astype(F32) > 0, back, low).astype(BF16)

    def grad_one(self, sel_ref, acc):
        gram = dot_nt(self.g1s[0:256, :], self.px[256:512, :]) + dot_nt(self.g1s[256:512, :], self.px[384:640, :])
        total = None
        for d in range(8):
            high, low = split2(gram[d * 32 : d * 32 + 32])
            sel = sel_ref[:, d * 256 : d * 256 + 256]
            term = dot_nt(high, sel) + dot_nt(low, sel)
            total = term if total is None else total + term
        acc[...] = total


def whole_kernel(crop_hbm, f1_hbm, f2_hbm, sel_hbm, cot_hbm, feat_ref, one_ref, two_ref,
                 crop_ref, f1_ref, f2_ref, sel_ref, cot_ref, wide, cots, px, maps, z1s, g2s, g1s,
                 cf, lp, fs, f1s, w1s, w2s, w3s, feats, widened, fetch, halo_send, halo_recv, *flows):
    place = Place()
    ready = greet(place)
    pairs = ((crop_hbm, crop_ref), (cot_hbm, cot_ref), (f1_hbm, f1_ref), (sel_hbm, sel_ref), (f2_hbm, f2_ref))
    fetched = [pltpu.make_async_copy(src, dst, fetch.at[k]) for k, (src, dst) in enumerate(pairs)]
    for copy in fetched:
        copy.start()
    halo = Halo(place, wide, cots, halo_send, halo_recv)
    halo.clear()
    local = Local(place.s, wide, cots, px, maps, z1s, g2s, g1s, w1s, w2s, w3s, widened)
    large = LargeFlow(place, *flows[0:6])
    small = SmallFlow(place, *flows[6:12])
    fetched[0].wait()
    flatten_planes(crop_ref, wide, cf, lp, fs)
    fetched[1].wait()
    cots[1] = cot_ref[...].astype(F32).T.astype(BF16)
    ready()
    halo.start()
    fetched[2].wait()
    f1s[108:128, :] = jnp.zeros((20, 32), F32)
    for t in range(27):
        f1s[4 * t : 4 * t + 4, :] = f1_ref[t].astype(F32)
    fetched[3].wait()
    w1 = dot_nn(f1s[...].T.astype(BF16), sel_ref[...]).astype(BF16)
    for d in range(8):
        w1s[32 * d : 32 * d + 32, :] = w1[:, 256 * d : 256 * d + 256]
    fetched[4].wait()
    w2s[...] = f2_ref[...].astype(F32).T.astype(BF16)
    for a in range(3):
        w3s[:, 64 * a : 64 * a + 64] = f2_ref[288 * (2 - a) : 288 * (3 - a), :]
    large.acc[432:512, :] = jnp.zeros((80, 128), F32)
    local.patch(5, 6, 7, 8)
    local.widen(1)
    halo.wait(4, 9)
    local.patch(4, 9)
    local.first(2)
    local.first(3)
    halo.wait(2, 10)
    local.patch(2, 3, 10, 11)
    local.first(1)
    local.first(4)
    pair = local.second(1) + local.second(2)
    local.grad_two(large.acc)
    large.shares(0)
    large.shares(1)
    local.features(pair, feats)
    halo.wait(0, 1, "left", 12, 13, "right")
    local.patch(0, 1, 12, 13)
    local.first(0)
    local.first(5)
    local.widen(0)
    local.second(0)
    local.widen(2)
    local.second(3)
    local.back(0)
    local.back(1)
    local.grad_one(sel_ref, small.acc)
    small.shares()
    feat_ref[...] = feats[...].T.astype(BF16)
    large.depth()
    large.gather()
    small.depth()
    small.give_back()
    large.finish()
    two_ref[0:432, :] = large.fin[0:432, 0:64].astype(F32)
    two_ref[432:864, :] = large.fin[0:432, 64:128].astype(F32)
    small.finish()
    one = small.out[...].T
    for t in range(27):
        one_ref[t] = one[4 * t : 4 * t + 4]
    halo.drain()
    large.drain()
    small.drain()


def store_kernel(*refs):
    sems = refs[6]
    copies = [pltpu.make_async_copy(refs[k], refs[3 + k], sems.at[k]) for k in range(3)]
    for copy in copies:
        copy.start()
    for copy in copies:
        copy.wait()


def local(crop, filter_one, filter_two, cotangent):
    sel = jnp.asarray(tap_selection(), BF16)
    large, small = flow_scratch()
    hbm = pl.BlockSpec(memory_space=pltpu.HBM)
    operands = (
        crop.reshape(1024, 64),
        filter_one.reshape(27, 4, 32),
        filter_two.reshape(864, 64),
        sel,
        cotangent.transpose(0, 2, 3, 4, 1).reshape(256, 64),
    )
    shapes = (
        jax.ShapeDtypeStruct((256, 64), BF16),
        jax.ShapeDtypeStruct((27, 4, 32), F32),
        jax.ShapeDtypeStruct((864, 64), F32),
    )
    results = pl.pallas_call(
        whole_kernel,
        out_shape=shapes,
        in_specs=[hbm] * 5,
        scratch_shapes=[
            pltpu.VMEM((1024, 64), BF16),
            pltpu.VMEM((27, 4, 32), BF16),
            pltpu.VMEM((864, 64), BF16),
            pltpu.VMEM((128, 2048), BF16),
            pltpu.VMEM((256, 64), BF16),
            pltpu.VMEM((14, 16, LANES), BF16),
            pltpu.VMEM((3, 64, 256), BF16),
            pltpu.VMEM((896, LANES), BF16),
            pltpu.VMEM((1728, LANES), BF16),
            pltpu.VMEM((512, LANES), BF16),
            pltpu.VMEM((256, LANES), BF16),
            pltpu.VMEM((512, LANES), BF16),
            pltpu.VMEM((1024, 64), F32),
            pltpu.VMEM((128, 512), BF16),
            pltpu.VMEM((64, LANES), BF16),
            pltpu.VMEM((128, 32), F32),
            pltpu.VMEM((256, 256), BF16),
            pltpu.VMEM((64, 864), BF16),
            pltpu.VMEM((288, 192), BF16),
            pltpu.VMEM((64, 256), F32),
            pltpu.VMEM((64, LANES), F32),
            pltpu.SemaphoreType.DMA((5,)),
            pltpu.SemaphoreType.DMA((10,)),
            pltpu.SemaphoreType.DMA((10,)),
            *large,
            *small,
        ],
        compiler_params=pltpu.CompilerParams(
            vmem_limit_bytes=32 * 1024 * 1024, collective_id=0, has_side_effects=True
        ),
    )(*[pltpu.with_memory_space_constraint(value, pltpu.HBM) for value in operands])
    feat, one, two = pl.pallas_call(
        store_kernel,
        out_shape=shapes,
        in_specs=[pl.BlockSpec(memory_space=pl.ANY)] * 3,
        out_specs=[hbm] * 3,
        scratch_shapes=[pltpu.SemaphoreType.DMA((3,))],
        compiler_params=pltpu.CompilerParams(vmem_limit_bytes=1024 * 1024),
    )(*results)
    feat = feat.reshape(1, 1, 16, 16, 64).transpose(0, 4, 1, 2, 3)
    return feat, one.reshape(3, 3, 3, 4, 32), two.reshape(3, 3, 3, 32, 64)


def solution(mesh):
    placed = (P("dp", None, "space", None, None), P(), P(), P("dp", None, "space", None, None))
    return jax.shard_map(
        local, mesh=mesh, in_specs=placed, out_specs=(P("dp", None, "space", None, None), P(), P()), check_vma=False
    )
```

```python
import functools

import jax
import jax.numpy as jnp
import numpy as np
from jax import lax
from jax.experimental import pallas as pl
from jax.experimental.pallas import tpu as pltpu
from jax.sharding import PartitionSpec as P

F32, BF16 = jnp.float32, jnp.bfloat16
LANES = 1024


def leaky(value):
    return jnp.maximum(value, 0.3 * value)


def dot_nn(a, b):
    return lax.dot_general(a, b, (((1,), (0,)), ((), ())), preferred_element_type=F32)


def dot_nt(a, b):
    return lax.dot_general(a, b, (((1,), (1,)), ((), ())), preferred_element_type=F32)


def split2(value):
    high = value.astype(BF16)
    return high, (value - high.astype(F32)).astype(BF16)


def tap_selection():
    table = np.zeros((128, 8, 256), np.float32)
    for d in range(8):
        dp, dq, dr = d // 4, d // 2 % 2, d % 2
        for pi in range(4):
            for sq in range(2):
                for sr in range(2):
                    for qe in range(2):
                        for re in range(2):
                            qi = (1 + qe) if sq == 0 else (0 if qe else 3)
                            ri = (1 + re) if sr == 0 else (0 if re else 3)
                            a, b, c = pi - dp, qi - dq, ri - dr
                            if min(a, b, c) < 0 or max(a, b, c) > 2:
                                continue
                            for i in range(4):
                                k = pi * 64 + (sq * 2 + sr) * 16 + (qe * 2 + re) * 4 + i
                                table[((a * 3 + b) * 3 + c) * 4 + i, d, k] = 1
    return table.reshape(128, 2048)


def lane_masks(rows):
    lane = lax.broadcasted_iota(jnp.int32, (rows, LANES), 1)
    return lane % 32, lane // 32


def ones(mask):
    return jnp.where(mask, 1.0, 0.0).astype(BF16)


def rolled(value, amount):
    return pltpu.roll(value, amount % LANES, 1)


NX, NY, NZH, NZL = 4, 4, 2, 4
ROWS = 16
HALF = NX * NY * ROWS
MESH = pl.DeviceIdType.MESH


class Place:
    def __init__(self):
        dp, self.s = lax.axis_index("dp"), lax.axis_index("space")
        self.zh, self.x = dp // NX, dp % NX
        self.core = self.s % 2
        self.y = self.s // 2 % NY
        self.zl = self.s // 2 // NY
        self.z = self.zh * NZL + self.zl

    def at(self, x, y, z, core):
        return {"dp": z // NZL * NX + x, "space": (z % NZL * NY + y) * 2 + core}

    def plane_peers(self):
        peers = []
        for dx, dy, flip in plane_offsets():
            x, y = (self.x + dx) % NX, (self.y + dy) % NY
            core = 1 - self.core if flip else self.core
            peers.append((self.at(x, y, self.z, core), core, core * HALF + (x * NY + y) * ROWS))
        return peers

    def depth_peer(self, dz):
        return self.at(self.x, self.y, (self.z + dz) % (NZH * NZL), self.core)

    def partner(self):
        return self.at(self.x, self.y, self.z, 1 - self.core)


def plane_offsets():
    far = lambda d: min(d[0], NX - d[0]) + min(d[1], NY - d[1])
    every = [(dx, dy, flip) for dx in range(NX) for dy in range(NY) for flip in (1, 0)]
    return sorted(every, key=lambda d: -far(d))[:-1]


def depth_offsets():
    count = NZH * NZL
    return sorted(range(1, count), key=lambda d: -min(d, count - d))


def chip_offsets():
    far = lambda d: min(d[0], NX - d[0]) + min(d[1], NY - d[1])
    return sorted([(dx, dy) for dx in range(NX) for dy in range(NY)], key=lambda d: -far(d))


def remote(src, dst, send, recv, peer):
    copy = pltpu.make_async_remote_copy(
        src_ref=src, dst_ref=dst, send_sem=send, recv_sem=recv, device_id=peer, device_id_type=MESH
    )
    return copy


def rows16(start):
    return pl.ds(pl.multiple_of(start, ROWS), ROWS)


def greet(place):
    barrier = pltpu.get_barrier_semaphore()
    count = lax.axis_size("space")
    peers = [peer for peer, _, _ in place.plane_peers()]
    peers += [place.depth_peer(d) for d in depth_offsets()]
    peers += [{"space": (place.s + hop + count) % count} for hop in (1, -1, 2, -2)]
    for peer in peers:
        pl.semaphore_signal(barrier, inc=1, device_id=peer, device_id_type=MESH)
    return lambda: pl.semaphore_wait(barrier, len(peers))


HALO_MOVES = ((1, 3, 1, 4), (-1, 0, 1, 9), (1, 1, 2, 2), (-1, 1, 2, 10), (1, 0, 1, 1), (-1, 3, 1, 12), (2, 3, 1, 0), (-2, 0, 1, 13))


class Halo:
    def __init__(self, place, wide, cots, send, recv):
        self.s, self.count = place.s, lax.axis_size("space")
        self.items = {}
        for k, (hop, own, planes, to) in enumerate(HALO_MOVES):
            self.add(to, hop, wide.at[5 + own : 5 + own + planes], wide.at[to : to + planes], send.at[k], recv.at[k])
            if k == 3:
                self.add("left", 1, cots.at[1], cots.at[0], send.at[8], recv.at[8])
                self.add("right", -1, cots.at[1], cots.at[2], send.at[9], recv.at[9])

    def add(self, name, hop, src, dst, send, recv):
        peer = {"space": (self.s + hop + self.count) % self.count}
        self.items[name] = (hop, dst, remote(src, dst, send, recv, peer))

    def exists(self, hop):
        there = self.s + hop
        return (there >= 0) & (there < self.count)

    def start(self):
        for hop, dst, copy in self.items.values():
            pl.when(self.exists(hop))(copy.start)

    def clear(self):
        for hop, dst, copy in self.items.values():

            @pl.when(jnp.logical_not(self.exists(-hop)))
            def _(dst=dst):
                dst[...] = jnp.zeros(dst.shape, BF16)

    def wait(self, *names):
        for name in names:
            hop, dst, copy = self.items[name]
            pl.when(self.exists(-hop))(copy.wait_recv)

    def drain(self):
        for hop, dst, copy in self.items.values():
            pl.when(self.exists(hop))(copy.wait_send)


class Flow:
    def __init__(self, place, sems):
        self.place, self.sems, self.sent = place, sems, []

    def send(self, phase, items):
        for src, dst, peer in items:
            remote(src, dst, self.sems.at[0, phase], self.sems.at[1, phase], peer).start()

    def arrive(self, phase, whole):
        self.sent.append((phase, whole))
        remote(whole, whole, self.sems.at[0, phase], self.sems.at[1, phase], self.place.partner()).wait_recv()

    def drain(self):
        for phase, whole in self.sent:
            remote(whole, whole, self.sems.at[0, phase], self.sems.at[1, phase], self.place.partner()).wait_send()


class LargeFlow(Flow):
    def __init__(self, place, acc, accb, r1, r2, fin, sems):
        super().__init__(place, sems)
        self.acc, self.accb, self.r1, self.r2, self.fin = acc, accb, r1, r2, fin
        self.peers = place.plane_peers()
        self.own = place.core * HALF + (place.x * NY + place.y) * ROWS

    def shares(self, half):
        at = slice(half * HALF, half * HALF + HALF)
        self.accb[at, :] = self.acc[at, :].astype(BF16)
        place = self.place
        for k, (dx, dy) in enumerate(chip_offsets()):
            x, y = (place.x + dx) % NX, (place.y + dy) % NY
            src = self.accb.at[rows16(half * HALF + (x * NY + y) * ROWS)]
            go = remote(src, self.r1.at[2 * k + place.core], self.sems.at[0, 0], self.sems.at[1, 0], place.at(x, y, place.z, half))
            if (dx, dy) == (0, 0):
                pl.when(place.core != half)(go.start)
            else:
                go.start()

    def depth(self):
        self.arrive(0, self.r1.at[1:])
        count = NX * NY - 1
        total = self.acc[rows16(self.own), :] + self.r1[2 * count + 1 - self.place.core].astype(F32)
        for k in range(2 * count):
            total = total + self.r1[k].astype(F32)
        self.r2[self.place.z] = total
        here = self.r2.at[self.place.z]
        self.send(1, [(here, here, self.place.depth_peer(d)) for d in depth_offsets()])

    def gather(self):
        self.arrive(1, self.r2.at[1:])
        total = self.r2[0]
        for z in range(1, NZH * NZL):
            total = total + self.r2[z]
        self.fin[rows16(self.own), :] = total.astype(BF16)
        here = self.fin.at[rows16(self.own)]
        self.send(2, [(here, here, peer) for peer, _, _ in self.peers])

    def finish(self):
        self.arrive(2, self.fin.at[ROWS:])


class SmallFlow(Flow):
    def __init__(self, place, acc, accb, q1, q2, out, sems):
        super().__init__(place, sems)
        self.acc, self.accb, self.q1, self.q2, self.out = acc, accb, q1, q2, out
        self.mine = place.core * ROWS
        self.own = place.core * NX * NY + place.x * NY + place.y

    def shares(self):
        for half in range(2):
            self.accb[half] = self.acc[half * ROWS : half * ROWS + ROWS, :].astype(BF16)
        self.q1[self.own] = self.accb[self.place.core]
        there = self.q1.at[self.own]
        self.send(0, [(self.accb.at[core], there, peer) for peer, core, _ in self.place.plane_peers()])

    def depth(self):
        self.arrive(0, self.q1.at[1:])
        total = self.q1[0].astype(F32)
        for j in range(1, 2 * NX * NY):
            total = total + self.q1[j].astype(F32)
        self.q2[self.place.z] = total
        here = self.q2.at[self.place.z]
        self.send(1, [(here, here, self.place.depth_peer(d)) for d in depth_offsets()])

    def give_back(self):
        self.arrive(1, self.q2.at[1:])
        total = self.q2[0]
        for z in range(1, NZH * NZL):
            total = total + self.q2[z]
        self.out[rows16(self.mine), :] = total
        here = self.out.at[rows16(self.mine)]
        self.send(2, [(here, here, self.place.partner())])

    def finish(self):
        self.arrive(2, self.out.at[0:ROWS])


def flow_scratch():
    n, depth = 2 * NX * NY, NZH * NZL
    large = [
        pltpu.VMEM((2 * HALF, 128), F32),
        pltpu.VMEM((2 * HALF, 128), BF16),
        pltpu.VMEM((n, ROWS, 128), BF16),
        pltpu.VMEM((depth, ROWS, 128), F32),
        pltpu.VMEM((2 * HALF, 128), BF16),
        pltpu.SemaphoreType.DMA((2, 3)),
    ]
    small = [
        pltpu.VMEM((2 * ROWS, 128), F32),
        pltpu.VMEM((2, ROWS, 128), BF16),
        pltpu.VMEM((n, ROWS, 128), BF16),
        pltpu.VMEM((depth, ROWS, 128), F32),
        pltpu.VMEM((2 * ROWS, 128), F32),
        pltpu.SemaphoreType.DMA((2, 3)),
    ]
    return large, small


def iota2(shape):
    return lax.broadcasted_iota(jnp.int32, shape, 0), lax.broadcasted_iota(jnp.int32, shape, 1)


def flatten_planes(crop_ref, wide, cf, lp, fs):
    cf[...] = crop_ref[...].astype(F32)
    for h in range(32):
        pair = [cf[pl.ds(2 * h + e, 16, stride=64), :] for e in range(2)]
        lp[h // 4 * 16 : h // 4 * 16 + 16, h % 4 * 128 : h % 4 * 128 + 128] = jnp.concatenate(pair, axis=1).astype(BF16)
    k, n = iota2((512, 512))
    to = (k // 64 % 2 * 2 + k % 2) * 128 + k // 128 * 32 + k % 64 // 2
    moved = dot_nn(lp[...], ones(to == n))
    for block in range(8):
        for c in range(4):
            fs[16 * c : 16 * c + 16, 128 * block : 128 * block + 128] = moved[
                16 * block : 16 * block + 16, 128 * c : 128 * c + 128
            ].astype(BF16)
    m, n = iota2((64, 64))
    rows = dot_nn(ones(m // 4 % 4 * 16 + m % 4 * 4 + m // 16 == n), fs[...])
    for p in range(4):
        wide[5 + p] = rows[16 * p : 16 * p + 16].astype(BF16)


class Local:
    def __init__(self, s, wide, cots, px, maps, z1s, g2s, g1s, w1s, w2s, w3s, widened):
        self.widened = widened
        self.wide, self.cots, self.px, self.maps = wide, cots, px, maps
        self.z1s, self.g2s, self.g1s, self.w1s, self.w2s, self.w3s = z1s, g2s, g1s, w1s, w2s, w3s
        r, q = lane_masks(16)
        row = lax.broadcasted_iota(jnp.int32, (16, LANES), 0)
        q_odd, r_odd = row // 8 == 1, row // 4 % 2 == 1
        self.r_up, self.r_down = ones(r_odd & (r != 0)), ones(~r_odd & (r != 31))
        self.q_up, self.q_down = ones(q_odd & (q != 0)), ones(~q_odd & (q != 31))
        self.left_ok = jnp.where(s > 0, 0.125, 0.0)
        self.right_ok = jnp.where(s < lax.axis_size("space") - 1, 0.125, 0.0)
        r, q = lane_masks(32)
        self.keep, self.keep_ones = {}, {}
        for db in (-1, 0, 1):
            for dc in (-1, 0, 1):
                ok = jnp.ones((32, LANES), jnp.bool_)
                if db:
                    ok = ok & ((q != 0) if db < 0 else (q != 31))
                if dc:
                    ok = ok & ((r != 0) if dc < 0 else (r != 31))
                self.keep[db, dc] = ok
                self.keep_ones[db, dc] = ones(ok)
        k, n = iota2((128, 512))
        self.spread = ones((n // 64 == k // 16) & (n % 32 // 2 == k % 16))
        k, n = iota2((256, 64))
        self.collect = ones((k // 64 == n // 16) & (k % 32 // 2 == n % 16))

    def patch(self, *planes):
        for plane in planes:
            x = self.wide[plane]
            xr = rolled(x, 1) * self.r_up + rolled(x, -1) * self.r_down
            xq = rolled(x, 32) * self.q_up + rolled(x, -32) * self.q_down
            xqr = rolled(xr, 32) * self.q_up + rolled(xr, -32) * self.q_down
            for k, piece in enumerate((x, xr, xq, xqr)):
                self.px[plane * 64 + k * 16 : plane * 64 + k * 16 + 16, :] = piece

    def first(self, plane):
        z = dot_nn(self.w1s[...], self.px[plane * 128 : plane * 128 + 256, :])
        if plane in (2, 3):
            self.z1s[(plane - 2) * 256 : (plane - 1) * 256, :] = z.astype(BF16)
        z = leaky(z)
        total = z[0:32]
        for d in range(1, 8):
            total = total + z[d * 32 : d * 32 + 32]
        a1 = (total * (self.left_ok if plane < 2 else self.right_ok if plane > 3 else 0.125)).astype(BF16)
        for b in range(3):
            for c in range(3):
                v = a1
                if (b, c) != (1, 1):
                    v = rolled(v, -(32 * (b - 1) + (c - 1))) * self.keep_ones[b - 1, c - 1]
                at = plane * 288 + (b * 3 + c) * 32
                self.maps[at : at + 32, :] = v

    def second(self, plane):
        z = dot_nn(self.w2s[...], self.maps[plane * 288 : plane * 288 + 864, :])
        wide = self.widened[...]
        self.g2s[plane * 64 : plane * 64 + 64, :] = jnp.where(z > 0, wide, 0.3 * wide).astype(BF16)
        return leaky(z)

    def widen(self, which):
        cot = self.cots[which]
        self.widened[:, 0:512] = dot_nn(cot[:, 0:128], self.spread) * 0.125
        self.widened[:, 512:1024] = dot_nn(cot[:, 128:256], self.spread) * 0.125

    def features(self, pair, feats):
        high, low = split2(pair)
        for j in range(4):
            lanes = slice(256 * j, 256 * j + 256)
            feats[:, 64 * j : 64 * j + 64] = (
                dot_nn(high[:, lanes], self.collect) + dot_nn(low[:, lanes], self.collect)
            ) * 0.125

    def grad_two(self, acc):
        both = self.g2s[64:192, :]
        low = dot_nt(self.maps[288:576, :], both[0:64])
        mid = dot_nt(self.maps[576:1152, :], both)
        high = dot_nt(self.maps[1152:1440, :], both[64:128])
        acc[0:288, 0:64] = low + mid[0:288, 64:128]
        acc[288:432, 0:64] = mid[0:144, 0:64] + mid[288:432, 64:128]
        acc[0:144, 64:128] = mid[144:288, 0:64] + mid[432:576, 64:128]
        acc[144:432, 64:128] = mid[288:576, 0:64] + high

    def back(self, plane):
        u = dot_nn(self.w3s[...], self.g2s[plane * 64 : plane * 64 + 192, :])
        back = None
        for b in range(3):
            for c in range(3):
                v = u[(b * 3 + c) * 32 : (b * 3 + c) * 32 + 32]
                if (b, c) != (1, 1):
                    v = rolled(v, -(32 * (1 - b) + (1 - c)))
                    v = jnp.where(self.keep[1 - b, 1 - c], v, 0.0)
                back = v if back is None else back + v
        back = back * 0.125
        low = 0.3 * back
        for d in range(8):
            at = plane * 256 + d * 32
            self.g1s[at : at + 32, :] = jnp.where(self.z1s[at : at + 32, :].astype(F32) > 0, back, low).astype(BF16)

    def grad_one(self, sel_ref, acc):
        gram = dot_nt(self.g1s[0:256, :], self.px[256:512, :]) + dot_nt(self.g1s[256:512, :], self.px[384:640, :])
        total = None
        for d in range(8):
            high, low = split2(gram[d * 32 : d * 32 + 32])
            sel = sel_ref[:, d * 256 : d * 256 + 256]
            term = dot_nt(high, sel) + dot_nt(low, sel)
            total = term if total is None else total + term
        acc[...] = total


def whole_kernel(crop_hbm, f1_hbm, f2_hbm, sel_hbm, cot_hbm, feat_ref, one_ref, two_ref,
                 crop_ref, f1_ref, f2_ref, sel_ref, cot_ref, wide, cots, px, maps, z1s, g2s, g1s,
                 cf, lp, fs, f1s, w1s, w2s, w3s, feats, widened, fetch, halo_send, halo_recv, *flows):
    place = Place()
    ready = greet(place)
    pairs = ((crop_hbm, crop_ref), (cot_hbm, cot_ref), (f1_hbm, f1_ref), (sel_hbm, sel_ref), (f2_hbm, f2_ref))
    fetched = [pltpu.make_async_copy(src, dst, fetch.at[k]) for k, (src, dst) in enumerate(pairs)]
    for copy in fetched:
        copy.start()
    halo = Halo(place, wide, cots, halo_send, halo_recv)
    halo.clear()
    local = Local(place.s, wide, cots, px, maps, z1s, g2s, g1s, w1s, w2s, w3s, widened)
    large = LargeFlow(place, *flows[0:6])
    small = SmallFlow(place, *flows[6:12])
    fetched[0].wait()
    flatten_planes(crop_ref, wide, cf, lp, fs)
    fetched[1].wait()
    cots[1] = cot_ref[...].astype(F32).T.astype(BF16)
    ready()
    halo.start()
    fetched[2].wait()
    f1s[108:128, :] = jnp.zeros((20, 32), F32)
    for t in range(27):
        f1s[4 * t : 4 * t + 4, :] = f1_ref[t].astype(F32)
    fetched[3].wait()
    w1 = dot_nn(f1s[...].T.astype(BF16), sel_ref[...]).astype(BF16)
    for d in range(8):
        w1s[32 * d : 32 * d + 32, :] = w1[:, 256 * d : 256 * d + 256]
    fetched[4].wait()
    w2s[...] = f2_ref[...].astype(F32).T.astype(BF16)
    for a in range(3):
        w3s[:, 64 * a : 64 * a + 64] = f2_ref[288 * (2 - a) : 288 * (3 - a), :]
    large.acc[432:512, :] = jnp.zeros((80, 128), F32)
    local.patch(5, 6, 7, 8)
    local.widen(1)
    halo.wait(4, 9)
    local.patch(4, 9)
    local.first(2)
    local.first(3)
    halo.wait(2, 10)
    local.patch(2, 3, 10, 11)
    local.first(1)
    local.first(4)
    pair = local.second(1) + local.second(2)
    local.grad_two(large.acc)
    large.shares(0)
    large.shares(1)
    local.features(pair, feats)
    halo.wait(0, 1, "left", 12, 13, "right")
    local.patch(0, 1, 12, 13)
    local.first(0)
    local.first(5)
    local.widen(0)
    local.second(0)
    local.widen(2)
    local.second(3)
    local.back(0)
    local.back(1)
    local.grad_one(sel_ref, small.acc)
    small.shares()
    feat_ref[...] = feats[...].T.astype(BF16)
    large.depth()
    small.depth()
    large.gather()
    small.give_back()
    large.finish()
    two_ref[0:432, :] = large.fin[0:432, 0:64].astype(F32)
    two_ref[432:864, :] = large.fin[0:432, 64:128].astype(F32)
    small.finish()
    one = small.out[...].T
    for t in range(27):
        one_ref[t] = one[4 * t : 4 * t + 4]
    halo.drain()
    large.drain()
    small.drain()


def store_kernel(*refs):
    sems = refs[6]
    copies = [pltpu.make_async_copy(refs[k], refs[3 + k], sems.at[k]) for k in range(3)]
    for copy in copies:
        copy.start()
    for copy in copies:
        copy.wait()


def local(crop, filter_one, filter_two, cotangent):
    sel = jnp.asarray(tap_selection(), BF16)
    large, small = flow_scratch()
    hbm = pl.BlockSpec(memory_space=pltpu.HBM)
    operands = (
        crop.reshape(1024, 64),
        filter_one.reshape(27, 4, 32),
        filter_two.reshape(864, 64),
        sel,
        cotangent.transpose(0, 2, 3, 4, 1).reshape(256, 64),
    )
    shapes = (
        jax.ShapeDtypeStruct((256, 64), BF16),
        jax.ShapeDtypeStruct((27, 4, 32), F32),
        jax.ShapeDtypeStruct((864, 64), F32),
    )
    results = pl.pallas_call(
        whole_kernel,
        out_shape=shapes,
        in_specs=[hbm] * 5,
        scratch_shapes=[
            pltpu.VMEM((1024, 64), BF16),
            pltpu.VMEM((27, 4, 32), BF16),
            pltpu.VMEM((864, 64), BF16),
            pltpu.VMEM((128, 2048), BF16),
            pltpu.VMEM((256, 64), BF16),
            pltpu.VMEM((14, 16, LANES), BF16),
            pltpu.VMEM((3, 64, 256), BF16),
            pltpu.VMEM((896, LANES), BF16),
            pltpu.VMEM((1728, LANES), BF16),
            pltpu.VMEM((512, LANES), BF16),
            pltpu.VMEM((256, LANES), BF16),
            pltpu.VMEM((512, LANES), BF16),
            pltpu.VMEM((1024, 64), F32),
            pltpu.VMEM((128, 512), BF16),
            pltpu.VMEM((64, LANES), BF16),
            pltpu.VMEM((128, 32), F32),
            pltpu.VMEM((256, 256), BF16),
            pltpu.VMEM((64, 864), BF16),
            pltpu.VMEM((288, 192), BF16),
            pltpu.VMEM((64, 256), F32),
            pltpu.VMEM((64, LANES), F32),
            pltpu.SemaphoreType.DMA((5,)),
            pltpu.SemaphoreType.DMA((10,)),
            pltpu.SemaphoreType.DMA((10,)),
            *large,
            *small,
        ],
        compiler_params=pltpu.CompilerParams(
            vmem_limit_bytes=32 * 1024 * 1024, collective_id=0, has_side_effects=True
        ),
    )(*[pltpu.with_memory_space_constraint(value, pltpu.HBM) for value in operands])
    feat, one, two = pl.pallas_call(
        store_kernel,
        out_shape=shapes,
        in_specs=[pl.BlockSpec(memory_space=pl.ANY)] * 3,
        out_specs=[hbm] * 3,
        scratch_shapes=[pltpu.SemaphoreType.DMA((3,))],
        compiler_params=pltpu.CompilerParams(vmem_limit_bytes=1024 * 1024),
    )(*results)
    feat = feat.reshape(1, 1, 16, 16, 64).transpose(0, 4, 1, 2, 3)
    return feat, one.reshape(3, 3, 3, 4, 32), two.reshape(3, 3, 3, 32, 64)


def solution(mesh):
    placed = (P("dp", None, "space", None, None), P(), P(), P("dp", None, "space", None, None))
    return jax.shard_map(
        local, mesh=mesh, in_specs=placed, out_specs=(P("dp", None, "space", None, None), P(), P()), check_vma=False
    )
```

```python
import functools

import jax
import jax.numpy as jnp
import numpy as np
from jax import lax
from jax.experimental import pallas as pl
from jax.experimental.pallas import tpu as pltpu
from jax.sharding import PartitionSpec as P

F32, BF16 = jnp.float32, jnp.bfloat16
LANES = 1024


def leaky(value):
    return jnp.maximum(value, 0.3 * value)


def dot_nn(a, b):
    return lax.dot_general(a, b, (((1,), (0,)), ((), ())), preferred_element_type=F32)


def dot_nt(a, b):
    return lax.dot_general(a, b, (((1,), (1,)), ((), ())), preferred_element_type=F32)


def split2(value):
    high = value.astype(BF16)
    return high, (value - high.astype(F32)).astype(BF16)


def tap_selection():
    table = np.zeros((128, 8, 256), np.float32)
    for d in range(8):
        dp, dq, dr = d // 4, d // 2 % 2, d % 2
        for pi in range(4):
            for sq in range(2):
                for sr in range(2):
                    for qe in range(2):
                        for re in range(2):
                            qi = (1 + qe) if sq == 0 else (0 if qe else 3)
                            ri = (1 + re) if sr == 0 else (0 if re else 3)
                            a, b, c = pi - dp, qi - dq, ri - dr
                            if min(a, b, c) < 0 or max(a, b, c) > 2:
                                continue
                            for i in range(4):
                                k = pi * 64 + (sq * 2 + sr) * 16 + (qe * 2 + re) * 4 + i
                                table[((a * 3 + b) * 3 + c) * 4 + i, d, k] = 1
    return table.reshape(128, 2048)


def lane_masks(rows):
    lane = lax.broadcasted_iota(jnp.int32, (rows, LANES), 1)
    return lane % 32, lane // 32


def ones(mask):
    return jnp.where(mask, 1.0, 0.0).astype(BF16)


def rolled(value, amount):
    return pltpu.roll(value, amount % LANES, 1)


NX, NY, NZH, NZL = 4, 4, 2, 4
ROWS = 16
HALF = NX * NY * ROWS
MESH = pl.DeviceIdType.LOGICAL


class Place:
    def __init__(self):
        self.dp, self.s = lax.axis_index("dp"), lax.axis_index("space")
        self.count = lax.axis_size("space")
        self.zh, self.x = lax.div(self.dp, NX), lax.rem(self.dp, NX)
        self.core = lax.rem(self.s, 2)
        chip = lax.div(self.s, 2)
        self.y, self.zl = lax.rem(chip, NY), lax.div(chip, NY)
        self.z = self.zh * NZL + self.zl
        self.xs = [lax.rem(self.x + d, NX) for d in range(NX)]
        self.ys = [lax.rem(self.y + d, NY) for d in range(NY)]
        self.base = self.zh * (NX * self.count) + self.zl * (2 * NY)
        self.columns = [self.base + x * self.count for x in self.xs]

    def near(self, dx, dy, core):
        return self.columns[dx] + self.ys[dy] * 2 + core

    def along(self, hop):
        return self.dp * self.count + lax.rem(self.s + hop + self.count, self.count)

    def plane_peers(self):
        peers = []
        for dx, dy, flip in plane_offsets():
            core = 1 - self.core if flip else self.core
            peers.append((self.near(dx, dy, core), core, core * HALF + (self.xs[dx] * NY + self.ys[dy]) * ROWS))
        return peers

    def depth_peer(self, dz):
        z = lax.rem(self.z + dz, NZH * NZL)
        here = self.x * self.count + self.y * 2 + self.core
        return here + lax.div(z, NZL) * (NX * self.count) + lax.rem(z, NZL) * (2 * NY)

    def partner(self):
        return self.near(0, 0, 1 - self.core)


def plane_offsets():
    far = lambda d: min(d[0], NX - d[0]) + min(d[1], NY - d[1])
    every = [(dx, dy, flip) for dx in range(NX) for dy in range(NY) for flip in (1, 0)]
    return sorted(every, key=lambda d: -far(d))[:-1]


def depth_offsets():
    count = NZH * NZL
    return sorted(range(1, count), key=lambda d: -min(d, count - d))


def chip_offsets():
    far = lambda d: min(d[0], NX - d[0]) + min(d[1], NY - d[1])
    return sorted([(dx, dy) for dx in range(NX) for dy in range(NY)], key=lambda d: -far(d))


def remote(src, dst, send, recv, peer):
    copy = pltpu.make_async_remote_copy(
        src_ref=src, dst_ref=dst, send_sem=send, recv_sem=recv, device_id=peer, device_id_type=MESH
    )
    return copy


def rows16(start):
    return pl.ds(pl.multiple_of(start, ROWS), ROWS)


def greet(place):
    barrier = pltpu.get_barrier_semaphore()
    peers = [peer for peer, _, _ in place.plane_peers()]
    peers += [place.depth_peer(d) for d in depth_offsets()]
    peers += [place.along(hop) for hop in (1, -1, 2, -2)]
    for peer in peers:
        pl.semaphore_signal(barrier, inc=1, device_id=peer, device_id_type=MESH)
    return lambda: pl.semaphore_wait(barrier, len(peers))


HALO_MOVES = ((1, 3, 1, 4), (-1, 0, 1, 9), (1, 1, 2, 2), (-1, 1, 2, 10), (1, 0, 1, 1), (-1, 3, 1, 12), (2, 3, 1, 0), (-2, 0, 1, 13))


class Halo:
    def __init__(self, place, wide, cots, send, recv):
        self.place, self.s, self.count = place, place.s, place.count
        self.items = {}
        for k, (hop, own, planes, to) in enumerate(HALO_MOVES):
            self.add(to, hop, wide.at[5 + own : 5 + own + planes], wide.at[to : to + planes], send.at[k], recv.at[k])
            if k == 3:
                self.add("left", 1, cots.at[1], cots.at[0], send.at[8], recv.at[8])
                self.add("right", -1, cots.at[1], cots.at[2], send.at[9], recv.at[9])

    def add(self, name, hop, src, dst, send, recv):
        peer = self.place.along(hop)
        self.items[name] = (hop, dst, remote(src, dst, send, recv, peer))

    def exists(self, hop):
        there = self.s + hop
        return (there >= 0) & (there < self.count)

    def start(self):
        for hop, dst, copy in self.items.values():
            pl.when(self.exists(hop))(copy.start)

    def clear(self):
        for hop, dst, copy in self.items.values():

            @pl.when(jnp.logical_not(self.exists(-hop)))
            def _(dst=dst):
                dst[...] = jnp.zeros(dst.shape, BF16)

    def wait(self, *names):
        for name in names:
            hop, dst, copy = self.items[name]
            pl.when(self.exists(-hop))(copy.wait_recv)

    def drain(self):
        for hop, dst, copy in self.items.values():
            pl.when(self.exists(hop))(copy.wait_send)


def tree_sum(terms):
    while len(terms) > 1:
        terms = [a + b for a, b in zip(terms[::2], terms[1::2])] + ([terms[-1]] if len(terms) % 2 else [])
    return terms[0]


class Flow:
    def __init__(self, place, sems):
        self.place, self.sems, self.sent = place, sems, []

    def send(self, phase, items):
        for src, dst, peer in items:
            remote(src, dst, self.sems.at[0, phase], self.sems.at[1, phase], peer).start()

    def arrive(self, phase, whole):
        self.sent.append((phase, whole))
        remote(whole, whole, self.sems.at[0, phase], self.sems.at[1, phase], self.place.partner()).wait_recv()

    def drain(self):
        for phase, whole in self.sent:
            remote(whole, whole, self.sems.at[0, phase], self.sems.at[1, phase], self.place.partner()).wait_send()


class LargeFlow(Flow):
    def __init__(self, place, acc, accb, r1, r2, fin, sems):
        super().__init__(place, sems)
        self.acc, self.accb, self.r1, self.r2, self.fin = acc, accb, r1, r2, fin
        self.peers = place.plane_peers()
        self.own = place.core * HALF + (place.x * NY + place.y) * ROWS

    def shares(self, half):
        at = slice(half * HALF, half * HALF + HALF)
        self.accb[at, :] = self.acc[at, :].astype(BF16)
        place = self.place
        for k, (dx, dy) in enumerate(chip_offsets()):
            src = self.accb.at[rows16(half * HALF + (place.xs[dx] * NY + place.ys[dy]) * ROWS)]
            go = remote(src, self.r1.at[2 * k + place.core], self.sems.at[0, 0], self.sems.at[1, 0], place.near(dx, dy, half))
            if (dx, dy) == (0, 0):
                pl.when(place.core != half)(go.start)
            else:
                go.start()

    def depth(self):
        self.arrive(0, self.r1.at[1:])
        count = NX * NY - 1
        lanes = [self.acc[rows16(self.own), :], self.r1[2 * count + 1 - self.place.core].astype(F32)]
        lanes += [self.r1[k].astype(F32) for k in range(2 * count)]
        total = tree_sum(lanes)
        self.r2[self.place.z] = total
        here = self.r2.at[self.place.z]
        self.send(1, [(here, here, self.place.depth_peer(d)) for d in depth_offsets()])

    def gather(self):
        self.arrive(1, self.r2.at[1:])
        total = tree_sum([self.r2[z] for z in range(NZH * NZL)])
        self.fin[rows16(self.own), :] = total.astype(BF16)
        here = self.fin.at[rows16(self.own)]
        self.send(2, [(here, here, peer) for peer, _, _ in self.peers])

    def finish(self):
        self.arrive(2, self.fin.at[ROWS:])


class SmallFlow(Flow):
    def __init__(self, place, acc, accb, q1, q2, out, sems):
        super().__init__(place, sems)
        self.acc, self.accb, self.q1, self.q2, self.out = acc, accb, q1, q2, out
        self.mine = place.core * ROWS
        self.own = place.core * NX * NY + place.x * NY + place.y

    def shares(self):
        for half in range(2):
            self.accb[half] = self.acc[half * ROWS : half * ROWS + ROWS, :].astype(BF16)
        self.q1[self.own] = self.accb[self.place.core]
        there = self.q1.at[self.own]
        self.send(0, [(self.accb.at[core], there, peer) for peer, core, _ in self.place.plane_peers()])

    def depth(self):
        self.arrive(0, self.q1.at[1:])
        total = tree_sum([self.q1[j].astype(F32) for j in range(2 * NX * NY)])
        self.q2[self.place.z] = total
        here = self.q2.at[self.place.z]
        self.send(1, [(here, here, self.place.depth_peer(d)) for d in depth_offsets()])

    def give_back(self):
        self.arrive(1, self.q2.at[1:])
        total = tree_sum([self.q2[z] for z in range(NZH * NZL)])
        self.out[rows16(self.mine), :] = total
        here = self.out.at[rows16(self.mine)]
        self.send(2, [(here, here, self.place.partner())])

    def finish(self):
        self.arrive(2, self.out.at[0:ROWS])


def flow_scratch():
    n, depth = 2 * NX * NY, NZH * NZL
    large = [
        pltpu.VMEM((2 * HALF, 128), F32),
        pltpu.VMEM((2 * HALF, 128), BF16),
        pltpu.VMEM((n, ROWS, 128), BF16),
        pltpu.VMEM((depth, ROWS, 128), F32),
        pltpu.VMEM((2 * HALF, 128), BF16),
        pltpu.SemaphoreType.DMA((2, 3)),
    ]
    small = [
        pltpu.VMEM((2 * ROWS, 128), F32),
        pltpu.VMEM((2, ROWS, 128), BF16),
        pltpu.VMEM((n, ROWS, 128), BF16),
        pltpu.VMEM((depth, ROWS, 128), F32),
        pltpu.VMEM((2 * ROWS, 128), F32),
        pltpu.SemaphoreType.DMA((2, 3)),
    ]
    return large, small


def iota2(shape):
    return lax.broadcasted_iota(jnp.int32, shape, 0), lax.broadcasted_iota(jnp.int32, shape, 1)


def flatten_planes(crop_ref, wide, cf, lp, fs):
    cf[...] = crop_ref[...].astype(F32)
    for h in range(32):
        pair = [cf[pl.ds(2 * h + e, 16, stride=64), :] for e in range(2)]
        lp[h // 4 * 16 : h // 4 * 16 + 16, h % 4 * 128 : h % 4 * 128 + 128] = jnp.concatenate(pair, axis=1).astype(BF16)
    k, n = iota2((512, 512))
    to = (k // 64 % 2 * 2 + k % 2) * 128 + k // 128 * 32 + k % 64 // 2
    moved = dot_nn(lp[...], ones(to == n))
    for block in range(8):
        for c in range(4):
            fs[16 * c : 16 * c + 16, 128 * block : 128 * block + 128] = moved[
                16 * block : 16 * block + 16, 128 * c : 128 * c + 128
            ].astype(BF16)
    m, n = iota2((64, 64))
    rows = dot_nn(ones(m // 4 % 4 * 16 + m % 4 * 4 + m // 16 == n), fs[...])
    for p in range(4):
        wide[5 + p] = rows[16 * p : 16 * p + 16].astype(BF16)


class Local:
    def __init__(self, s, wide, cots, px, maps, z1s, g2s, g1s, w1s, w2s, w3s, widened):
        self.widened = widened
        self.wide, self.cots, self.px, self.maps = wide, cots, px, maps
        self.z1s, self.g2s, self.g1s, self.w1s, self.w2s, self.w3s = z1s, g2s, g1s, w1s, w2s, w3s
        r, q = lane_masks(16)
        row = lax.broadcasted_iota(jnp.int32, (16, LANES), 0)
        q_odd, r_odd = row // 8 == 1, row // 4 % 2 == 1
        self.r_up, self.r_down = ones(r_odd & (r != 0)), ones(~r_odd & (r != 31))
        self.q_up, self.q_down = ones(q_odd & (q != 0)), ones(~q_odd & (q != 31))
        self.left_ok = jnp.where(s > 0, 0.125, 0.0)
        self.right_ok = jnp.where(s < lax.axis_size("space") - 1, 0.125, 0.0)
        r, q = lane_masks(32)
        self.keep, self.keep_ones = {}, {}
        for db in (-1, 0, 1):
            for dc in (-1, 0, 1):
                ok = jnp.ones((32, LANES), jnp.bool_)
                if db:
                    ok = ok & ((q != 0) if db < 0 else (q != 31))
                if dc:
                    ok = ok & ((r != 0) if dc < 0 else (r != 31))
                self.keep[db, dc] = ok
                self.keep_ones[db, dc] = ones(ok)
        k, n = iota2((128, 512))
        self.spread = ones((n // 64 == k // 16) & (n % 32 // 2 == k % 16))
        k, n = iota2((256, 64))
        self.collect = ones((k // 64 == n // 16) & (k % 32 // 2 == n % 16))

    def patch(self, *planes):
        for plane in planes:
            x = self.wide[plane]
            xr = rolled(x, 1) * self.r_up + rolled(x, -1) * self.r_down
            xq = rolled(x, 32) * self.q_up + rolled(x, -32) * self.q_down
            xqr = rolled(xr, 32) * self.q_up + rolled(xr, -32) * self.q_down
            for k, piece in enumerate((x, xr, xq, xqr)):
                self.px[plane * 64 + k * 16 : plane * 64 + k * 16 + 16, :] = piece

    def first(self, plane):
        z = dot_nn(self.w1s[...], self.px[plane * 128 : plane * 128 + 256, :])
        if plane in (2, 3):
            self.z1s[(plane - 2) * 256 : (plane - 1) * 256, :] = z.astype(BF16)
        z = leaky(z)
        total = z[0:32]
        for d in range(1, 8):
            total = total + z[d * 32 : d * 32 + 32]
        a1 = (total * (self.left_ok if plane < 2 else self.right_ok if plane > 3 else 0.125)).astype(BF16)
        for b in range(3):
            for c in range(3):
                v = a1
                if (b, c) != (1, 1):
                    v = rolled(v, -(32 * (b - 1) + (c - 1))) * self.keep_ones[b - 1, c - 1]
                at = plane * 288 + (b * 3 + c) * 32
                self.maps[at : at + 32, :] = v

    def second(self, plane):
        z = dot_nn(self.w2s[...], self.maps[plane * 288 : plane * 288 + 864, :])
        wide = self.widened[...]
        self.g2s[plane * 64 : plane * 64 + 64, :] = jnp.where(z > 0, wide, 0.3 * wide).astype(BF16)
        return leaky(z)

    def widen(self, which):
        cot = self.cots[which]
        self.widened[:, 0:512] = dot_nn(cot[:, 0:128], self.spread) * 0.125
        self.widened[:, 512:1024] = dot_nn(cot[:, 128:256], self.spread) * 0.125

    def features(self, pair, feats):
        high, low = split2(pair)
        for j in range(4):
            lanes = slice(256 * j, 256 * j + 256)
            feats[:, 64 * j : 64 * j + 64] = (
                dot_nn(high[:, lanes], self.collect) + dot_nn(low[:, lanes], self.collect)
            ) * 0.125

    def grad_two(self, acc):
        both = self.g2s[64:192, :]
        low = dot_nt(self.maps[288:576, :], both[0:64])
        mid = dot_nt(self.maps[576:1152, :], both)
        high = dot_nt(self.maps[1152:1440, :], both[64:128])
        acc[0:288, 0:64] = low + mid[0:288, 64:128]
        acc[288:432, 0:64] = mid[0:144, 0:64] + mid[288:432, 64:128]
        acc[0:144, 64:128] = mid[144:288, 0:64] + mid[432:576, 64:128]
        acc[144:432, 64:128] = mid[288:576, 0:64] + high

    def back(self, plane):
        u = dot_nn(self.w3s[...], self.g2s[plane * 64 : plane * 64 + 192, :])
        back = None
        for b in range(3):
            for c in range(3):
                v = u[(b * 3 + c) * 32 : (b * 3 + c) * 32 + 32]
                if (b, c) != (1, 1):
                    v = rolled(v, -(32 * (1 - b) + (1 - c)))
                    v = jnp.where(self.keep[1 - b, 1 - c], v, 0.0)
                back = v if back is None else back + v
        back = back * 0.125
        low = 0.3 * back
        for d in range(8):
            at = plane * 256 + d * 32
            self.g1s[at : at + 32, :] = jnp.where(self.z1s[at : at + 32, :].astype(F32) > 0, back, low).astype(BF16)

    def grad_one(self, sel_ref, acc):
        gram = dot_nt(self.g1s[0:256, :], self.px[256:512, :]) + dot_nt(self.g1s[256:512, :], self.px[384:640, :])
        total = None
        for d in range(8):
            high, low = split2(gram[d * 32 : d * 32 + 32])
            sel = sel_ref[:, d * 256 : d * 256 + 256]
            term = dot_nt(high, sel) + dot_nt(low, sel)
            total = term if total is None else total + term
        acc[...] = total


def whole_kernel(crop_hbm, f1_hbm, f2_hbm, sel_hbm, cot_hbm, feat_ref, one_ref, two_ref,
                 crop_ref, f1_ref, f2_ref, sel_ref, cot_ref, wide, cots, px, maps, z1s, g2s, g1s,
                 cf, lp, fs, f1s, w1s, w2s, w3s, feats, widened, fetch, halo_send, halo_recv, *flows):
    place = Place()
    ready = greet(place)
    pairs = ((crop_hbm, crop_ref), (cot_hbm, cot_ref), (f1_hbm, f1_ref), (sel_hbm, sel_ref), (f2_hbm, f2_ref))
    fetched = [pltpu.make_async_copy(src, dst, fetch.at[k]) for k, (src, dst) in enumerate(pairs)]
    for copy in fetched:
        copy.start()
    halo = Halo(place, wide, cots, halo_send, halo_recv)
    halo.clear()
    local = Local(place.s, wide, cots, px, maps, z1s, g2s, g1s, w1s, w2s, w3s, widened)
    large = LargeFlow(place, *flows[0:6])
    small = SmallFlow(place, *flows[6:12])
    fetched[0].wait()
    flatten_planes(crop_ref, wide, cf, lp, fs)
    fetched[1].wait()
    cots[1] = cot_ref[...].astype(F32).T.astype(BF16)
    ready()
    halo.start()
    fetched[2].wait()
    f1s[108:128, :] = jnp.zeros((20, 32), F32)
    for t in range(27):
        f1s[4 * t : 4 * t + 4, :] = f1_ref[t].astype(F32)
    fetched[3].wait()
    w1 = dot_nn(f1s[...].T.astype(BF16), sel_ref[...]).astype(BF16)
    for d in range(8):
        w1s[32 * d : 32 * d + 32, :] = w1[:, 256 * d : 256 * d + 256]
    fetched[4].wait()
    w2s[...] = f2_ref[...].astype(F32).T.astype(BF16)
    for a in range(3):
        w3s[:, 64 * a : 64 * a + 64] = f2_ref[288 * (2 - a) : 288 * (3 - a), :]
    large.acc[432:512, :] = jnp.zeros((80, 128), F32)
    local.patch(5, 6, 7, 8)
    local.widen(1)
    halo.wait(4, 9)
    local.patch(4, 9)
    local.first(2)
    local.first(3)
    halo.wait(2, 10)
    local.patch(2, 3, 10, 11)
    local.first(1)
    local.first(4)
    pair = local.second(1) + local.second(2)
    local.grad_two(large.acc)
    large.shares(0)
    large.shares(1)
    local.features(pair, feats)
    halo.wait(0, 1, "left", 12, 13, "right")
    local.patch(0, 1, 12, 13)
    local.first(0)
    local.first(5)
    local.widen(0)
    local.second(0)
    local.widen(2)
    local.second(3)
    local.back(0)
    local.back(1)
    local.grad_one(sel_ref, small.acc)
    small.shares()
    feat_ref[...] = feats[...].T.astype(BF16)
    large.depth()
    small.depth()
    large.gather()
    small.give_back()
    small.finish()
    one = small.out[...].T
    for t in range(27):
        one_ref[t] = one[4 * t : 4 * t + 4]
    halo.drain()
    small.drain()
    large.finish()
    two_ref[0:432, :] = large.fin[0:432, 0:64].astype(F32)
    two_ref[432:864, :] = large.fin[0:432, 64:128].astype(F32)
    large.drain()


def store_kernel(*refs):
    sems = refs[6]
    copies = [pltpu.make_async_copy(refs[k], refs[3 + k], sems.at[k]) for k in range(3)]
    for copy in copies:
        copy.start()
    for copy in copies:
        copy.wait()


def local(crop, filter_one, filter_two, cotangent):
    sel = jnp.asarray(tap_selection(), BF16)
    large, small = flow_scratch()
    hbm = pl.BlockSpec(memory_space=pltpu.HBM)
    operands = (
        crop.reshape(1024, 64),
        filter_one.reshape(27, 4, 32),
        filter_two.reshape(864, 64),
        sel,
        cotangent.transpose(0, 2, 3, 4, 1).reshape(256, 64),
    )
    shapes = (
        jax.ShapeDtypeStruct((256, 64), BF16),
        jax.ShapeDtypeStruct((27, 4, 32), F32),
        jax.ShapeDtypeStruct((864, 64), F32),
    )
    results = pl.pallas_call(
        whole_kernel,
        out_shape=shapes,
        in_specs=[hbm] * 5,
        scratch_shapes=[
            pltpu.VMEM((1024, 64), BF16),
            pltpu.VMEM((27, 4, 32), BF16),
            pltpu.VMEM((864, 64), BF16),
            pltpu.VMEM((128, 2048), BF16),
            pltpu.VMEM((256, 64), BF16),
            pltpu.VMEM((14, 16, LANES), BF16),
            pltpu.VMEM((3, 64, 256), BF16),
            pltpu.VMEM((896, LANES), BF16),
            pltpu.VMEM((1728, LANES), BF16),
            pltpu.VMEM((512, LANES), BF16),
            pltpu.VMEM((256, LANES), BF16),
            pltpu.VMEM((512, LANES), BF16),
            pltpu.VMEM((1024, 64), F32),
            pltpu.VMEM((128, 512), BF16),
            pltpu.VMEM((64, LANES), BF16),
            pltpu.VMEM((128, 32), F32),
            pltpu.VMEM((256, 256), BF16),
            pltpu.VMEM((64, 864), BF16),
            pltpu.VMEM((288, 192), BF16),
            pltpu.VMEM((64, 256), F32),
            pltpu.VMEM((64, LANES), F32),
            pltpu.SemaphoreType.DMA((5,)),
            pltpu.SemaphoreType.DMA((10,)),
            pltpu.SemaphoreType.DMA((10,)),
            *large,
            *small,
        ],
        compiler_params=pltpu.CompilerParams(
            vmem_limit_bytes=32 * 1024 * 1024, collective_id=0, has_side_effects=True
        ),
    )(*[pltpu.with_memory_space_constraint(value, pltpu.HBM) for value in operands])
    feat, one, two = pl.pallas_call(
        store_kernel,
        out_shape=shapes,
        in_specs=[pl.BlockSpec(memory_space=pl.ANY)] * 3,
        out_specs=[hbm] * 3,
        scratch_shapes=[pltpu.SemaphoreType.DMA((3,))],
        compiler_params=pltpu.CompilerParams(vmem_limit_bytes=1024 * 1024),
    )(*results)
    feat = feat.reshape(1, 1, 16, 16, 64).transpose(0, 4, 1, 2, 3)
    return feat, one.reshape(3, 3, 3, 4, 32), two.reshape(3, 3, 3, 32, 64)


def solution(mesh):
    placed = (P("dp", None, "space", None, None), P(), P(), P("dp", None, "space", None, None))
    return jax.shard_map(
        local, mesh=mesh, in_specs=placed, out_specs=(P("dp", None, "space", None, None), P(), P()), check_vma=False
    )
```

```python
import functools

import jax
import jax.numpy as jnp
import numpy as np
from jax import lax
from jax.experimental import pallas as pl
from jax.experimental.pallas import tpu as pltpu
from jax.sharding import PartitionSpec as P

F32, BF16 = jnp.float32, jnp.bfloat16
LANES = 1024


def leaky(value):
    return jnp.maximum(value, 0.3 * value)


def dot_nn(a, b):
    return lax.dot_general(a, b, (((1,), (0,)), ((), ())), preferred_element_type=F32)


def dot_nt(a, b):
    return lax.dot_general(a, b, (((1,), (1,)), ((), ())), preferred_element_type=F32)


def split2(value):
    high = value.astype(BF16)
    return high, (value - high.astype(F32)).astype(BF16)


def tap_selection():
    table = np.zeros((128, 8, 256), np.float32)
    for d in range(8):
        dp, dq, dr = d // 4, d // 2 % 2, d % 2
        for pi in range(4):
            for sq in range(2):
                for sr in range(2):
                    for qe in range(2):
                        for re in range(2):
                            qi = (1 + qe) if sq == 0 else (0 if qe else 3)
                            ri = (1 + re) if sr == 0 else (0 if re else 3)
                            a, b, c = pi - dp, qi - dq, ri - dr
                            if min(a, b, c) < 0 or max(a, b, c) > 2:
                                continue
                            for i in range(4):
                                k = pi * 64 + (sq * 2 + sr) * 16 + (qe * 2 + re) * 4 + i
                                table[((a * 3 + b) * 3 + c) * 4 + i, d, k] = 1
    return table.reshape(128, 2048)


def lane_masks(rows):
    lane = lax.broadcasted_iota(jnp.int32, (rows, LANES), 1)
    return lane % 32, lane // 32


def ones(mask):
    return jnp.where(mask, 1.0, 0.0).astype(BF16)


def rolled(value, amount):
    return pltpu.roll(value, amount % LANES, 1)


NX, NY, NZH, NZL = 4, 4, 2, 4
ROWS = 16
HALF = NX * NY * ROWS
MESH = pl.DeviceIdType.LOGICAL


class Place:
    def __init__(self):
        self.dp, self.s = lax.axis_index("dp"), lax.axis_index("space")
        self.count = lax.axis_size("space")
        self.zh, self.x = lax.div(self.dp, NX), lax.rem(self.dp, NX)
        self.core = lax.rem(self.s, 2)
        chip = lax.div(self.s, 2)
        self.y, self.zl = lax.rem(chip, NY), lax.div(chip, NY)
        self.z = self.zh * NZL + self.zl
        self.xs = [lax.rem(self.x + d, NX) for d in range(NX)]
        self.ys = [lax.rem(self.y + d, NY) for d in range(NY)]
        self.base = self.zh * (NX * self.count) + self.zl * (2 * NY)
        self.columns = [self.base + x * self.count for x in self.xs]

    def near(self, dx, dy, core):
        return self.columns[dx] + self.ys[dy] * 2 + core

    def along(self, hop):
        return self.dp * self.count + lax.rem(self.s + hop + self.count, self.count)

    def plane_peers(self):
        peers = []
        for dx, dy, flip in plane_offsets():
            core = 1 - self.core if flip else self.core
            peers.append((self.near(dx, dy, core), core, core * HALF + (self.xs[dx] * NY + self.ys[dy]) * ROWS))
        return peers

    def depth_peer(self, dz):
        z = lax.rem(self.z + dz, NZH * NZL)
        here = self.x * self.count + self.y * 2 + self.core
        return here + lax.div(z, NZL) * (NX * self.count) + lax.rem(z, NZL) * (2 * NY)

    def partner(self):
        return self.near(0, 0, 1 - self.core)


def plane_offsets():
    far = lambda d: min(d[0], NX - d[0]) + min(d[1], NY - d[1])
    every = [(dx, dy, flip) for dx in range(NX) for dy in range(NY) for flip in (1, 0)]
    return sorted(every, key=lambda d: -far(d))[:-1]


def depth_offsets():
    count = NZH * NZL
    return sorted(range(1, count), key=lambda d: -min(d, count - d))


def chip_offsets():
    far = lambda d: min(d[0], NX - d[0]) + min(d[1], NY - d[1])
    return sorted([(dx, dy) for dx in range(NX) for dy in range(NY)], key=lambda d: -far(d))


def remote(src, dst, send, recv, peer):
    copy = pltpu.make_async_remote_copy(
        src_ref=src, dst_ref=dst, send_sem=send, recv_sem=recv, device_id=peer, device_id_type=MESH
    )
    return copy


def rows16(start):
    return pl.ds(pl.multiple_of(start, ROWS), ROWS)


def greet(place):
    barrier = pltpu.get_barrier_semaphore()
    peers = [peer for peer, _, _ in place.plane_peers()]
    peers += [place.depth_peer(d) for d in depth_offsets()]
    peers += [place.along(hop) for hop in (1, -1, 2, -2)]
    for peer in peers:
        pl.semaphore_signal(barrier, inc=1, device_id=peer, device_id_type=MESH)
    return lambda: pl.semaphore_wait(barrier, len(peers))


HALO_MOVES = ((1, 3, 1, 4), (-1, 0, 1, 9), (1, 1, 2, 2), (-1, 1, 2, 10), (1, 0, 1, 1), (-1, 3, 1, 12), (2, 3, 1, 0), (-2, 0, 1, 13))


class Halo:
    def __init__(self, place, wide, cots, send, recv):
        self.place, self.s, self.count = place, place.s, place.count
        self.items = {}
        for k, (hop, own, planes, to) in enumerate(HALO_MOVES):
            self.add(to, hop, wide.at[5 + own : 5 + own + planes], wide.at[to : to + planes], send.at[k], recv.at[k])
            if k == 3:
                self.add("left", 1, cots.at[1], cots.at[0], send.at[8], recv.at[8])
                self.add("right", -1, cots.at[1], cots.at[2], send.at[9], recv.at[9])

    def add(self, name, hop, src, dst, send, recv):
        peer = self.place.along(hop)
        self.items[name] = (hop, dst, remote(src, dst, send, recv, peer))

    def exists(self, hop):
        there = self.s + hop
        return (there >= 0) & (there < self.count)

    def start(self):
        for hop, dst, copy in self.items.values():
            pl.when(self.exists(hop))(copy.start)

    def clear(self):
        for hop, dst, copy in self.items.values():

            @pl.when(jnp.logical_not(self.exists(-hop)))
            def _(dst=dst):
                dst[...] = jnp.zeros(dst.shape, BF16)

    def wait(self, *names):
        for name in names:
            hop, dst, copy = self.items[name]
            pl.when(self.exists(-hop))(copy.wait_recv)

    def drain(self):
        for hop, dst, copy in self.items.values():
            pl.when(self.exists(hop))(copy.wait_send)


def tree_sum(terms):
    while len(terms) > 1:
        terms = [a + b for a, b in zip(terms[::2], terms[1::2])] + ([terms[-1]] if len(terms) % 2 else [])
    return terms[0]


class Flow:
    def __init__(self, place, sems):
        self.place, self.sems, self.sent = place, sems, []

    def send(self, phase, items):
        for src, dst, peer in items:
            remote(src, dst, self.sems.at[0, phase], self.sems.at[1, phase], peer).start()

    def arrive(self, phase, whole):
        self.sent.append((phase, whole))
        remote(whole, whole, self.sems.at[0, phase], self.sems.at[1, phase], self.place.partner()).wait_recv()

    def drain(self):
        for phase, whole in self.sent:
            remote(whole, whole, self.sems.at[0, phase], self.sems.at[1, phase], self.place.partner()).wait_send()


class LargeFlow(Flow):
    def __init__(self, place, acc, accb, r1, r2, fin, sems):
        super().__init__(place, sems)
        self.acc, self.accb, self.r1, self.r2, self.fin = acc, accb, r1, r2, fin
        self.peers = place.plane_peers()
        self.own = place.core * HALF + (place.x * NY + place.y) * ROWS

    def shares(self, half):
        at = slice(half * HALF, half * HALF + HALF)
        self.accb[at, :] = self.acc[at, :].astype(BF16)
        place = self.place
        for k, (dx, dy) in enumerate(chip_offsets()):
            src = self.accb.at[rows16(half * HALF + (place.xs[dx] * NY + place.ys[dy]) * ROWS)]
            go = remote(src, self.r1.at[2 * k + place.core], self.sems.at[0, 0], self.sems.at[1, 0], place.near(dx, dy, half))
            if (dx, dy) == (0, 0):
                pl.when(place.core != half)(go.start)
            else:
                go.start()

    def depth(self):
        self.arrive(0, self.r1.at[1:])
        count = NX * NY - 1
        lanes = [self.acc[rows16(self.own), :], self.r1[2 * count + 1 - self.place.core].astype(F32)]
        lanes += [self.r1[k].astype(F32) for k in range(2 * count)]
        total = tree_sum(lanes)
        self.r2[self.place.z] = total
        here = self.r2.at[self.place.z]
        self.send(1, [(here, here, self.place.depth_peer(d)) for d in depth_offsets()])

    def gather(self):
        self.arrive(1, self.r2.at[1:])
        total = tree_sum([self.r2[z] for z in range(NZH * NZL)])
        self.fin[rows16(self.own), :] = total.astype(BF16)
        here = self.fin.at[rows16(self.own)]
        self.send(2, [(here, here, peer) for peer, _, _ in self.peers])

    def finish(self):
        self.arrive(2, self.fin.at[ROWS:])


class SmallFlow(Flow):
    def __init__(self, place, acc, accb, q1, q2, out, sems):
        super().__init__(place, sems)
        self.acc, self.accb, self.q1, self.q2, self.out = acc, accb, q1, q2, out
        self.mine = place.core * ROWS
        self.own = place.core * NX * NY + place.x * NY + place.y

    def shares(self):
        for half in range(2):
            self.accb[half] = self.acc[half * ROWS : half * ROWS + ROWS, :].astype(BF16)
        self.q1[self.own] = self.accb[self.place.core]
        there = self.q1.at[self.own]
        self.send(0, [(self.accb.at[core], there, peer) for peer, core, _ in self.place.plane_peers()])

    def depth(self):
        self.arrive(0, self.q1.at[1:])
        total = tree_sum([self.q1[j].astype(F32) for j in range(2 * NX * NY)])
        self.q2[self.place.z] = total
        here = self.q2.at[self.place.z]
        self.send(1, [(here, here, self.place.depth_peer(d)) for d in depth_offsets()])

    def give_back(self):
        self.arrive(1, self.q2.at[1:])
        total = tree_sum([self.q2[z] for z in range(NZH * NZL)])
        self.out[rows16(self.mine), :] = total
        here = self.out.at[rows16(self.mine)]
        self.send(2, [(here, here, self.place.partner())])

    def finish(self):
        self.arrive(2, self.out.at[0:ROWS])


def flow_scratch():
    n, depth = 2 * NX * NY, NZH * NZL
    large = [
        pltpu.VMEM((2 * HALF, 128), F32),
        pltpu.VMEM((2 * HALF, 128), BF16),
        pltpu.VMEM((n, ROWS, 128), BF16),
        pltpu.VMEM((depth, ROWS, 128), F32),
        pltpu.VMEM((2 * HALF, 128), BF16),
        pltpu.SemaphoreType.DMA((2, 3)),
    ]
    small = [
        pltpu.VMEM((2 * ROWS, 128), F32),
        pltpu.VMEM((2, ROWS, 128), BF16),
        pltpu.VMEM((n, ROWS, 128), BF16),
        pltpu.VMEM((depth, ROWS, 128), F32),
        pltpu.VMEM((2 * ROWS, 128), F32),
        pltpu.SemaphoreType.DMA((2, 3)),
    ]
    return large, small


def iota2(shape):
    return lax.broadcasted_iota(jnp.int32, shape, 0), lax.broadcasted_iota(jnp.int32, shape, 1)


def flatten_planes(crop_ref, wide, cf, lp, fs):
    cf[...] = crop_ref[...].astype(F32)
    for h in range(32):
        pair = [cf[pl.ds(2 * h + e, 16, stride=64), :] for e in range(2)]
        lp[h // 4 * 16 : h // 4 * 16 + 16, h % 4 * 128 : h % 4 * 128 + 128] = jnp.concatenate(pair, axis=1).astype(BF16)
    k, n = iota2((512, 512))
    to = (k // 64 % 2 * 2 + k % 2) * 128 + k // 128 * 32 + k % 64 // 2
    moved = dot_nn(lp[...], ones(to == n))
    for block in range(8):
        for c in range(4):
            fs[16 * c : 16 * c + 16, 128 * block : 128 * block + 128] = moved[
                16 * block : 16 * block + 16, 128 * c : 128 * c + 128
            ].astype(BF16)
    m, n = iota2((64, 64))
    rows = dot_nn(ones(m // 4 % 4 * 16 + m % 4 * 4 + m // 16 == n), fs[...])
    for p in range(4):
        wide[5 + p] = rows[16 * p : 16 * p + 16].astype(BF16)


class Local:
    def __init__(self, s, wide, cots, px, maps, z1s, g2s, g1s, w1s, w2s, w3s, widened):
        self.widened = widened
        self.wide, self.cots, self.px, self.maps = wide, cots, px, maps
        self.z1s, self.g2s, self.g1s, self.w1s, self.w2s, self.w3s = z1s, g2s, g1s, w1s, w2s, w3s
        r, q = lane_masks(16)
        row = lax.broadcasted_iota(jnp.int32, (16, LANES), 0)
        q_odd, r_odd = row // 8 == 1, row // 4 % 2 == 1
        self.r_up, self.r_down = ones(r_odd & (r != 0)), ones(~r_odd & (r != 31))
        self.q_up, self.q_down = ones(q_odd & (q != 0)), ones(~q_odd & (q != 31))
        self.left_ok = jnp.where(s > 0, 0.125, 0.0)
        self.right_ok = jnp.where(s < lax.axis_size("space") - 1, 0.125, 0.0)
        r, q = lane_masks(32)
        self.keep, self.keep_ones = {}, {}
        for db in (-1, 0, 1):
            for dc in (-1, 0, 1):
                ok = jnp.ones((32, LANES), jnp.bool_)
                if db:
                    ok = ok & ((q != 0) if db < 0 else (q != 31))
                if dc:
                    ok = ok & ((r != 0) if dc < 0 else (r != 31))
                self.keep[db, dc] = ok
                self.keep_ones[db, dc] = ones(ok)
        k, n = iota2((128, 512))
        self.spread = ones((n // 64 == k // 16) & (n % 32 // 2 == k % 16))
        k, n = iota2((256, 64))
        self.collect = ones((k // 64 == n // 16) & (k % 32 // 2 == n % 16))

    def patch(self, *planes):
        for plane in planes:
            x = self.wide[plane]
            xr = rolled(x, 1) * self.r_up + rolled(x, -1) * self.r_down
            xq = rolled(x, 32) * self.q_up + rolled(x, -32) * self.q_down
            xqr = rolled(xr, 32) * self.q_up + rolled(xr, -32) * self.q_down
            for k, piece in enumerate((x, xr, xq, xqr)):
                self.px[plane * 64 + k * 16 : plane * 64 + k * 16 + 16, :] = piece

    def first(self, plane):
        z = dot_nn(self.w1s[...], self.px[plane * 128 : plane * 128 + 256, :])
        if plane in (2, 3):
            self.z1s[(plane - 2) * 256 : (plane - 1) * 256, :] = z.astype(BF16)
        z = leaky(z)
        total = z[0:32]
        for d in range(1, 8):
            total = total + z[d * 32 : d * 32 + 32]
        a1 = (total * (self.left_ok if plane < 2 else self.right_ok if plane > 3 else 0.125)).astype(BF16)
        for b in range(3):
            for c in range(3):
                v = a1
                if (b, c) != (1, 1):
                    v = rolled(v, -(32 * (b - 1) + (c - 1))) * self.keep_ones[b - 1, c - 1]
                at = plane * 288 + (b * 3 + c) * 32
                self.maps[at : at + 32, :] = v

    def second(self, plane):
        z = dot_nn(self.w2s[...], self.maps[plane * 288 : plane * 288 + 864, :])
        wide = self.widened[...]
        self.g2s[plane * 64 : plane * 64 + 64, :] = jnp.where(z > 0, wide, 0.3 * wide).astype(BF16)
        return leaky(z)

    def widen(self, which):
        cot = self.cots[which]
        self.widened[:, 0:512] = dot_nn(cot[:, 0:128], self.spread) * 0.125
        self.widened[:, 512:1024] = dot_nn(cot[:, 128:256], self.spread) * 0.125

    def features(self, pair, feats):
        high, low = split2(pair)
        for j in range(4):
            lanes = slice(256 * j, 256 * j + 256)
            feats[:, 64 * j : 64 * j + 64] = (
                dot_nn(high[:, lanes], self.collect) + dot_nn(low[:, lanes], self.collect)
            ) * 0.125

    def grad_two(self, acc):
        both = self.g2s[64:192, :]
        low = dot_nt(self.maps[288:576, :], both[0:64])
        mid = dot_nt(self.maps[576:1152, :], both)
        high = dot_nt(self.maps[1152:1440, :], both[64:128])
        acc[0:288, 0:64] = low + mid[0:288, 64:128]
        acc[288:432, 0:64] = mid[0:144, 0:64] + mid[288:432, 64:128]
        acc[0:144, 64:128] = mid[144:288, 0:64] + mid[432:576, 64:128]
        acc[144:432, 64:128] = mid[288:576, 0:64] + high

    def back(self, plane):
        u = dot_nn(self.w3s[...], self.g2s[plane * 64 : plane * 64 + 192, :])
        back = None
        for b in range(3):
            for c in range(3):
                v = u[(b * 3 + c) * 32 : (b * 3 + c) * 32 + 32]
                if (b, c) != (1, 1):
                    v = rolled(v, -(32 * (1 - b) + (1 - c)))
                    v = jnp.where(self.keep[1 - b, 1 - c], v, 0.0)
                back = v if back is None else back + v
        back = back * 0.125
        low = 0.3 * back
        for d in range(8):
            at = plane * 256 + d * 32
            self.g1s[at : at + 32, :] = jnp.where(self.z1s[at : at + 32, :].astype(F32) > 0, back, low).astype(BF16)

    def grad_one(self, sel_ref, acc):
        gram = dot_nt(self.g1s[0:256, :], self.px[256:512, :]) + dot_nt(self.g1s[256:512, :], self.px[384:640, :])
        total = None
        for d in range(8):
            high, low = split2(gram[d * 32 : d * 32 + 32])
            sel = sel_ref[:, d * 256 : d * 256 + 256]
            term = dot_nt(high, sel) + dot_nt(low, sel)
            total = term if total is None else total + term
        acc[...] = total


def whole_kernel(crop_hbm, f1_hbm, f2_hbm, sel_hbm, cot_hbm, feat_ref, one_ref, two_ref,
                 crop_ref, f1_ref, f2_ref, sel_ref, cot_ref, wide, cots, px, maps, z1s, g2s, g1s,
                 cf, lp, fs, f1s, w1s, w2s, w3s, feats, widened, fetch, halo_send, halo_recv, *flows):
    place = Place()
    ready = greet(place)
    pairs = ((crop_hbm, crop_ref), (cot_hbm, cot_ref), (f1_hbm, f1_ref), (sel_hbm, sel_ref), (f2_hbm, f2_ref))
    fetched = [pltpu.make_async_copy(src, dst, fetch.at[k]) for k, (src, dst) in enumerate(pairs)]
    for copy in fetched:
        copy.start()
    halo = Halo(place, wide, cots, halo_send, halo_recv)
    halo.clear()
    local = Local(place.s, wide, cots, px, maps, z1s, g2s, g1s, w1s, w2s, w3s, widened)
    large = LargeFlow(place, *flows[0:6])
    small = SmallFlow(place, *flows[6:12])
    fetched[0].wait()
    flatten_planes(crop_ref, wide, cf, lp, fs)
    fetched[1].wait()
    cots[1] = cot_ref[...].astype(F32).T.astype(BF16)
    ready()
    halo.start()
    fetched[2].wait()
    f1s[108:128, :] = jnp.zeros((20, 32), F32)
    for t in range(27):
        f1s[4 * t : 4 * t + 4, :] = f1_ref[t].astype(F32)
    fetched[3].wait()
    w1 = dot_nn(f1s[...].T.astype(BF16), sel_ref[...]).astype(BF16)
    for d in range(8):
        w1s[32 * d : 32 * d + 32, :] = w1[:, 256 * d : 256 * d + 256]
    fetched[4].wait()
    w2s[...] = f2_ref[...].astype(F32).T.astype(BF16)
    for a in range(3):
        w3s[:, 64 * a : 64 * a + 64] = f2_ref[288 * (2 - a) : 288 * (3 - a), :]
    large.acc[432:512, :] = jnp.zeros((80, 128), F32)
    local.patch(5, 6, 7, 8)
    local.widen(1)
    halo.wait(4, 9)
    local.patch(4, 9)
    local.first(2)
    local.first(3)
    halo.wait(2, 10)
    local.patch(2, 3, 10, 11)
    local.first(1)
    local.first(4)
    pair = local.second(1) + local.second(2)
    local.grad_two(large.acc)
    large.shares(0)
    large.shares(1)
    halo.wait(0, 1, "left", 12, 13, "right")
    local.patch(0, 1, 12, 13)
    local.first(0)
    local.first(5)
    local.widen(0)
    local.second(0)
    local.widen(2)
    local.second(3)
    local.back(0)
    local.back(1)
    local.grad_one(sel_ref, small.acc)
    small.shares()
    local.features(pair, feats)
    feat_ref[...] = feats[...].T.astype(BF16)
    large.depth()
    small.depth()
    large.gather()
    small.give_back()
    small.finish()
    one = small.out[...].T
    for t in range(27):
        one_ref[t] = one[4 * t : 4 * t + 4]
    halo.drain()
    small.drain()
    large.finish()
    two_ref[0:432, :] = large.fin[0:432, 0:64].astype(F32)
    two_ref[432:864, :] = large.fin[0:432, 64:128].astype(F32)
    large.drain()


def store_kernel(*refs):
    sems = refs[6]
    copies = [pltpu.make_async_copy(refs[k], refs[3 + k], sems.at[k]) for k in range(3)]
    for copy in copies:
        copy.start()
    for copy in copies:
        copy.wait()


def local(crop, filter_one, filter_two, cotangent):
    sel = jnp.asarray(tap_selection(), BF16)
    large, small = flow_scratch()
    hbm = pl.BlockSpec(memory_space=pltpu.HBM)
    operands = (
        crop.reshape(1024, 64),
        filter_one.reshape(27, 4, 32),
        filter_two.reshape(864, 64),
        sel,
        cotangent.transpose(0, 2, 3, 4, 1).reshape(256, 64),
    )
    shapes = (
        jax.ShapeDtypeStruct((256, 64), BF16),
        jax.ShapeDtypeStruct((27, 4, 32), F32),
        jax.ShapeDtypeStruct((864, 64), F32),
    )
    results = pl.pallas_call(
        whole_kernel,
        out_shape=shapes,
        in_specs=[hbm] * 5,
        scratch_shapes=[
            pltpu.VMEM((1024, 64), BF16),
            pltpu.VMEM((27, 4, 32), BF16),
            pltpu.VMEM((864, 64), BF16),
            pltpu.VMEM((128, 2048), BF16),
            pltpu.VMEM((256, 64), BF16),
            pltpu.VMEM((14, 16, LANES), BF16),
            pltpu.VMEM((3, 64, 256), BF16),
            pltpu.VMEM((896, LANES), BF16),
            pltpu.VMEM((1728, LANES), BF16),
            pltpu.VMEM((512, LANES), BF16),
            pltpu.VMEM((256, LANES), BF16),
            pltpu.VMEM((512, LANES), BF16),
            pltpu.VMEM((1024, 64), F32),
            pltpu.VMEM((128, 512), BF16),
            pltpu.VMEM((64, LANES), BF16),
            pltpu.VMEM((128, 32), F32),
            pltpu.VMEM((256, 256), BF16),
            pltpu.VMEM((64, 864), BF16),
            pltpu.VMEM((288, 192), BF16),
            pltpu.VMEM((64, 256), F32),
            pltpu.VMEM((64, LANES), F32),
            pltpu.SemaphoreType.DMA((5,)),
            pltpu.SemaphoreType.DMA((10,)),
            pltpu.SemaphoreType.DMA((10,)),
            *large,
            *small,
        ],
        compiler_params=pltpu.CompilerParams(
            vmem_limit_bytes=32 * 1024 * 1024, collective_id=0, has_side_effects=True
        ),
    )(*[pltpu.with_memory_space_constraint(value, pltpu.HBM) for value in operands])
    feat, one, two = pl.pallas_call(
        store_kernel,
        out_shape=shapes,
        in_specs=[pl.BlockSpec(memory_space=pl.ANY)] * 3,
        out_specs=[hbm] * 3,
        scratch_shapes=[pltpu.SemaphoreType.DMA((3,))],
        compiler_params=pltpu.CompilerParams(vmem_limit_bytes=1024 * 1024),
    )(*results)
    feat = feat.reshape(1, 1, 16, 16, 64).transpose(0, 4, 1, 2, 3)
    return feat, one.reshape(3, 3, 3, 4, 32), two.reshape(3, 3, 3, 32, 64)


def solution(mesh):
    placed = (P("dp", None, "space", None, None), P(), P(), P("dp", None, "space", None, None))
    return jax.shard_map(
        local, mesh=mesh, in_specs=placed, out_specs=(P("dp", None, "space", None, None), P(), P()), check_vma=False
    )
```
